128 devices in a mesh: gx: 8 (over y, core), gy: 16 (over x, z).
Axes of the slice: x: 4, y: 4, z: 4, core: 2. Of those that a mesh axis runs over, the one named last changes fastest.
Arguments:
- voxels: bfloat16 [1024, 512, 128], P(('gx', 'gy')), may hold values from -6 to 6
- neighbours: int32 [1024, 6], P(('gx', 'gy')), may hold values from -1 to 7, as said below
- block_count: int32 [128], P(('gx', 'gy')), may hold values from 1 to 8, as said below
- conv_weight: bfloat16 [27, 128, 128], replicated, may hold values from -0.109375 to 0.109375
- qkv_weight: bfloat16 [128, 384], replicated, may hold values from -10 to 10
- out_weight: bfloat16 [128, 128], replicated, may hold values from -0.5 to 0.5
Outputs:
- refined: bfloat16 [1024, 512, 128], P(('gx', 'gy'))
The draws below stay inside these ranges and needn't reach their ends.
Inputs may be any that keep to these rules, and one draw needn't show every extreme that they name: `neighbours`: each device holds one scene column of blocks at distinct heights of 16, in slots 0 to block_count - 1 in rising height. Entries name the face neighbour's slot on its own device (the x faces on the device one index lower or higher along gx, the y faces along gy, the z faces on the same device), or -1 where that neighbour is not active; the relation is mutual, and rows of unused slots are -1. `block_count`: some device holds 8 active blocks.
All inputs are finite; a program needn't handle non-finite values.
Results may differ from the reference program's by a relative error of at most 0.013.
Values may be sent and summed in bfloat16 or wider, within the bound.
A program may use at most 128 MiB of HBM per device.

```python
import math
import jax
import jax.numpy as jnp
from jax import lax

C = 128
HEADS = 4
SIDE = 8
VOX = 512
BLK_DEV = 8
ZLEV = 16
NBLK = 1024
N_GX = 8
N_GY = 16


def scene_layout(key):
    base = jax.random.fold_in(key, 11)
    key_count, key_full, key_rank = jax.random.split(base, 3)
    devices = N_GX * N_GY
    device_ids = jnp.arange(devices, dtype=jnp.int32)
    counts = jax.random.randint(key_count, (devices,), 1, BLK_DEV + 1).astype(jnp.int32)
    full_device = jax.random.randint(key_full, (), 0, devices).astype(jnp.int32)
    counts = jnp.where(device_ids == full_device, BLK_DEV, counts).astype(jnp.int32)
    levels = jnp.arange(ZLEV, dtype=jnp.int32)
    scores = jax.random.randint(key_rank, (devices, ZLEV), 0, 1 << 20).astype(jnp.int32) * ZLEV + levels[None, :]
    ordering = jnp.argsort(scores, axis=1)
    ranking = jnp.argsort(ordering, axis=1).astype(jnp.int32)
    ranking = jnp.where((device_ids == full_device)[:, None], levels[None, :], ranking)
    occupied = ranking < counts[:, None]
    slot_ids = (jnp.cumsum(occupied.astype(jnp.int32), axis=1) - 1).astype(jnp.int32)
    return (counts, occupied, slot_ids)


def draw_neighbours(key, part):
    counts, occupied, slot_ids = scene_layout(key)
    devices = N_GX * N_GY
    device_ids = jnp.arange(devices, dtype=jnp.int32)
    column_x = device_ids // N_GY
    column_y = device_ids % N_GY
    occ_padded = jnp.pad(occupied, ((0, 0), (1, 1)))
    slot_padded = jnp.pad(slot_ids, ((0, 0), (1, 1)))

    def look(device_step, device_ok, level_step):
        source_ids = jnp.clip(device_ids + device_step, 0, devices - 1)
        occ_rows = occ_padded[source_ids][:, 1 + level_step:1 + level_step + ZLEV]
        slot_rows = slot_padded[source_ids][:, 1 + level_step:1 + level_step + ZLEV]
        present = device_ok[:, None] & occ_rows
        return jnp.where(present, slot_rows, -1).astype(jnp.int32)
    always = device_ids >= 0
    columns = [look(-N_GY, column_x > 0, 0), look(N_GY, column_x < N_GX - 1, 0), look(-1, column_y > 0, 0), look(1, column_y < N_GY - 1, 0), look(0, always, -1), look(0, always, 1)]
    neighbour_table = jnp.stack(columns, axis=-1)
    row_ids = jnp.where(occupied, device_ids[:, None] * BLK_DEV + slot_ids, devices * BLK_DEV).astype(jnp.int32)
    filled = jnp.full((devices * BLK_DEV, 6), -1, dtype=jnp.int32)
    filled = filled.at[row_ids.reshape(-1)].set(neighbour_table.reshape(-1, 6), mode='drop')
    return filled


def draw_block_count(key, part):
    counts, occupied, slot_ids = scene_layout(key)
    return counts


def draw_qkv_weight(key, part):
    key_query, key_key, key_value = jax.random.split(jax.random.fold_in(key, 5), 3)
    spread = 1.6 / C ** 0.5
    query_cols = jnp.clip(jax.random.normal(key_query, (C, C), jnp.float32), -4.0, 4.0) * spread
    key_cols = jnp.clip(jax.random.normal(key_key, (C, C), jnp.float32), -4.0, 4.0) * spread
    value_cols = jnp.clip(jax.random.normal(key_value, (C, C), jnp.float32), -4.0, 4.0) / C ** 0.5
    return jnp.concatenate([query_cols, key_cols, value_cols], axis=1).astype(jnp.bfloat16)


def steps_of(stream_key, extent, pieces, smallest, largest):
    def one(axis_at, parts):
        heights = jax.random.uniform(jax.random.fold_in(jax.random.fold_in(stream_key, 6), axis_at), (parts,), jnp.float32, smallest / len(pieces), largest / len(pieces))
        return jnp.repeat(jnp.exp(heights), extent[axis_at] // parts).reshape((-1,) + (1,) * (len(extent) - axis_at - 1))

    factor_of = one(*pieces[0])
    for cut in pieces[1:]:
        factor_of = factor_of * one(*cut)
    return factor_of


def gaussian(own_key, dims, scale, limit, pieces=(), kind=jnp.bfloat16):
    entries = scale * jax.random.normal(own_key, dims, jnp.float32)
    if pieces:
        entries = entries * steps_of(own_key, dims, pieces, -0.22, 0.18)
    return jnp.clip(entries, -limit, limit).astype(kind)


def setup_inputs(seed: int = 0) -> dict:
    key_list = jax.random.split(jax.random.key(seed), 7)
    voxels = gaussian(key_list[0], (NBLK, VOX, C), 1.0, 6.0, ((0, 128),))
    neighbours = draw_neighbours(jax.random.fold_in(key_list[6], 71), 0)
    block_count = draw_block_count(jax.random.fold_in(key_list[6], 71), 0)
    conv_weight = gaussian(key_list[3], (27, C, C), (27 * C) ** -0.5, 0.109375)
    qkv_weight = draw_qkv_weight(jax.random.fold_in(key_list[6], 71), 0)
    out_weight = gaussian(key_list[5], (C, C), C ** -0.5, 0.5)
    return {"voxels": voxels, "neighbours": neighbours, "block_count": block_count, "conv_weight": conv_weight, "qkv_weight": qkv_weight, "out_weight": out_weight}


def padded_cells(block_cubes, face_cells):
    padded = jnp.pad(block_cubes, ((0, 0), (1, 1), (1, 1), (1, 1), (0, 0)))
    padded = padded.at[:, 0, 1:-1, 1:-1].set(face_cells[0])
    padded = padded.at[:, -1, 1:-1, 1:-1].set(face_cells[1])
    padded = padded.at[:, 1:-1, 0, 1:-1].set(face_cells[2])
    padded = padded.at[:, 1:-1, -1, 1:-1].set(face_cells[3])
    padded = padded.at[:, 1:-1, 1:-1, 0].set(face_cells[4])
    padded = padded.at[:, 1:-1, 1:-1, -1].set(face_cells[5])
    return padded

def convolve(padded, conv_weight):
    channels = padded.shape[-1]
    running = jnp.zeros((padded.shape[0] * SIDE ** 3, conv_weight.shape[2]), jnp.float32)
    tap_index = 0
    for step_x in range(3):
        for step_y in range(3):
            for step_z in range(3):
                window = padded[:, step_x:step_x + SIDE, step_y:step_y + SIDE, step_z:step_z + SIDE].reshape(-1, channels)
                running = running + jnp.dot(window, conv_weight[tap_index], preferred_element_type=jnp.float32)
                tap_index = tap_index + 1
    return running

def project(row_data, weight):
    values = row_data.astype(jnp.float32)
    mean_square = lax.optimization_barrier(jnp.mean(values * values, axis=-1, keepdims=True))
    guarded = mean_square + 1e-06
    inverse = lax.rsqrt(guarded)
    normed = (values * inverse).astype(jnp.bfloat16)
    return jnp.dot(normed, weight, preferred_element_type=jnp.float32).astype(jnp.bfloat16)

def attend_block(queries, key_rows, value_rows, key_ok):
    voxel_count, channels = queries.shape
    head_width = channels // HEADS
    q_heads = queries.reshape(voxel_count, HEADS, head_width).astype(jnp.float32)
    k_heads = key_rows.reshape(-1, HEADS, head_width).astype(jnp.float32)
    v_heads = value_rows.reshape(-1, HEADS, head_width).astype(jnp.float32)
    scores = jnp.einsum('qhd,khd->hqk', q_heads, k_heads) / math.sqrt(head_width)
    key_mask = jnp.repeat(key_ok, voxel_count)
    scores = jnp.where(key_mask[None, None, :], scores, jnp.float32(-1e+30))
    row_max = lax.optimization_barrier(jnp.max(scores, axis=-1, keepdims=True))
    weights = jnp.exp(scores - row_max)
    probabilities = (weights / lax.optimization_barrier(jnp.sum(weights, axis=-1, keepdims=True))).astype(jnp.bfloat16)
    mixture = jnp.einsum('hqk,khd->qhd', probabilities.astype(jnp.float32), v_heads)
    return mixture.reshape(voxel_count, channels).astype(jnp.bfloat16)

def reference(voxels, neighbours, block_count, conv_weight, qkv_weight, out_weight):
    blocks, voxel_count, channels = voxels.shape
    row_ids = jnp.arange(blocks, dtype=jnp.int32)
    device = row_ids // BLK_DEV
    offsets = jnp.array([-N_GY, N_GY, -1, 1, 0, 0], dtype=jnp.int32)
    global_ids = jnp.where(neighbours >= 0, (device[:, None] + offsets[None, :]) * BLK_DEV + neighbours, -1).astype(jnp.int32)
    present = global_ids >= 0
    safe_ids = jnp.maximum(global_ids, 0).astype(jnp.int32)
    block_cubes = voxels.reshape(blocks, SIDE, SIDE, SIDE, channels)
    layers = [block_cubes[:, -1], block_cubes[:, 0], block_cubes[:, :, -1], block_cubes[:, :, 0], block_cubes[:, :, :, -1], block_cubes[:, :, :, 0]]
    face_cells = []
    for face_index in range(6):
        chosen = layers[face_index][safe_ids[:, face_index]]
        face_cells.append(jnp.where(present[:, face_index, None, None, None], chosen, jnp.zeros((), voxels.dtype)))
    padded = padded_cells(block_cubes, face_cells)
    conv_sum = convolve(padded, conv_weight)
    mixed_in = (voxels.reshape(-1, channels).astype(jnp.float32) + conv_sum).astype(jnp.bfloat16)
    packed = project(mixed_in, qkv_weight)
    queries = packed[:, :channels].reshape(blocks, voxel_count, channels)
    key_values = packed[:, channels:].reshape(blocks, voxel_count, 2 * channels)
    key_ids = jnp.concatenate([row_ids[:, None], safe_ids], axis=1).astype(jnp.int32)
    key_ok = jnp.concatenate([jnp.ones((blocks, 1), dtype=bool), present], axis=1)

    def one_block(block_items):
        block_queries, block_keys, block_ok = block_items
        chosen = key_values[block_keys]
        return attend_block(block_queries, chosen[..., :channels], chosen[..., channels:], block_ok)
    attended = lax.map(one_block, (queries, key_ids, key_ok))
    result = mixed_in.astype(jnp.float32) + jnp.dot(attended.reshape(-1, channels), out_weight, preferred_element_type=jnp.float32)
    active = row_ids % BLK_DEV < block_count[device]
    result = jnp.where(active[:, None, None], result.reshape(blocks, voxel_count, channels), jnp.float32(0.0))
    return result.astype(jnp.bfloat16)
```

```python
import functools
import math

import jax
import jax.numpy as jnp
from jax import lax
from jax.experimental import pallas as pl
from jax.experimental.pallas import tpu as pltpu
from jax.sharding import PartitionSpec as P

HEADS = 4
SIDE = 8
LIMIT = 90.0
F32 = jnp.float32
BF16 = jnp.bfloat16
NT = (((1,), (1,)), ((), ()))


def passed_along(value, axis, steps):
    count = lax.axis_size(axis)
    initial, last = (max(0, -steps), min(count, count - steps))
    return lax.ppermute(value, axis, [(source, source + steps) for source in range(initial, last)])


def shifted_z(x, below, above):
    at = lax.broadcasted_iota(jnp.int32, x.shape, 1)
    down = pltpu.roll(jnp.where(at == SIDE - 1, below, x), 1, 1)
    up = pltpu.roll(jnp.where(at == 0, above, x), SIDE - 1, 1)
    return [down, x, up]


def conv_block(b, nb_ref, vox_ref, faces, w_s, a_s, b_s, mixed_ref, normed_ref):
    rows, ch = SIDE * SIDE, vox_ref.shape[-1]

    def picked(ref, face):
        slot = nb_ref[b, face]
        value = ref[jnp.maximum(slot, 0)].astype(F32).reshape(-1, SIDE, ch)
        return jnp.where(slot >= 0, value, 0.0)

    own = vox_ref[b].astype(F32).reshape(rows, SIDE, ch)
    inner = shifted_z(own, picked(vox_ref, 4), picked(vox_ref, 5))
    xm, xp, ym, yp = [shifted_z(picked(ref, f), 0.0, 0.0) for f, ref in enumerate(faces)]
    blank = jnp.zeros((SIDE, ch), F32)
    for e in range(3):
        for s in range(SIDE + 2):
            if s == 0 or s == SIDE + 1:
                mid = (xm if s == 0 else xp)[e].reshape(rows, ch)
                top = bottom = blank
            else:
                mid = inner[e][(s - 1) * SIDE : s * SIDE].reshape(rows, ch)
                top, bottom = ym[e][s - 1], yp[e][s - 1]
            a_s[e, s] = jnp.concatenate([top, mid, bottom], axis=0).astype(BF16)
            b_s[e, s] = mid.astype(BF16)
    acc = None
    for c in range(3):
        for e in range(3):
            pieces = []
            for r in range(4):
                slabs = [
                    b_s[e, 2 * k + r] if c == 1 else a_s[e, 2 * k + r, c * SIDE : c * SIDE + rows]
                    for k in range(4)
                ]
                pieces.append(jnp.concatenate(slabs, axis=0))
            lhs = jnp.concatenate(pieces, axis=1)
            at = (c * 3 + e) * 4 * ch
            part = jnp.dot(lhs, w_s[at : at + 4 * ch], preferred_element_type=F32)
            acc = part if acc is None else acc + part
    for k in range(4):
        for o in range(2):
            x = 2 * k + o
            here = own[x * SIDE : (x + 1) * SIDE].reshape(rows, ch)
            mixed = (here + acc[k * rows : (k + 1) * rows, o * ch : (o + 1) * ch]).astype(BF16)
            mixed_ref[b, x * rows : (x + 1) * rows] = mixed
            wide = mixed.astype(F32)
            square = jnp.mean(wide * wide, axis=-1, keepdims=True)
            normed_ref[b, x * rows : (x + 1) * rows] = (wide * lax.rsqrt(square + 1e-06)).astype(BF16)


def pair_weights(cw_ref, w_s):
    ch = cw_ref.shape[-1]
    for ce in range(9):
        for r in range(4):
            for o in range(2):
                row = (ce * 4 + r) * ch
                tap = r - o
                value = cw_ref[tap * 9 + ce] if 0 <= tap <= 2 else jnp.zeros((ch, ch), BF16)
                w_s[row : row + ch, o * ch : (o + 1) * ch] = value


def conv_kernel(nb_ref, vox_ref, f0, f1, f2, f3, cw_ref, mixed_ref, normed_ref, w_s, a_s, b_s):
    pair_weights(cw_ref, w_s)

    @pl.loop(0, vox_ref.shape[0])
    def _(b):
        conv_block(b, nb_ref, vox_ref, (f0, f1, f2, f3), w_s, a_s, b_s, mixed_ref, normed_ref)


def head_lanes(shape, h, width):
    lane = lax.broadcasted_iota(jnp.int32, shape, len(shape) - 1)
    return (lane // width) == h


def largest_norm(x, width):
    ch = x.shape[-1]
    wide = x.astype(F32)
    i = lax.broadcasted_iota(jnp.int32, (ch, ch), 0) // width
    j = lax.broadcasted_iota(jnp.int32, (ch, ch), 1) // width
    same = jnp.where(i == j, 1.0, 0.0).astype(BF16)
    sums = jnp.dot((wide * wide).astype(BF16), same, preferred_element_type=F32)
    return jnp.max(sums) * 1.02


def put_head_masks(v_ref, slots, width):
    ch = HEADS * width
    for s in range(slots):
        for h in range(HEADS):
            mask = head_lanes((v_ref.shape[2], ch), h, width)
            v_ref[s, h, :, ch:] = jnp.where(mask, 1.0, 0.0).astype(BF16)


def put_key_set(normed, w_ref, k_ref, v_ref, slot, width):
    ch = HEADS * width
    kv = jnp.dot(normed, w_ref[:, ch:], preferred_element_type=F32).astype(BF16)
    keys, values = kv[:, :ch], kv[:, ch:]
    k_ref[slot] = keys
    for h in range(HEADS):
        mask = head_lanes(values.shape, h, width)
        v_ref[slot, h, :, :ch] = jnp.where(mask, values, jnp.zeros_like(values))
    return largest_norm(keys, width)


def put_queries(queries, q_s, width):
    for h in range(HEADS):
        mask = head_lanes(queries.shape, h, width)
        q_s[h] = jnp.where(mask, queries, jnp.zeros_like(queries))


def add_pair(q_s, k_ref, v_ref, slot, acc_s):
    keys = k_ref[slot]
    total = None
    for h in range(HEADS):
        scores = lax.dot_general(q_s[h], keys, NT, preferred_element_type=F32)
        weights = jnp.exp2(scores).astype(BF16)
        part = jnp.dot(weights, v_ref[slot, h], preferred_element_type=F32)
        total = part if total is None else total + part
    acc_s[...] += total


def add_pair_running(q_s, k_ref, v_ref, slot, acc_s, m_s, width):
    keys = k_ref[slot]
    ch = HEADS * width
    for h in range(HEADS):
        scores = lax.dot_general(q_s[h], keys, NT, preferred_element_type=F32)
        old = m_s[:, h * width : h * width + 1]
        new = jnp.maximum(old, jnp.max(scores, axis=1, keepdims=True))
        weights = jnp.exp2(scores - new).astype(BF16)
        part = jnp.dot(weights, v_ref[slot, h], preferred_element_type=F32)
        mask = head_lanes((scores.shape[0], ch), h, width)
        scale = jnp.where(mask, jnp.exp2(old - new), 1.0)
        acc_s[:, :ch] = acc_s[:, :ch] * scale + part[:, :ch]
        acc_s[:, ch:] = acc_s[:, ch:] * scale + part[:, ch:]
        m_s[...] = jnp.where(mask, new, m_s[...])


def local_kernel(
    nb_ref, cnt_ref, normed_ref, w_ref, acc_ref, m_ref, q_ref, fast_ref, qn_ref, k_s, v_s, q_s, kn_s, list_s
):
    b = pl.program_id(0)
    slots, _, ch = normed_ref.shape
    width = ch // HEADS

    @pl.when(b == 0)
    def _():
        put_head_masks(v_s, slots, width)

        @pl.loop(0, cnt_ref[0])
        def _(s):
            kn_s[s] = put_key_set(normed_ref[s], w_ref, k_s, v_s, s, width)

    fast_ref[b] = 1
    qn_ref[b] = 0.0

    @pl.when(b < cnt_ref[0])
    def _():
        factor = math.log2(math.e) / math.sqrt(width)
        queries = jnp.dot(normed_ref[b], w_ref[:, :ch], preferred_element_type=F32)
        queries = (queries * factor).astype(BF16)
        q_ref[0] = queries
        put_queries(queries, q_s, width)
        acc_ref[0] = jnp.zeros(acc_ref.shape[1:], F32)
        list_s[0] = b
        n = jnp.int32(1)
        kn = kn_s[b]
        for face in (4, 5):
            slot = nb_ref[b, face]
            list_s[n] = jnp.maximum(slot, 0)
            n = jnp.where(slot >= 0, n + 1, n)
            kn = jnp.where(slot >= 0, jnp.maximum(kn, kn_s[jnp.maximum(slot, 0)]), kn)
        qn = largest_norm(queries, width)
        fast = qn * kn <= LIMIT * LIMIT
        qn_ref[b] = qn
        fast_ref[b] = fast.astype(jnp.int32)

        @pl.when(fast)
        def _():
            @pl.loop(0, n)
            def _(i):
                add_pair(q_s, k_s, v_s, list_s[i], acc_ref.at[0])

        @pl.when(jnp.logical_not(fast))
        def _():
            m_ref[0] = jnp.full(m_ref.shape[1:], -1e30, F32)

            @pl.loop(0, n)
            def _(i):
                add_pair_running(q_s, k_s, v_s, list_s[i], acc_ref.at[0], m_ref.at[0], width)


def remote_kernel(
    nb_ref, cnt_ref, fast_ref, qn_ref, acc_ref, m_ref, q_ref, mixed_ref, r0, r1, r2, r3, w_ref, wo_ref,
    out_ref, k_s, v_s, q_s, acc_s, m_s
):
    b = pl.program_id(0)
    ch = q_ref.shape[-1]
    width = ch // HEADS

    @pl.when(b == 0)
    def _():
        put_head_masks(v_s, 4, width)

    @pl.when(b >= cnt_ref[0])
    def _():
        out_ref[0] = jnp.zeros(out_ref.shape[1:], out_ref.dtype)

    @pl.when(b < cnt_ref[0])
    def _():
        put_queries(q_ref[0], q_s, width)
        acc_s[...] = acc_ref[0]
        n = jnp.int32(0)
        kn = jnp.float32(0.0)
        for face, ref in enumerate((r0, r1, r2, r3)):
            there = nb_ref[b, face] >= 0

            def put(ref=ref, n=n, kn=kn):
                return jnp.maximum(kn, put_key_set(ref[0], w_ref, k_s, v_s, n, width))

            kn = lax.cond(there, put, lambda kn=kn: kn)
            n = jnp.where(there, n + 1, n)
        local = fast_ref[b] == 1
        fast = jnp.logical_and(local, qn_ref[b] * kn <= LIMIT * LIMIT)

        @pl.when(fast)
        def _():
            @pl.loop(0, n)
            def _(i):
                add_pair(q_s, k_s, v_s, i, acc_s)

        @pl.when(jnp.logical_not(fast))
        def _():
            m_s[...] = jnp.where(local, jnp.zeros(m_s.shape, F32), m_ref[0])

            @pl.loop(0, n)
            def _(i):
                add_pair_running(q_s, k_s, v_s, i, acc_s, m_s, width)

        attended = (acc_s[:, :ch] / acc_s[:, ch:]).astype(BF16)
        moved = jnp.dot(attended, wo_ref[...], preferred_element_type=F32)
        out_ref[0] = (mixed_ref[0].astype(F32) + moved).astype(out_ref.dtype)


def body(voxels, neighbours, block_count, conv_weight, qkv_weight, out_weight):
    blocks, vox, ch = voxels.shape
    cubes = voxels.reshape(blocks, SIDE, SIDE, SIDE, ch)
    faces = [
        passed_along(cubes[:, -1], "gx", 1),
        passed_along(cubes[:, 0], "gx", -1),
        passed_along(cubes[:, :, -1], "gy", 1),
        passed_along(cubes[:, :, 0], "gy", -1),
    ]
    vmem = pl.BlockSpec(memory_space=pltpu.VMEM)
    smem = pl.BlockSpec(memory_space=pltpu.SMEM)
    like = jax.ShapeDtypeStruct(voxels.shape, BF16)
    mixed, normed = pl.pallas_call(
        conv_kernel,
        out_shape=[like, like],
        in_specs=[smem] + [vmem] * 6,
        out_specs=[vmem, vmem],
        scratch_shapes=[
            pltpu.VMEM((36 * ch, 2 * ch), BF16),
            pltpu.VMEM((3, SIDE + 2, SIDE * SIDE + 2 * SIDE, ch), BF16),
            pltpu.VMEM((3, SIDE + 2, SIDE * SIDE, ch), BF16),
        ],
        cost_estimate=pl.CostEstimate(flops=2 * 9 * 256 * 512 * 256 * blocks, bytes_accessed=4 << 20, transcendentals=0),
        name="conv",
    )(neighbours, voxels, *faces, conv_weight)
    received = [
        passed_along(normed, "gx", 1),
        passed_along(normed, "gx", -1),
        passed_along(normed, "gy", 1),
        passed_along(normed, "gy", -1),
    ]

    def block(*tail):
        return pl.BlockSpec((1,) + tail, lambda b, *_: (b, 0, 0))

    def whole(*shape):
        return pl.BlockSpec(shape, lambda b, *_: (0,) * len(shape))

    acc, m, q, fast, qn = pl.pallas_call(
        local_kernel,
        out_shape=[
            jax.ShapeDtypeStruct((blocks, vox, 2 * ch), F32),
            jax.ShapeDtypeStruct((blocks, vox, ch), F32),
            like,
            jax.ShapeDtypeStruct((blocks,), jnp.int32),
            jax.ShapeDtypeStruct((blocks,), F32),
        ],
        grid_spec=pltpu.PrefetchScalarGridSpec(
            num_scalar_prefetch=2,
            grid=(blocks,),
            in_specs=[whole(blocks, vox, ch), whole(ch, 3 * ch)],
            out_specs=[block(vox, 2 * ch), block(vox, ch), block(vox, ch), smem, smem],
            scratch_shapes=[
                pltpu.VMEM((blocks, vox, ch), BF16),
                pltpu.VMEM((blocks, HEADS, vox, 2 * ch), BF16),
                pltpu.VMEM((HEADS, vox, ch), BF16),
                pltpu.SMEM((blocks,), F32),
                pltpu.SMEM((4,), jnp.int32),
            ],
        ),
        cost_estimate=pl.CostEstimate(flops=22 * 2 * 512 * 512 * 128 * 12, bytes_accessed=8 << 20, transcendentals=22 << 20),
        name="local",
    )(neighbours, block_count, normed, qkv_weight)

    def from_neighbour(face):
        return pl.BlockSpec((1, vox, ch), lambda b, nb, *_: (jnp.maximum(nb[b, face], 0), 0, 0))

    return pl.pallas_call(
        remote_kernel,
        out_shape=like,
        grid_spec=pltpu.PrefetchScalarGridSpec(
            num_scalar_prefetch=2,
            grid=(blocks,),
            in_specs=[smem, smem, block(vox, 2 * ch), block(vox, ch), block(vox, ch), block(vox, ch)]
            + [from_neighbour(f) for f in range(4)]
            + [whole(ch, 3 * ch), whole(ch, ch)],
            out_specs=block(vox, ch),
            scratch_shapes=[
                pltpu.VMEM((4, vox, ch), BF16),
                pltpu.VMEM((4, HEADS, vox, 2 * ch), BF16),
                pltpu.VMEM((HEADS, vox, ch), BF16),
                pltpu.VMEM((vox, 2 * ch), F32),
                pltpu.VMEM((vox, ch), F32),
            ],
        ),
        cost_estimate=pl.CostEstimate(flops=9 * 2 * 512 * 512 * 128 * 12, bytes_accessed=8 << 20, transcendentals=9 << 20),
        name="remote",
    )(neighbours, block_count, fast, qn, acc, m, q, mixed, *received, qkv_weight, out_weight)


def solution(mesh):
    placed = (P(("gx", "gy"), None, None), P(("gx", "gy"), None), P(("gx", "gy")), P(), P(), P())
    return jax.shard_map(
        body, mesh=mesh, in_specs=placed, out_specs=P(("gx", "gy"), None, None), check_vma=False
    )
```

```python
import functools
import math

import jax
import jax.numpy as jnp
from jax import lax
from jax.experimental import pallas as pl
from jax.experimental.pallas import tpu as pltpu
from jax.sharding import PartitionSpec as P

HEADS = 4
SIDE = 8
LIMIT = 90.0
F32 = jnp.float32
BF16 = jnp.bfloat16
NT = (((1,), (1,)), ((), ()))
MESH = pl.DeviceIdType.MESH


def passed_along(value, axis, steps):
    count = lax.axis_size(axis)
    initial, last = (max(0, -steps), min(count, count - steps))
    return lax.ppermute(value, axis, [(source, source + steps) for source in range(initial, last)])


def shifted_z(x, below, above):
    at = lax.broadcasted_iota(jnp.int32, x.shape, 1)
    down = pltpu.roll(jnp.where(at == SIDE - 1, below, x), 1, 1)
    up = pltpu.roll(jnp.where(at == 0, above, x), SIDE - 1, 1)
    return [down, x, up]


def conv_block(b, nb_ref, vox_ref, faces, w_s, a_s, b_s, mixed_ref, normed_ref):
    rows, ch = SIDE * SIDE, vox_ref.shape[-1]

    def picked(ref, face):
        slot = nb_ref[b, face]
        value = ref[jnp.maximum(slot, 0)].astype(F32).reshape(-1, SIDE, ch)
        return jnp.where(slot >= 0, value, 0.0)

    own = vox_ref[b].astype(F32).reshape(rows, SIDE, ch)
    inner = shifted_z(own, picked(vox_ref, 4), picked(vox_ref, 5))
    xm, xp, ym, yp = [shifted_z(picked(ref, f), 0.0, 0.0) for f, ref in enumerate(faces)]
    blank = jnp.zeros((SIDE, ch), F32)
    for e in range(3):
        for s in range(SIDE + 2):
            if s == 0 or s == SIDE + 1:
                mid = (xm if s == 0 else xp)[e].reshape(rows, ch)
                top = bottom = blank
            else:
                mid = inner[e][(s - 1) * SIDE : s * SIDE].reshape(rows, ch)
                top, bottom = ym[e][s - 1], yp[e][s - 1]
            a_s[e, s] = jnp.concatenate([top, mid, bottom], axis=0).astype(BF16)
            b_s[e, s] = mid.astype(BF16)
    acc = None
    for c in range(3):
        for e in range(3):
            pieces = []
            for r in range(4):
                slabs = [
                    b_s[e, 2 * k + r] if c == 1 else a_s[e, 2 * k + r, c * SIDE : c * SIDE + rows]
                    for k in range(4)
                ]
                pieces.append(jnp.concatenate(slabs, axis=0))
            lhs = jnp.concatenate(pieces, axis=1)
            at = (c * 3 + e) * 4 * ch
            part = jnp.dot(lhs, w_s[at : at + 4 * ch], preferred_element_type=F32)
            acc = part if acc is None else acc + part
    for k in range(4):
        for o in range(2):
            x = 2 * k + o
            here = own[x * SIDE : (x + 1) * SIDE].reshape(rows, ch)
            mixed = (here + acc[k * rows : (k + 1) * rows, o * ch : (o + 1) * ch]).astype(BF16)
            mixed_ref[b, x * rows : (x + 1) * rows] = mixed
            wide = mixed.astype(F32)
            square = jnp.mean(wide * wide, axis=-1, keepdims=True)
            normed_ref[b, x * rows : (x + 1) * rows] = (wide * lax.rsqrt(square + 1e-06)).astype(BF16)


def pair_weights(cw_ref, w_s):
    ch = cw_ref.shape[-1]
    for ce in range(9):
        for r in range(4):
            for o in range(2):
                row = (ce * 4 + r) * ch
                tap = r - o
                value = cw_ref[tap * 9 + ce] if 0 <= tap <= 2 else jnp.zeros((ch, ch), BF16)
                w_s[row : row + ch, o * ch : (o + 1) * ch] = value


def conv_kernel(
    sizes, nb_ref, vox_ref, cube_ref, cw_ref, mixed_ref, normed_ref, low_ref, high_ref,
    w_s, a_s, b_s, face_s, face_out, face_in, send_sem, recv_sem
):
    gx, gy = lax.axis_index("gx"), lax.axis_index("gy")
    n_gx, n_gy = sizes
    blocks = vox_ref.shape[0]
    up_x, down_x = lax.rem(gx + 1, n_gx), lax.rem(gx + n_gx - 1, n_gx)
    up_y, down_y = lax.rem(gy + 1, n_gy), lax.rem(gy + n_gy - 1, n_gy)
    peers = [(up_x, gy), (down_x, gy), (gx, up_y), (gx, down_y)]
    layers = [cube_ref.at[:, SIDE - 1], cube_ref.at[:, 0], cube_ref.at[:, :, SIDE - 1], cube_ref.at[:, :, 0]]

    barrier = pltpu.get_barrier_semaphore()
    for peer in peers:
        pl.semaphore_signal(barrier, inc=1, device_id=peer, device_id_type=MESH)
    pl.semaphore_wait(barrier, 4)

    copies = [
        pltpu.make_async_remote_copy(
            src_ref=layer, dst_ref=face_s.at[f], send_sem=face_out.at[f], recv_sem=face_in.at[f],
            device_id=peers[f], device_id_type=MESH,
        )
        for f, layer in enumerate(layers)
    ]
    for copy in copies:
        copy.start()

    def passing(b, side):
        return pltpu.make_async_remote_copy(
            src_ref=normed_ref.at[b], dst_ref=(low_ref, high_ref)[side].at[b],
            send_sem=send_sem.at[side, b], recv_sem=recv_sem.at[side, b],
            device_id=peers[side], device_id_type=MESH,
        )

    pair_weights(cw_ref, w_s)
    for copy in copies:
        copy.wait()
    faces = [face_s.at[f] for f in range(4)]

    @pl.loop(0, blocks)
    def _(b):
        conv_block(b, nb_ref, vox_ref, faces, w_s, a_s, b_s, mixed_ref, normed_ref)

        @pl.when(b > 0)
        def _():
            passing(b - 1, 0).start()
            passing(b - 1, 1).start()

    passing(blocks - 1, 0).start()
    passing(blocks - 1, 1).start()

    @pl.loop(0, blocks)
    def _(b):
        passing(b, 0).wait()
        passing(b, 1).wait()


def head_lanes(shape, h, width):
    lane = lax.broadcasted_iota(jnp.int32, shape, len(shape) - 1)
    return (lane // width) == h


def largest_norm(x, width):
    ch = x.shape[-1]
    wide = x.astype(F32)
    i = lax.broadcasted_iota(jnp.int32, (ch, ch), 0) // width
    j = lax.broadcasted_iota(jnp.int32, (ch, ch), 1) // width
    same = jnp.where(i == j, 1.0, 0.0).astype(BF16)
    sums = jnp.dot((wide * wide).astype(BF16), same, preferred_element_type=F32)
    return jnp.max(sums) * 1.02


def put_head_masks(v_ref, slots, width):
    ch = HEADS * width
    for s in range(slots):
        for h in range(HEADS):
            mask = head_lanes((v_ref.shape[2], ch), h, width)
            v_ref[s, h, :, ch:] = jnp.where(mask, 1.0, 0.0).astype(BF16)


def put_key_set(normed, w_ref, k_ref, v_ref, slot, width):
    ch = HEADS * width
    kv = jnp.dot(normed, w_ref[:, ch:], preferred_element_type=F32).astype(BF16)
    keys, values = kv[:, :ch], kv[:, ch:]
    k_ref[slot] = keys
    for h in range(HEADS):
        mask = head_lanes(values.shape, h, width)
        v_ref[slot, h, :, :ch] = jnp.where(mask, values, jnp.zeros_like(values))
    return largest_norm(keys, width)


def put_queries(queries, q_s, width):
    for h in range(HEADS):
        mask = head_lanes(queries.shape, h, width)
        q_s[h] = jnp.where(mask, queries, jnp.zeros_like(queries))


def add_pair(q_s, k_ref, v_ref, slot, acc_s):
    keys = k_ref[slot]
    values = v_ref[slot].reshape(-1, acc_s.shape[-1])
    rows = 256
    for at in range(0, acc_s.shape[0], rows):
        weights = []
        for h in range(HEADS):
            scores = lax.dot_general(q_s[h, at : at + rows], keys, NT, preferred_element_type=F32)
            weights.append(jnp.exp2(scores).astype(BF16))
        part = jnp.dot(jnp.concatenate(weights, axis=1), values, preferred_element_type=F32)
        acc_s[at : at + rows] += part


def add_pair_running(q_s, k_ref, v_ref, slot, acc_s, m_s, width):
    keys = k_ref[slot]
    ch = HEADS * width
    for h in range(HEADS):
        scores = lax.dot_general(q_s[h], keys, NT, preferred_element_type=F32)
        old = m_s[:, h * width : h * width + 1]
        new = jnp.maximum(old, jnp.max(scores, axis=1, keepdims=True))
        weights = jnp.exp2(scores - new).astype(BF16)
        part = jnp.dot(weights, v_ref[slot, h], preferred_element_type=F32)
        mask = head_lanes((scores.shape[0], ch), h, width)
        scale = jnp.where(mask, jnp.exp2(old - new), 1.0)
        acc_s[:, :ch] = acc_s[:, :ch] * scale + part[:, :ch]
        acc_s[:, ch:] = acc_s[:, ch:] * scale + part[:, ch:]
        m_s[...] = jnp.where(mask, new, m_s[...])


def local_kernel(
    nb_ref, cnt_ref, normed_ref, low_ref, high_ref, w_ref,
    acc_ref, m_ref, q_ref, fast_ref, qn_ref, k_s, v_s, q_s, kn_s, list_s
):
    b = pl.program_id(0)
    slots, _, ch = normed_ref.shape
    width = ch // HEADS

    @pl.when(b == 0)
    def _():
        put_head_masks(v_s, slots + 2, width)

        @pl.loop(0, cnt_ref[0])
        def _(s):
            kn_s[s] = put_key_set(normed_ref[s], w_ref, k_s, v_s, s, width)

    fast_ref[b] = 1
    qn_ref[b] = 0.0

    @pl.when(b < cnt_ref[0])
    def _():
        factor = math.log2(math.e) / math.sqrt(width)
        queries = jnp.dot(normed_ref[b], w_ref[:, :ch], preferred_element_type=F32)
        queries = (queries * factor).astype(BF16)
        q_ref[0] = queries
        put_queries(queries, q_s, width)
        acc_ref[0] = jnp.zeros(acc_ref.shape[1:], F32)
        list_s[0] = b
        n = jnp.int32(1)
        kn = kn_s[b]
        for face in (4, 5):
            slot = nb_ref[b, face]
            list_s[n] = jnp.maximum(slot, 0)
            n = jnp.where(slot >= 0, n + 1, n)
            kn = jnp.where(slot >= 0, jnp.maximum(kn, kn_s[jnp.maximum(slot, 0)]), kn)
        for face, ref in enumerate((low_ref, high_ref)):
            there = nb_ref[b, face] >= 0

            def put(ref=ref, face=face, kn=kn):
                return jnp.maximum(kn, put_key_set(ref[0], w_ref, k_s, v_s, slots + face, width))

            kn = lax.cond(there, put, lambda kn=kn: kn)
            list_s[n] = slots + face
            n = jnp.where(there, n + 1, n)
        qn = largest_norm(queries, width)
        fast = qn * kn <= LIMIT * LIMIT
        qn_ref[b] = qn
        fast_ref[b] = fast.astype(jnp.int32)

        @pl.when(fast)
        def _():
            @pl.loop(0, n)
            def _(i):
                add_pair(q_s, k_s, v_s, list_s[i], acc_ref.at[0])

        @pl.when(jnp.logical_not(fast))
        def _():
            m_ref[0] = jnp.full(m_ref.shape[1:], -1e30, F32)

            @pl.loop(0, n)
            def _(i):
                add_pair_running(q_s, k_s, v_s, list_s[i], acc_ref.at[0], m_ref.at[0], width)


def remote_kernel(
    nb_ref, cnt_ref, fast_ref, qn_ref, acc_ref, m_ref, q_ref, mixed_ref, low_ref, high_ref, w_ref, wo_ref,
    out_ref, k_s, v_s, q_s, acc_s, m_s
):
    b = pl.program_id(0)
    ch = q_ref.shape[-1]
    width = ch // HEADS

    @pl.when(b == 0)
    def _():
        put_head_masks(v_s, 2, width)

    @pl.when(b >= cnt_ref[0])
    def _():
        out_ref[0] = jnp.zeros(out_ref.shape[1:], out_ref.dtype)

    @pl.when(b < cnt_ref[0])
    def _():
        put_queries(q_ref[0], q_s, width)
        acc_s[...] = acc_ref[0]
        n = jnp.int32(0)
        kn = jnp.float32(0.0)
        for face, ref in ((2, low_ref), (3, high_ref)):
            there = nb_ref[b, face] >= 0

            def put(ref=ref, n=n, kn=kn):
                return jnp.maximum(kn, put_key_set(ref[0], w_ref, k_s, v_s, n, width))

            kn = lax.cond(there, put, lambda kn=kn: kn)
            n = jnp.where(there, n + 1, n)
        local = fast_ref[b] == 1
        fast = jnp.logical_and(local, qn_ref[b] * kn <= LIMIT * LIMIT)

        @pl.when(fast)
        def _():
            @pl.loop(0, n)
            def _(i):
                add_pair(q_s, k_s, v_s, i, acc_s)

        @pl.when(jnp.logical_not(fast))
        def _():
            m_s[...] = jnp.where(local, jnp.zeros(m_s.shape, F32), m_ref[0])

            @pl.loop(0, n)
            def _(i):
                add_pair_running(q_s, k_s, v_s, i, acc_s, m_s, width)

        attended = (acc_s[:, :ch] / acc_s[:, ch:]).astype(BF16)
        moved = jnp.dot(attended, wo_ref[...], preferred_element_type=F32)
        out_ref[0] = (mixed_ref[0].astype(F32) + moved).astype(out_ref.dtype)


def body(voxels, neighbours, block_count, conv_weight, qkv_weight, out_weight):
    blocks, vox, ch = voxels.shape
    cubes = voxels.reshape(blocks, SIDE, SIDE, SIDE, ch)
    vmem = pl.BlockSpec(memory_space=pltpu.VMEM)
    smem = pl.BlockSpec(memory_space=pltpu.SMEM)
    hbm = pl.BlockSpec(memory_space=pl.ANY)
    like = jax.ShapeDtypeStruct(voxels.shape, BF16)
    n_gx, n_gy = lax.axis_size("gx"), lax.axis_size("gy")
    mixed, normed, low_x, high_x = pl.pallas_call(
        functools.partial(conv_kernel, (n_gx, n_gy)),
        out_shape=[like] * 4,
        in_specs=[smem, vmem, hbm, vmem],
        out_specs=[vmem, vmem, hbm, hbm],
        scratch_shapes=[
            pltpu.VMEM((36 * ch, 2 * ch), BF16),
            pltpu.VMEM((3, SIDE + 2, SIDE * SIDE + 2 * SIDE, ch), BF16),
            pltpu.VMEM((3, SIDE + 2, SIDE * SIDE, ch), BF16),
            pltpu.VMEM((4, blocks, SIDE, SIDE, ch), BF16),
            pltpu.SemaphoreType.DMA((4,)),
            pltpu.SemaphoreType.DMA((4,)),
            pltpu.SemaphoreType.DMA((2, blocks)),
            pltpu.SemaphoreType.DMA((2, blocks)),
        ],
        compiler_params=pltpu.CompilerParams(collective_id=0, has_side_effects=True),
        cost_estimate=pl.CostEstimate(flops=2 * 9 * 256 * 512 * 256 * blocks, bytes_accessed=4 << 20, transcendentals=0),
        name="conv",
    )(neighbours, voxels, cubes, conv_weight)
    low_y, high_y = passed_along(normed, "gy", 1), passed_along(normed, "gy", -1)

    def block(*tail):
        return pl.BlockSpec((1,) + tail, lambda b, *_: (b, 0, 0))

    def whole(*shape):
        return pl.BlockSpec(shape, lambda b, *_: (0,) * len(shape))

    def from_neighbour(face):
        return pl.BlockSpec((1, vox, ch), lambda b, nb, *_: (jnp.maximum(nb[b, face], 0), 0, 0))

    acc, m, q, fast, qn = pl.pallas_call(
        local_kernel,
        out_shape=[
            jax.ShapeDtypeStruct((blocks, vox, 2 * ch), F32),
            jax.ShapeDtypeStruct((blocks, vox, ch), F32),
            like,
            jax.ShapeDtypeStruct((blocks,), jnp.int32),
            jax.ShapeDtypeStruct((blocks,), F32),
        ],
        grid_spec=pltpu.PrefetchScalarGridSpec(
            num_scalar_prefetch=2,
            grid=(blocks,),
            in_specs=[whole(blocks, vox, ch), from_neighbour(0), from_neighbour(1), whole(ch, 3 * ch)],
            out_specs=[block(vox, 2 * ch), block(vox, ch), block(vox, ch), smem, smem],
            scratch_shapes=[
                pltpu.VMEM((blocks + 2, vox, ch), BF16),
                pltpu.VMEM((blocks + 2, HEADS, vox, 2 * ch), BF16),
                pltpu.VMEM((HEADS, vox, ch), BF16),
                pltpu.SMEM((blocks,), F32),
                pltpu.SMEM((6,), jnp.int32),
            ],
        ),
        cost_estimate=pl.CostEstimate(flops=22 * 2 * 512 * 512 * 128 * 12, bytes_accessed=8 << 20, transcendentals=22 << 20),
        name="local",
    )(neighbours, block_count, normed, low_x, high_x, qkv_weight)

    return pl.pallas_call(
        remote_kernel,
        out_shape=like,
        grid_spec=pltpu.PrefetchScalarGridSpec(
            num_scalar_prefetch=2,
            grid=(blocks,),
            in_specs=[smem, smem, block(vox, 2 * ch), block(vox, ch), block(vox, ch), block(vox, ch)]
            + [from_neighbour(2), from_neighbour(3)]
            + [whole(ch, 3 * ch), whole(ch, ch)],
            out_specs=block(vox, ch),
            scratch_shapes=[
                pltpu.VMEM((2, vox, ch), BF16),
                pltpu.VMEM((2, HEADS, vox, 2 * ch), BF16),
                pltpu.VMEM((HEADS, vox, ch), BF16),
                pltpu.VMEM((vox, 2 * ch), F32),
                pltpu.VMEM((vox, ch), F32),
            ],
        ),
        cost_estimate=pl.CostEstimate(flops=9 * 2 * 512 * 512 * 128 * 12, bytes_accessed=8 << 20, transcendentals=9 << 20),
        name="remote",
    )(neighbours, block_count, fast, qn, acc, m, q, mixed, low_y, high_y, qkv_weight, out_weight)


def solution(mesh):
    placed = (P(("gx", "gy"), None, None), P(("gx", "gy"), None), P(("gx", "gy")), P(), P(), P())
    return jax.shard_map(
        body, mesh=mesh, in_specs=placed, out_specs=P(("gx", "gy"), None, None), check_vma=False
    )
```

```python
import functools
import math

import jax
import jax.numpy as jnp
from jax import lax
from jax.experimental import pallas as pl
from jax.experimental.pallas import tpu as pltpu
from jax.sharding import PartitionSpec as P

HEADS = 4
SIDE = 8
LIMIT = 90.0
F32 = jnp.float32
BF16 = jnp.bfloat16
NT = (((1,), (1,)), ((), ()))
ROWS = 128
LANES = 256
VALUE_ROWS = 48
MESH = pl.DeviceIdType.MESH


def shifted_z(x, below, above):
    at = lax.broadcasted_iota(jnp.int32, x.shape, 1)
    down = pltpu.roll(jnp.where(at == SIDE - 1, below, x), 1, 1)
    up = pltpu.roll(jnp.where(at == 0, above, x), SIDE - 1, 1)
    return [down, x, up]


def conv_block(b, nb_ref, vox_ref, faces, w_s, a_s, b_s, mixed_ref, normed_ref, between):
    rows, ch = SIDE * SIDE, vox_ref.shape[-1]

    def picked(ref, face):
        slot = nb_ref[b, face]
        value = ref[jnp.maximum(slot, 0)].astype(F32).reshape(-1, SIDE, ch)
        return jnp.where(slot >= 0, value, 0.0)

    own = vox_ref[b].astype(F32).reshape(rows, SIDE, ch)
    inner = shifted_z(own, picked(vox_ref, 4), picked(vox_ref, 5))
    xm, xp, ym, yp = [shifted_z(picked(ref, f), 0.0, 0.0) for f, ref in enumerate(faces)]
    blank = jnp.zeros((SIDE, ch), F32)
    for e in range(3):
        for s in range(SIDE + 2):
            if s == 0 or s == SIDE + 1:
                mid = (xm if s == 0 else xp)[e].reshape(rows, ch)
                top = bottom = blank
            else:
                mid = inner[e][(s - 1) * SIDE : s * SIDE].reshape(rows, ch)
                top, bottom = ym[e][s - 1], yp[e][s - 1]
            a_s[e, s] = jnp.concatenate([top, mid, bottom], axis=0).astype(BF16)
            b_s[e, s] = mid.astype(BF16)
    between()
    acc = None
    for c in range(3):
        for e in range(3):
            pieces = []
            for r in range(4):
                slabs = [
                    b_s[e, 2 * k + r] if c == 1 else a_s[e, 2 * k + r, c * SIDE : c * SIDE + rows]
                    for k in range(4)
                ]
                pieces.append(jnp.concatenate(slabs, axis=0))
            lhs = jnp.concatenate(pieces, axis=1)
            at = (c * 3 + e) * 4 * ch
            part = jnp.dot(lhs, w_s[at : at + 4 * ch], preferred_element_type=F32)
            acc = part if acc is None else acc + part
    for k in range(4):
        for o in range(2):
            x = 2 * k + o
            here = own[x * SIDE : (x + 1) * SIDE].reshape(rows, ch)
            mixed = (here + acc[k * rows : (k + 1) * rows, o * ch : (o + 1) * ch]).astype(BF16)
            mixed_ref[b, x * rows : (x + 1) * rows] = mixed
            wide = mixed.astype(F32)
            square = jnp.mean(wide * wide, axis=-1, keepdims=True)
            normed_ref[b, x * rows : (x + 1) * rows] = (wide * lax.rsqrt(square + 1e-06)).astype(BF16)


def pair_weights(cw_ref, w_s):
    ch = cw_ref.shape[-1]
    for ce in range(9):
        for r in range(4):
            for o in range(2):
                row = (ce * 4 + r) * ch
                tap = r - o
                value = cw_ref[tap * 9 + ce] if 0 <= tap <= 2 else jnp.zeros((ch, ch), BF16)
                w_s[row : row + ch, o * ch : (o + 1) * ch] = value


def clear_operands(q_s, k_s, v_s):
    q_s[...] = jnp.zeros(q_s.shape, q_s.dtype)
    k_s[...] = jnp.zeros(k_s.shape, k_s.dtype)
    v_s[...] = jnp.ones(v_s.shape, v_s.dtype)


def put_queries(queries, q_s, width):
    for h in range(HEADS):
        q_s[h, h * width : (h + 1) * width] = queries[h * width : (h + 1) * width]


def put_key_set(keys, values, k_s, v_s, slot, width):
    k_s[slot, :, : HEADS * width] = keys
    for h in range(HEADS):
        v_s[slot, h, :width] = values[h * width : (h + 1) * width]


def largest_norm(x, width):
    wide = x.astype(F32)
    return jnp.max(jnp.sum((wide * wide).reshape(HEADS, width, -1), axis=1)) * 1.02


def product(lhs, rhs, transpose=False):
    m, depth = lhs.shape
    n = rhs.shape[0 if transpose else 1]
    halves = n // LANES == 1
    rows = m // 2 if halves else m

    def inner(*accs):
        for u in range(2):
            part = lhs[u * rows : (u + 1) * rows] if halves else lhs
            for t in range(depth // LANES):
                deep = slice(t * LANES, (t + 1) * LANES)
                wide = slice(0, LANES) if halves else slice(u * LANES, (u + 1) * LANES)
                tile = rhs[wide, deep] if transpose else rhs[deep, wide]
                pltpu.matmul_push_rhs(tile, t % 2, u, transpose=transpose)
                pltpu.matmul_acc_lhs(accs[u], part[:, deep], load_staged_rhs=t % 2)
        return jnp.concatenate([pltpu.matmul_pop(acc) for acc in accs], axis=0 if halves else 1)

    return pl.run_scoped(inner, *[pltpu.ACC(u)((rows, LANES), F32) for u in range(2)])


def padded(x, rows, cols):
    if x.shape[1] < cols:
        x = jnp.concatenate([x, jnp.zeros((x.shape[0], cols - x.shape[1]), x.dtype)], axis=1)
    if x.shape[0] < rows:
        x = jnp.concatenate([x, jnp.zeros((rows - x.shape[0], x.shape[1]), x.dtype)], axis=0)
    return x


def add_pair(slot, q_s, k_s, v_s, score_acc, value_acc):
    per_tile, per_head = LANES // ROWS, k_s.shape[1] // ROWS
    ring = len(score_acc[0])
    units = range(2)

    def chunk(unit, h, c):
        return score_acc[unit][(per_head * h + c) % ring]

    def stage_queries(h, unit, reg):
        pltpu.matmul_push_rhs(q_s[h, :, unit * LANES : (unit + 1) * LANES], reg, unit)

    def score(h, unit, chunks, reg):
        for c in chunks:
            rows = k_s[slot, c * ROWS : (c + 1) * ROWS]
            pltpu.matmul_acc_lhs(chunk(unit, h, c), rows, load_staged_rhs=reg if c == 0 else None)

    def stage_weights(h, unit, tile, reg):
        parts = [
            jnp.exp2(pltpu.matmul_pop(chunk(unit, h, c))).astype(BF16)
            for c in range(tile * per_tile, (tile + 1) * per_tile)
        ]
        pltpu.matmul_push_rhs(jnp.concatenate(parts, axis=0), reg, unit)

    def mix(h, unit, tile, reg):
        rows = v_s[slot, h, :, tile * LANES : (tile + 1) * LANES]
        pltpu.matmul_acc_lhs(value_acc[unit][h], rows, load_staged_rhs=reg)

    for u in units:
        stage_queries(0, u, 0)
    for u in units:
        score(0, u, range(per_head), 0)
    for u in units:
        stage_queries(1, u, 1)
    reg = 1
    for h in range(HEADS):
        if h + 1 < HEADS:
            for u in units:
                score(h + 1, u, range(per_tile), reg)
        for u in units:
            stage_weights(h, u, 0, 1 - reg)
        if h + 1 < HEADS:
            for u in units:
                score(h + 1, u, range(per_tile, per_head), None)
        for u in units:
            stage_weights(h, u, 1, reg)
        for u in units:
            mix(h, u, 0, 1 - reg)
        if h + 2 < HEADS:
            for u in units:
                stage_queries(h + 2, u, 1 - reg)
        for u in units:
            mix(h, u, 1, reg)
        reg = 1 - reg


def add_pairs(n, q_s, k_s, v_s, store):
    ring = 6

    def inner(*accs):
        score_acc = [accs[:ring], accs[ring : 2 * ring]]
        value_acc = [accs[2 * ring : 2 * ring + HEADS], accs[2 * ring + HEADS :]]
        if isinstance(n, int):
            for i in range(n):
                add_pair(i, q_s, k_s, v_s, score_acc, value_acc)
        else:

            @pl.loop(0, n)
            def _(i):
                add_pair(i, q_s, k_s, v_s, score_acc, value_acc)

        for h in range(HEADS):
            for u in range(2):
                store(h, slice(u * LANES, (u + 1) * LANES), pltpu.matmul_pop(value_acc[u][h]))

    scores = [pltpu.ACC(u)((ROWS, LANES), F32) for u in range(2) for _ in range(ring)]
    values = [pltpu.ACC(u)((VALUE_ROWS, LANES), F32) for u in range(2) for _ in range(HEADS)]
    pl.run_scoped(inner, *scores, *values)


def add_pair_running(slot, q_s, k_s, v_s, o_s, m_s):
    for h in range(HEADS):
        scores = product(k_s[slot], q_s[h])
        old = m_s[h]
        new = jnp.maximum(old, jnp.max(scores, axis=0, keepdims=True))
        weights = jnp.exp2(scores - new).astype(BF16)
        o_s[h] = o_s[h] * jnp.exp2(old - new) + product(v_s[slot, h], weights)
        m_s[h] = new


def front_kernel(
    sizes, nb_ref, vox_ref, cube_ref, cw_ref, w_ref,
    mixed_ref, q_ref, k_ref, v_ref, own_ref, wt_ref, qn_ref, kn_ref, got0, got1, got2, got3,
    w_s, a_s, b_s, normed_s, face_s, q_s, face_out, face_in, send_sem, recv_sem
):
    gx, gy = lax.axis_index("gx"), lax.axis_index("gy")
    n_gx, n_gy = sizes
    blocks, _, ch = vox_ref.shape
    width = ch // HEADS
    got = (got0, got1, got2, got3)
    up_x, down_x = lax.rem(gx + 1, n_gx), lax.rem(gx + n_gx - 1, n_gx)
    up_y, down_y = lax.rem(gy + 1, n_gy), lax.rem(gy + n_gy - 1, n_gy)
    peers = [(up_x, gy), (down_x, gy), (gx, up_y), (gx, down_y)]
    layers = [cube_ref.at[:, SIDE - 1], cube_ref.at[:, 0], cube_ref.at[:, :, SIDE - 1], cube_ref.at[:, :, 0]]

    barrier = pltpu.get_barrier_semaphore()
    for peer in peers:
        pl.semaphore_signal(barrier, inc=1, device_id=peer, device_id_type=MESH)
    pl.semaphore_wait(barrier, 4)

    copies = [
        pltpu.make_async_remote_copy(
            src_ref=layer, dst_ref=face_s.at[f], send_sem=face_out.at[f], recv_sem=face_in.at[f],
            device_id=peers[f], device_id_type=MESH,
        )
        for f, layer in enumerate(layers)
    ]
    for f in (2, 3, 0, 1):
        copies[f].start()

    def passing(b, side):
        return pltpu.make_async_remote_copy(
            src_ref=normed_s.at[b], dst_ref=got[side].at[b],
            send_sem=send_sem.at[side, b], recv_sem=recv_sem.at[side, b],
            device_id=peers[side], device_id_type=MESH,
        )

    def pass_on(b):
        for side in (2, 3, 0, 1):
            passing(b, side).start()

    pair_weights(cw_ref, w_s)
    q_s[...] = jnp.zeros(q_s.shape, q_s.dtype)
    wt_ref[...] = w_ref[...].astype(F32).T.astype(BF16)
    for copy in copies:
        copy.wait()
    faces = [face_s.at[f] for f in range(4)]

    @pl.loop(0, blocks)
    def _(b):
        def between():
            @pl.when(b > 0)
            def _():
                pass_on(b - 1)

        conv_block(b, nb_ref, vox_ref, faces, w_s, a_s, b_s, mixed_ref, normed_s, between)

    pass_on(blocks - 1)

    @pl.loop(0, blocks)
    def _(b):
        factor = math.log2(math.e) / math.sqrt(width)
        normed = normed_s[b]
        keys = jnp.dot(normed, w_ref[:, ch : 2 * ch], preferred_element_type=F32).astype(BF16)
        turned = lax.dot_general(wt_ref[...], normed, NT, preferred_element_type=F32)
        queries = (turned[:ch] * factor).astype(BF16)
        values = turned[2 * ch :].astype(BF16)
        q_ref[b], k_ref[b], v_ref[b] = queries, keys, values
        qn_ref[b] = largest_norm(queries, width)
        kn_ref[b] = largest_norm(turned[ch : 2 * ch], width)
        put_queries(queries, q_s, width)
        ones = jnp.ones((VALUE_ROWS - width, values.shape[1]), BF16)
        for h in range(HEADS):
            scores = jnp.dot(keys, q_s[h], preferred_element_type=F32)
            weights = jnp.exp2(scores).astype(BF16)
            rows = jnp.concatenate([values[h * width : (h + 1) * width], ones], axis=0)
            own_ref[b, h] = jnp.dot(rows, weights, preferred_element_type=F32)

    @pl.loop(0, blocks)
    def _(b):
        for side in range(4):
            passing(b, side).wait()


def back_kernel(
    nb_ref, cnt_ref, qn_ref, kn_ref, mixed_ref, q_ref, own_ref, k_ref, v_ref, k_lo, v_lo, k_hi, v_hi,
    r0, r1, r2, r3, w_ref, wt_ref, wo_ref, out_ref, q_s, k_s, v_s, o_s, m_s
):
    b = pl.program_id(0)
    ch = mixed_ref.shape[-1]
    width = ch // HEADS

    @pl.when(b == 0)
    def _():
        clear_operands(q_s, k_s, v_s)

    @pl.when(b >= cnt_ref[0])
    def _():
        out_ref[0] = jnp.zeros(out_ref.shape[1:], out_ref.dtype)

    @pl.when(b < cnt_ref[0])
    def _():
        put_queries(q_ref[0], q_s, width)
        n = jnp.int32(0)
        kn = kn_ref[b]
        for face, keys, values in ((4, k_lo, v_lo), (5, k_hi, v_hi)):
            slot = nb_ref[b, face]

            @pl.when(slot >= 0)
            def _(keys=keys, values=values, n=n):
                put_key_set(keys[0], values[0], k_s, v_s, n, width)

            n = jnp.where(slot >= 0, n + 1, n)
            kn = jnp.where(slot >= 0, jnp.maximum(kn, kn_ref[jnp.maximum(slot, 0)]), kn)
        for face, ref in enumerate((r0, r1, r2, r3)):
            there = nb_ref[b, face] >= 0

            def put(ref=ref, n=n, kn=kn):
                normed = padded(ref[0], 0, LANES)
                keys = product(normed, padded(w_ref[:, ch : 2 * ch], LANES, LANES))[:, :ch].astype(BF16)
                turned = product(padded(wt_ref[ch:], 0, LANES), normed, transpose=True)
                put_key_set(keys, turned[ch:].astype(BF16), k_s, v_s, n, width)
                return jnp.maximum(kn, largest_norm(turned[:ch], width))

            kn = lax.cond(there, put, lambda kn=kn: kn)
            n = jnp.where(there, n + 1, n)
        fast = qn_ref[b] * kn <= LIMIT * LIMIT

        @pl.when(fast)
        def _():
            def store(h, lanes, value):
                o_s[h, :, lanes] = own_ref[0, h, :, lanes] + value

            add_pairs(n, q_s, k_s, v_s, store)

        @pl.when(jnp.logical_not(fast))
        def _():
            put_key_set(k_ref[0], v_ref[0], k_s, v_s, n, width)
            o_s[...] = jnp.zeros(o_s.shape, F32)
            m_s[...] = jnp.full(m_s.shape, -1e30, F32)

            @pl.loop(0, n + 1)
            def _(i):
                add_pair_running(i, q_s, k_s, v_s, o_s, m_s)

        parts = [o_s[h, :width] / o_s[h, width : width + 1] for h in range(HEADS)]
        attended = jnp.concatenate(parts, axis=0).T.astype(BF16)
        moved = product(padded(attended, 0, LANES), padded(wo_ref[...], LANES, LANES))[:, :ch]
        out_ref[0] = (mixed_ref[0].astype(F32) + moved).astype(out_ref.dtype)


def body(voxels, neighbours, block_count, conv_weight, qkv_weight, out_weight):
    blocks, vox, ch = voxels.shape
    cubes = voxels.reshape(blocks, SIDE, SIDE, SIDE, ch)
    vmem = pl.BlockSpec(memory_space=pltpu.VMEM)
    smem = pl.BlockSpec(memory_space=pltpu.SMEM)
    hbm = pl.BlockSpec(memory_space=pl.ANY)
    like = jax.ShapeDtypeStruct(voxels.shape, BF16)
    turned = jax.ShapeDtypeStruct((blocks, ch, vox), BF16)
    scalars = jax.ShapeDtypeStruct((blocks,), F32)
    n_gx, n_gy = lax.axis_size("gx"), lax.axis_size("gy")

    def operands(slots):
        return [
            pltpu.VMEM((HEADS, 2 * ch, vox), BF16),
            pltpu.VMEM((slots, vox, 2 * ch), BF16),
            pltpu.VMEM((slots, HEADS, VALUE_ROWS, vox), BF16),
        ]

    mixed, q, k, v, own, wt, qn, kn, *got = pl.pallas_call(
        functools.partial(front_kernel, (n_gx, n_gy)),
        out_shape=[
            like, turned, like, turned,
            jax.ShapeDtypeStruct((blocks, HEADS, VALUE_ROWS, vox), F32),
            jax.ShapeDtypeStruct((3 * ch, ch), BF16),
            scalars, scalars,
        ] + [like] * 4,
        in_specs=[smem, vmem, hbm, vmem, vmem],
        out_specs=[vmem] * 6 + [smem, smem] + [hbm] * 4,
        scratch_shapes=[
            pltpu.VMEM((36 * ch, 2 * ch), BF16),
            pltpu.VMEM((3, SIDE + 2, SIDE * SIDE + 2 * SIDE, ch), BF16),
            pltpu.VMEM((3, SIDE + 2, SIDE * SIDE, ch), BF16),
            pltpu.VMEM(voxels.shape, BF16),
            pltpu.VMEM((4, blocks, SIDE, SIDE, ch), BF16),
            pltpu.VMEM((HEADS, ch, vox), BF16),
            pltpu.SemaphoreType.DMA((4,)),
            pltpu.SemaphoreType.DMA((4,)),
            pltpu.SemaphoreType.DMA((4, blocks)),
            pltpu.SemaphoreType.DMA((4, blocks)),
        ],
        compiler_params=pltpu.CompilerParams(collective_id=0, has_side_effects=True),
        name="front",
    )(neighbours, voxels, cubes, conv_weight, qkv_weight)

    def block(*tail):
        return pl.BlockSpec((1,) + tail, lambda b, *_: (b,) + (0,) * len(tail))

    def whole(*shape):
        return pl.BlockSpec(shape, lambda b, *_: (0,) * len(shape))

    def across(face, *tail):
        return pl.BlockSpec((1,) + tail, lambda b, nb, *_: (jnp.maximum(nb[b, face], 0),) + (0,) * len(tail))

    return pl.pallas_call(
        back_kernel,
        out_shape=like,
        grid_spec=pltpu.PrefetchScalarGridSpec(
            num_scalar_prefetch=2,
            grid=(blocks,),
            in_specs=[smem, smem, block(vox, ch), block(ch, vox), block(HEADS, VALUE_ROWS, vox), block(vox, ch), block(ch, vox)]
            + [across(4, vox, ch), across(4, ch, vox), across(5, vox, ch), across(5, ch, vox)]
            + [across(f, vox, ch) for f in range(4)]
            + [whole(ch, 3 * ch), whole(3 * ch, ch), whole(ch, ch)],
            out_specs=block(vox, ch),
            scratch_shapes=[
                *operands(7),
                pltpu.VMEM((HEADS, VALUE_ROWS, vox), F32),
                pltpu.VMEM((HEADS, 1, vox), F32),
            ],
        ),
        name="back",
    )(neighbours, block_count, qn, kn, mixed, q, own, k, v, k, v, k, v, *got, qkv_weight, wt, out_weight)


def solution(mesh):
    placed = (P(("gx", "gy"), None, None), P(("gx", "gy"), None), P(("gx", "gy")), P(), P(), P())
    return jax.shard_map(
        body, mesh=mesh, in_specs=placed, out_specs=P(("gx", "gy"), None, None), check_vma=False
    )
```

```python
import functools
import math

import jax
import jax.numpy as jnp
from jax import lax
from jax.experimental import pallas as pl
from jax.experimental.pallas import tpu as pltpu
from jax.sharding import PartitionSpec as P

HEADS = 4
SIDE = 8
LIMIT = 90.0
F32 = jnp.float32
BF16 = jnp.bfloat16
NT = (((1,), (1,)), ((), ()))
ROWS = 128
LANES = 256
VALUE_ROWS = 48
MESH = pl.DeviceIdType.MESH


def shifted_z(x, below, above):
    at = lax.broadcasted_iota(jnp.int32, x.shape, 1)
    down = pltpu.roll(jnp.where(at == SIDE - 1, below, x), 1, 1)
    up = pltpu.roll(jnp.where(at == 0, above, x), SIDE - 1, 1)
    return [down, x, up]


def conv_block(b, nb_ref, vox_ref, faces, w_s, a_s, b_s, mixed_ref, normed_ref, between):
    rows, ch = SIDE * SIDE, vox_ref.shape[-1]

    def picked(ref, face):
        slot = nb_ref[b, face]
        value = ref[jnp.maximum(slot, 0)].astype(F32).reshape(-1, SIDE, ch)
        return jnp.where(slot >= 0, value, 0.0)

    own = vox_ref[b].astype(F32).reshape(rows, SIDE, ch)
    inner = shifted_z(own, picked(vox_ref, 4), picked(vox_ref, 5))
    xm, xp, ym, yp = [shifted_z(picked(ref, f), 0.0, 0.0) for f, ref in enumerate(faces)]
    blank = jnp.zeros((SIDE, ch), F32)
    for e in range(3):
        for s in range(SIDE + 2):
            if s == 0 or s == SIDE + 1:
                mid = (xm if s == 0 else xp)[e].reshape(rows, ch)
                top = bottom = blank
            else:
                mid = inner[e][(s - 1) * SIDE : s * SIDE].reshape(rows, ch)
                top, bottom = ym[e][s - 1], yp[e][s - 1]
            a_s[e, s] = jnp.concatenate([top, mid, bottom], axis=0).astype(BF16)
            b_s[e, s] = mid.astype(BF16)
    between()
    acc = None
    for c in range(3):
        for e in range(3):
            pieces = []
            for r in range(4):
                slabs = [
                    b_s[e, 2 * k + r] if c == 1 else a_s[e, 2 * k + r, c * SIDE : c * SIDE + rows]
                    for k in range(4)
                ]
                pieces.append(jnp.concatenate(slabs, axis=0))
            lhs = jnp.concatenate(pieces, axis=1)
            at = (c * 3 + e) * 4 * ch
            part = jnp.dot(lhs, w_s[at : at + 4 * ch], preferred_element_type=F32)
            acc = part if acc is None else acc + part
    for k in range(4):
        for o in range(2):
            x = 2 * k + o
            here = own[x * SIDE : (x + 1) * SIDE].reshape(rows, ch)
            mixed = (here + acc[k * rows : (k + 1) * rows, o * ch : (o + 1) * ch]).astype(BF16)
            mixed_ref[b, x * rows : (x + 1) * rows] = mixed
            wide = mixed.astype(F32)
            square = jnp.mean(wide * wide, axis=-1, keepdims=True)
            normed_ref[b, x * rows : (x + 1) * rows] = (wide * lax.rsqrt(square + 1e-06)).astype(BF16)


def pair_weights(cw_ref, w_s):
    ch = cw_ref.shape[-1]
    for ce in range(9):
        for r in range(4):
            for o in range(2):
                row = (ce * 4 + r) * ch
                tap = r - o
                value = cw_ref[tap * 9 + ce] if 0 <= tap <= 2 else jnp.zeros((ch, ch), BF16)
                w_s[row : row + ch, o * ch : (o + 1) * ch] = value


def clear_operands(q_s, k_s, v_s):
    q_s[...] = jnp.zeros(q_s.shape, q_s.dtype)
    k_s[...] = jnp.zeros(k_s.shape, k_s.dtype)
    v_s[...] = jnp.ones(v_s.shape, v_s.dtype)


def put_queries(queries, q_s, width):
    for h in range(HEADS):
        q_s[h, h * width : (h + 1) * width] = queries[h * width : (h + 1) * width]


def put_key_set(keys, values, k_s, v_s, slot, width):
    k_s[slot, :, : HEADS * width] = keys
    for h in range(HEADS):
        v_s[slot, h, :width] = values[h * width : (h + 1) * width]


def largest_norm(x, width):
    wide = x.astype(F32)
    return jnp.max(jnp.sum((wide * wide).reshape(HEADS, width, -1), axis=1)) * 1.02


def product(lhs, rhs, transpose=False):
    m, depth = lhs.shape
    n = rhs.shape[0 if transpose else 1]
    halves = n // LANES == 1
    rows = m // 2 if halves else m

    def inner(*accs):
        for u in range(2):
            part = lhs[u * rows : (u + 1) * rows] if halves else lhs
            for t in range(depth // LANES):
                deep = slice(t * LANES, (t + 1) * LANES)
                wide = slice(0, LANES) if halves else slice(u * LANES, (u + 1) * LANES)
                tile = rhs[wide, deep] if transpose else rhs[deep, wide]
                pltpu.matmul_push_rhs(tile, t % 2, u, transpose=transpose)
                pltpu.matmul_acc_lhs(accs[u], part[:, deep], load_staged_rhs=t % 2)
        return jnp.concatenate([pltpu.matmul_pop(acc) for acc in accs], axis=0 if halves else 1)

    return pl.run_scoped(inner, *[pltpu.ACC(u)((rows, LANES), F32) for u in range(2)])


def padded(x, rows, cols):
    if x.shape[1] < cols:
        x = jnp.concatenate([x, jnp.zeros((x.shape[0], cols - x.shape[1]), x.dtype)], axis=1)
    if x.shape[0] < rows:
        x = jnp.concatenate([x, jnp.zeros((rows - x.shape[0], x.shape[1]), x.dtype)], axis=0)
    return x


def add_pair(slot, q_s, k_s, v_s, score_acc, value_acc):
    per_tile, per_head = LANES // ROWS, k_s.shape[1] // ROWS
    ring = len(score_acc[0])
    units = range(2)

    def chunk(unit, h, c):
        return score_acc[unit][(per_head * h + c) % ring]

    def stage_queries(h, unit, reg):
        pltpu.matmul_push_rhs(q_s[h, :, unit * LANES : (unit + 1) * LANES], reg, unit)

    def score(h, unit, chunks, reg):
        for c in chunks:
            rows = k_s[slot, c * ROWS : (c + 1) * ROWS]
            pltpu.matmul_acc_lhs(chunk(unit, h, c), rows, load_staged_rhs=reg if c == 0 else None)

    def stage_weights(h, unit, tile, reg):
        parts = [
            jnp.exp2(pltpu.matmul_pop(chunk(unit, h, c))).astype(BF16)
            for c in range(tile * per_tile, (tile + 1) * per_tile)
        ]
        pltpu.matmul_push_rhs(jnp.concatenate(parts, axis=0), reg, unit)

    def mix(h, unit, tile, reg):
        rows = v_s[slot, h, :, tile * LANES : (tile + 1) * LANES]
        pltpu.matmul_acc_lhs(value_acc[unit][h], rows, load_staged_rhs=reg)

    for u in units:
        stage_queries(0, u, 0)
    for u in units:
        score(0, u, range(per_head), 0)
    for u in units:
        stage_queries(1, u, 1)
    reg = 1
    for h in range(HEADS):
        if h + 1 < HEADS:
            for u in units:
                score(h + 1, u, range(per_tile), reg)
        for u in units:
            stage_weights(h, u, 0, 1 - reg)
        if h + 1 < HEADS:
            for u in units:
                score(h + 1, u, range(per_tile, per_head), None)
        for u in units:
            stage_weights(h, u, 1, reg)
        for u in units:
            mix(h, u, 0, 1 - reg)
        if h + 2 < HEADS:
            for u in units:
                stage_queries(h + 2, u, 1 - reg)
        for u in units:
            mix(h, u, 1, reg)
        reg = 1 - reg


def add_pairs(n, q_s, k_s, v_s, store):
    ring = 6

    def inner(*accs):
        score_acc = [accs[:ring], accs[ring : 2 * ring]]
        value_acc = [accs[2 * ring : 2 * ring + HEADS], accs[2 * ring + HEADS :]]
        if isinstance(n, int):
            for i in range(n):
                add_pair(i, q_s, k_s, v_s, score_acc, value_acc)
        else:

            @pl.loop(0, n)
            def _(i):
                add_pair(i, q_s, k_s, v_s, score_acc, value_acc)

        for h in range(HEADS):
            for u in range(2):
                store(h, slice(u * LANES, (u + 1) * LANES), pltpu.matmul_pop(value_acc[u][h]))

    scores = [pltpu.ACC(u)((ROWS, LANES), F32) for u in range(2) for _ in range(ring)]
    values = [pltpu.ACC(u)((VALUE_ROWS, LANES), F32) for u in range(2) for _ in range(HEADS)]
    pl.run_scoped(inner, *scores, *values)


def add_pair_running(slot, q_s, k_s, v_s, o_s, m_s):
    for h in range(HEADS):
        scores = product(k_s[slot], q_s[h])
        old = m_s[h]
        new = jnp.maximum(old, jnp.max(scores, axis=0, keepdims=True))
        weights = jnp.exp2(scores - new).astype(BF16)
        o_s[h] = o_s[h] * jnp.exp2(old - new) + product(v_s[slot, h], weights)
        m_s[h] = new


def front_kernel(
    sizes, nb_ref, vox_ref, cube_ref, cw_ref, w_ref,
    mixed_ref, q_ref, k_ref, v_ref, sum_ref, den_ref, wt_ref, qn_ref, kn_ref, pick_ref, got0, got1, got2, got3,
    w_s, a_s, b_s, normed_s, face_s, q_s, face_out, face_in, send_sem, recv_sem
):
    gx, gy = lax.axis_index("gx"), lax.axis_index("gy")
    n_gx, n_gy = sizes
    blocks, _, ch = vox_ref.shape
    width = ch // HEADS
    got = (got0, got1, got2, got3)
    up_x, down_x = lax.rem(gx + 1, n_gx), lax.rem(gx + n_gx - 1, n_gx)
    up_y, down_y = lax.rem(gy + 1, n_gy), lax.rem(gy + n_gy - 1, n_gy)
    peers = [(up_x, gy), (down_x, gy), (gx, up_y), (gx, down_y)]
    layers = [cube_ref.at[:, SIDE - 1], cube_ref.at[:, 0], cube_ref.at[:, :, SIDE - 1], cube_ref.at[:, :, 0]]

    barrier = pltpu.get_barrier_semaphore()
    for peer in peers:
        pl.semaphore_signal(barrier, inc=1, device_id=peer, device_id_type=MESH)
    pl.semaphore_wait(barrier, 4)

    copies = [
        pltpu.make_async_remote_copy(
            src_ref=layer, dst_ref=face_s.at[f], send_sem=face_out.at[f], recv_sem=face_in.at[f],
            device_id=peers[f], device_id_type=MESH,
        )
        for f, layer in enumerate(layers)
    ]
    for f in (2, 3, 0, 1):
        copies[f].start()

    def passing(b, side):
        return pltpu.make_async_remote_copy(
            src_ref=normed_s.at[b], dst_ref=got[side].at[b],
            send_sem=send_sem.at[side, b], recv_sem=recv_sem.at[side, b],
            device_id=peers[side], device_id_type=MESH,
        )

    def pass_on(b):
        for side in (2, 3, 0, 1):
            passing(b, side).start()

    pair_weights(cw_ref, w_s)
    q_s[...] = jnp.zeros(q_s.shape, q_s.dtype)
    wt_ref[...] = w_ref[...].astype(F32).T.astype(BF16)
    for copy in copies:
        copy.wait()
    faces = [face_s.at[f] for f in range(4)]

    @pl.loop(0, blocks)
    def _(b):
        def between():
            @pl.when(b > 0)
            def _():
                pass_on(b - 1)

        conv_block(b, nb_ref, vox_ref, faces, w_s, a_s, b_s, mixed_ref, normed_s, between)

    pass_on(blocks - 1)

    @pl.loop(0, blocks)
    def _(b):
        factor = math.log2(math.e) / math.sqrt(width)
        normed = normed_s[b]
        keys = jnp.dot(normed, w_ref[:, ch : 2 * ch], preferred_element_type=F32).astype(BF16)
        turned = lax.dot_general(wt_ref[...], normed, NT, preferred_element_type=F32)
        queries = (turned[:ch] * factor).astype(BF16)
        values = turned[2 * ch :].astype(BF16)
        q_ref[b], k_ref[b], v_ref[b] = queries, keys, values
        qn_ref[b] = largest_norm(queries, width)
        kn_ref[b] = largest_norm(turned[ch : 2 * ch], width)

    @pl.loop(0, blocks)
    def _(b):
        put_queries(q_ref[b], q_s, width)
        ones = jnp.ones((VALUE_ROWS - width, q_ref.shape[2]), BF16)

        def pair(slot, first):
            at = jnp.where(slot >= 0, slot, b)
            keys, values = k_ref[at], v_ref[at]
            for h in range(HEADS):
                scores = jnp.dot(keys, q_s[h], preferred_element_type=F32)
                weights = jnp.exp2(scores).astype(BF16)
                rows = jnp.concatenate([values[h * width : (h + 1) * width], ones], axis=0)
                if not first:
                    rows = jnp.where(slot >= 0, rows, jnp.zeros_like(rows))
                part = jnp.dot(rows, weights, preferred_element_type=F32)
                if first:
                    sum_ref[b, h * width : (h + 1) * width] = part[:width]
                    den_ref[b, h : h + 1] = part[width : width + 1]
                else:
                    sum_ref[b, h * width : (h + 1) * width] += part[:width]
                    den_ref[b, h : h + 1] += part[width : width + 1]

        pair(b, True)

        @pl.when(b > 0)
        def _():
            pair(nb_ref[b, 4], False)

        @pl.when(b < blocks - 1)
        def _():
            pair(nb_ref[b, 5], False)

    for side in range(4):
        last = jnp.int32(0)
        for b in range(blocks):
            slot = nb_ref[b, side]
            last = jnp.where(slot >= 0, slot, last)
            pick_ref[b, side] = last

    @pl.loop(0, blocks)
    def _(b):
        for side in range(4):
            passing(b, side).wait()


def back_kernel(
    nb_ref, cnt_ref, pick_ref, qn_ref, kn_ref, mixed_ref, q_ref, sum_ref, den_ref, k_any, v_any,
    r0, r1, r2, r3, w_ref, wt_ref, wo_ref, out_ref, q_s, k_s, v_s, o_s, m_s, key_s, value_s
):
    b = pl.program_id(0)
    ch = mixed_ref.shape[-1]
    width = ch // HEADS

    @pl.when(b == 0)
    def _():
        clear_operands(q_s, k_s, v_s)

    @pl.when(b >= cnt_ref[0])
    def _():
        out_ref[0] = jnp.zeros(out_ref.shape[1:], out_ref.dtype)

    @pl.when(b < cnt_ref[0])
    def _():
        n = jnp.int32(0)
        kn = kn_ref[b]
        for face in (4, 5):
            slot = nb_ref[b, face]
            kn = jnp.where(slot >= 0, jnp.maximum(kn, kn_ref[jnp.maximum(slot, 0)]), kn)
        for face, ref in enumerate((r0, r1, r2, r3)):
            there = nb_ref[b, face] >= 0

            def put(ref=ref, n=n, kn=kn):
                normed = padded(ref[0], 0, LANES)
                keys = product(normed, padded(w_ref[:, ch : 2 * ch], LANES, LANES))[:, :ch].astype(BF16)
                turned = product(padded(wt_ref[ch:], 0, LANES), normed, transpose=True)
                put_key_set(keys, turned[ch:].astype(BF16), k_s, v_s, n, width)
                return jnp.maximum(kn, largest_norm(turned[:ch], width))

            kn = lax.cond(there, put, lambda kn=kn: kn)
            n = jnp.where(there, n + 1, n)
        fast = qn_ref[b] * kn <= LIMIT * LIMIT

        def finish(take):
            parts = []
            for h in range(HEADS):
                total, weight = take(h)
                parts.append(total / weight)
            attended = jnp.concatenate(parts, axis=0).T.astype(BF16)
            moved = product(padded(attended, 0, LANES), padded(wo_ref[...], LANES, LANES))[:, :ch]
            out_ref[0] = (mixed_ref[0].astype(F32) + moved).astype(out_ref.dtype)

        @pl.when(fast)
        def _():
            @pl.when(n == 0)
            def _():
                o_s[...] = jnp.zeros(o_s.shape, F32)

            @pl.when(n > 0)
            def _():
                put_queries(q_ref[0], q_s, width)

                def store(h, lanes, value):
                    o_s[h, :, lanes] = value

                add_pairs(n, q_s, k_s, v_s, store)

            for h in range(HEADS):
                o_s[h, :width] += sum_ref[0, h * width : (h + 1) * width]
                o_s[h, width : width + 1] += den_ref[0, h : h + 1]

        @pl.when(jnp.logical_not(fast))
        def _():
            put_queries(q_ref[0], q_s, width)
            count = n
            for slot in (b, nb_ref[b, 4], nb_ref[b, 5]):

                @pl.when(slot >= 0)
                def _(slot=slot, count=count):
                    pltpu.sync_copy(k_any.at[slot], key_s)
                    pltpu.sync_copy(v_any.at[slot], value_s)
                    put_key_set(key_s[...], value_s[...], k_s, v_s, count, width)

                count = jnp.where(slot >= 0, count + 1, count)
            o_s[...] = jnp.zeros(o_s.shape, F32)
            m_s[...] = jnp.full(m_s.shape, -1e30, F32)

            @pl.loop(0, count)
            def _(i):
                add_pair_running(i, q_s, k_s, v_s, o_s, m_s)

        finish(lambda h: (o_s[h, :width], o_s[h, width : width + 1]))


def body(voxels, neighbours, block_count, conv_weight, qkv_weight, out_weight):
    blocks, vox, ch = voxels.shape
    cubes = voxels.reshape(blocks, SIDE, SIDE, SIDE, ch)
    vmem = pl.BlockSpec(memory_space=pltpu.VMEM)
    smem = pl.BlockSpec(memory_space=pltpu.SMEM)
    hbm = pl.BlockSpec(memory_space=pl.ANY)
    like = jax.ShapeDtypeStruct(voxels.shape, BF16)
    turned = jax.ShapeDtypeStruct((blocks, ch, vox), BF16)
    scalars = jax.ShapeDtypeStruct((blocks,), F32)
    n_gx, n_gy = lax.axis_size("gx"), lax.axis_size("gy")

    def operands(slots):
        return [
            pltpu.VMEM((HEADS, 2 * ch, vox), BF16),
            pltpu.VMEM((slots, vox, 2 * ch), BF16),
            pltpu.VMEM((slots, HEADS, VALUE_ROWS, vox), BF16),
        ]

    mixed, q, k, v, total, weight, wt, qn, kn, pick, *got = pl.pallas_call(
        functools.partial(front_kernel, (n_gx, n_gy)),
        out_shape=[
            like, turned, like, turned,
            jax.ShapeDtypeStruct((blocks, ch, vox), F32),
            jax.ShapeDtypeStruct((blocks, HEADS, vox), F32),
            jax.ShapeDtypeStruct((3 * ch, ch), BF16),
            scalars, scalars, jax.ShapeDtypeStruct((blocks, 4), jnp.int32),
        ] + [like] * 4,
        in_specs=[smem, vmem, hbm, vmem, vmem],
        out_specs=[vmem] * 7 + [smem] * 3 + [hbm] * 4,
        scratch_shapes=[
            pltpu.VMEM((36 * ch, 2 * ch), BF16),
            pltpu.VMEM((3, SIDE + 2, SIDE * SIDE + 2 * SIDE, ch), BF16),
            pltpu.VMEM((3, SIDE + 2, SIDE * SIDE, ch), BF16),
            pltpu.VMEM(voxels.shape, BF16),
            pltpu.VMEM((4, blocks, SIDE, SIDE, ch), BF16),
            pltpu.VMEM((HEADS, ch, vox), BF16),
            pltpu.SemaphoreType.DMA((4,)),
            pltpu.SemaphoreType.DMA((4,)),
            pltpu.SemaphoreType.DMA((4, blocks)),
            pltpu.SemaphoreType.DMA((4, blocks)),
        ],
        compiler_params=pltpu.CompilerParams(collective_id=0, has_side_effects=True),
        name="front",
    )(neighbours, voxels, cubes, conv_weight, qkv_weight)

    def block(*tail):
        return pl.BlockSpec((1,) + tail, lambda b, *_: (b,) + (0,) * len(tail))

    def whole(*shape):
        return pl.BlockSpec(shape, lambda b, *_: (0,) * len(shape))

    def across(face, *tail):
        return pl.BlockSpec((1,) + tail, lambda b, nb, cnt, pick: (pick[b, face],) + (0,) * len(tail))

    return pl.pallas_call(
        back_kernel,
        out_shape=like,
        grid_spec=pltpu.PrefetchScalarGridSpec(
            num_scalar_prefetch=3,
            grid=(blocks,),
            in_specs=[smem, smem, block(vox, ch), block(ch, vox), block(ch, vox), block(HEADS, vox), hbm, hbm]
            + [across(f, vox, ch) for f in range(4)]
            + [whole(ch, 3 * ch), whole(3 * ch, ch), whole(ch, ch)],
            out_specs=block(vox, ch),
            scratch_shapes=[
                *operands(7),
                pltpu.VMEM((HEADS, VALUE_ROWS, vox), F32),
                pltpu.VMEM((HEADS, 1, vox), F32),
                pltpu.VMEM((vox, ch), BF16),
                pltpu.VMEM((ch, vox), BF16),
            ],
        ),
        name="back",
    )(neighbours, block_count, pick, qn, kn, mixed, q, total, weight, k, v, *got, qkv_weight, wt, out_weight)


def solution(mesh):
    placed = (P(("gx", "gy"), None, None), P(("gx", "gy"), None), P(("gx", "gy")), P(), P(), P())
    return jax.shard_map(
        body, mesh=mesh, in_specs=placed, out_specs=P(("gx", "gy"), None, None), check_vma=False
    )
```

```python
import functools
import math

import jax
import jax.numpy as jnp
from jax import lax
from jax.experimental import pallas as pl
from jax.experimental.pallas import tpu as pltpu
from jax.sharding import PartitionSpec as P

HEADS = 4
SIDE = 8
LIMIT = 90.0
F32 = jnp.float32
BF16 = jnp.bfloat16
NT = (((1,), (1,)), ((), ()))
ROWS = 128
LANES = 256
VALUE_ROWS = 48
MESH = pl.DeviceIdType.MESH


def shifted_z(x, below, above):
    at = lax.broadcasted_iota(jnp.int32, x.shape, 1)
    down = pltpu.roll(jnp.where(at == SIDE - 1, below, x), 1, 1)
    up = pltpu.roll(jnp.where(at == 0, above, x), SIDE - 1, 1)
    return [down, x, up]


def conv_block(b, nb_ref, vox_ref, faces, w_s, a_s, b_s, mixed_ref, normed_ref, between):
    rows, ch = SIDE * SIDE, vox_ref.shape[-1]

    def picked(ref, face):
        slot = nb_ref[b, face]
        value = ref[jnp.maximum(slot, 0)].astype(F32).reshape(-1, SIDE, ch)
        return jnp.where(slot >= 0, value, 0.0)

    own = vox_ref[b].astype(F32).reshape(rows, SIDE, ch)
    inner = shifted_z(own, picked(vox_ref, 4), picked(vox_ref, 5))
    xm, xp, ym, yp = [shifted_z(picked(ref, f), 0.0, 0.0) for f, ref in enumerate(faces)]
    blank = jnp.zeros((SIDE, ch), F32)
    for e in range(3):
        for s in range(SIDE + 2):
            if s == 0 or s == SIDE + 1:
                mid = (xm if s == 0 else xp)[e].reshape(rows, ch)
                top = bottom = blank
            else:
                mid = inner[e][(s - 1) * SIDE : s * SIDE].reshape(rows, ch)
                top, bottom = ym[e][s - 1], yp[e][s - 1]
            a_s[e, s] = jnp.concatenate([top, mid, bottom], axis=0).astype(BF16)
            b_s[e, s] = mid.astype(BF16)
    between()

    def tile(c, e, unit):
        def slab(x):
            return b_s[e, x] if c == 1 else a_s[e, x, c * SIDE : c * SIDE + rows]

        pairs = [2 * k + 2 * unit for k in range(4)]
        return jnp.concatenate([jnp.concatenate([slab(x), slab(x + 1)], axis=1) for x in pairs], axis=0)

    def inner(*accs):
        for c in range(3):
            for e in range(3):
                for unit in range(2):
                    reg = (c * 3 + e) % 2
                    at = ((c * 3 + e) * 2 + unit) * LANES
                    pltpu.matmul_push_rhs(w_s[at : at + LANES], reg, unit)
                    pltpu.matmul_acc_lhs(accs[unit], tile(c, e, unit), load_staged_rhs=reg)
        return pltpu.matmul_pop(accs[0]) + pltpu.matmul_pop(accs[1])

    acc = pl.run_scoped(inner, *[pltpu.ACC(u)((4 * rows, LANES), F32) for u in range(2)])
    for k in range(4):
        for o in range(2):
            x = 2 * k + o
            here = own[x * SIDE : (x + 1) * SIDE].reshape(rows, ch)
            mixed = (here + acc[k * rows : (k + 1) * rows, o * ch : (o + 1) * ch]).astype(BF16)
            mixed_ref[b, x * rows : (x + 1) * rows] = mixed
            wide = mixed.astype(F32)
            square = jnp.mean(wide * wide, axis=-1, keepdims=True)
            normed_ref[b, x * rows : (x + 1) * rows] = (wide * lax.rsqrt(square + 1e-06)).astype(BF16)


def pair_weights(cw_ref, w_s):
    ch = cw_ref.shape[-1]
    for ce in range(9):
        for r in range(4):
            for o in range(2):
                row = (ce * 4 + r) * ch
                tap = r - o
                value = cw_ref[tap * 9 + ce] if 0 <= tap <= 2 else jnp.zeros((ch, ch), BF16)
                w_s[row : row + ch, o * ch : (o + 1) * ch] = value


def clear_operands(q_s, k_s, v_s):
    q_s[...] = jnp.zeros(q_s.shape, q_s.dtype)
    k_s[...] = jnp.zeros(k_s.shape, k_s.dtype)
    v_s[...] = jnp.ones(v_s.shape, v_s.dtype)


def put_queries(queries, q_s, width):
    for h in range(HEADS):
        q_s[h, h * width : (h + 1) * width] = queries[h * width : (h + 1) * width]


def put_key_set(keys, values, k_s, v_s, slot, width):
    k_s[slot, :, : HEADS * width] = keys
    for h in range(HEADS):
        v_s[slot, h, :width] = values[h * width : (h + 1) * width]


def largest_norm(x, width):
    wide = x.astype(F32)
    return jnp.max(jnp.sum((wide * wide).reshape(HEADS, width, -1), axis=1)) * 1.02


def product(lhs, rhs, transpose=False):
    m, depth = lhs.shape
    n = rhs.shape[0 if transpose else 1]
    halves = n // LANES == 1
    rows = m // 2 if halves else m

    def inner(*accs):
        for u in range(2):
            part = lhs[u * rows : (u + 1) * rows] if halves else lhs
            for t in range(depth // LANES):
                deep = slice(t * LANES, (t + 1) * LANES)
                wide = slice(0, LANES) if halves else slice(u * LANES, (u + 1) * LANES)
                tile = rhs[wide, deep] if transpose else rhs[deep, wide]
                pltpu.matmul_push_rhs(tile, t % 2, u, transpose=transpose)
                pltpu.matmul_acc_lhs(accs[u], part[:, deep], load_staged_rhs=t % 2)
        return jnp.concatenate([pltpu.matmul_pop(acc) for acc in accs], axis=0 if halves else 1)

    return pl.run_scoped(inner, *[pltpu.ACC(u)((rows, LANES), F32) for u in range(2)])


def padded(x, rows, cols):
    if x.shape[1] < cols:
        x = jnp.concatenate([x, jnp.zeros((x.shape[0], cols - x.shape[1]), x.dtype)], axis=1)
    if x.shape[0] < rows:
        x = jnp.concatenate([x, jnp.zeros((rows - x.shape[0], x.shape[1]), x.dtype)], axis=0)
    return x


def add_pair(slot, q_s, k_s, v_s, score_acc, value_acc, there=None):
    per_tile, per_head = LANES // ROWS, k_s.shape[1] // ROWS
    ring = len(score_acc[0])
    units = range(2)

    def chunk(unit, h, c):
        return score_acc[unit][(per_head * h + c) % ring]

    def stage_queries(h, unit, reg):
        pltpu.matmul_push_rhs(q_s[h, :, unit * LANES : (unit + 1) * LANES], reg, unit)

    def score(h, unit, chunks, reg):
        for c in chunks:
            rows = k_s[slot, c * ROWS : (c + 1) * ROWS]
            pltpu.matmul_acc_lhs(chunk(unit, h, c), rows, load_staged_rhs=reg if c == 0 else None)

    def stage_weights(h, unit, tile, reg):
        parts = [
            jnp.exp2(pltpu.matmul_pop(chunk(unit, h, c))).astype(BF16)
            for c in range(tile * per_tile, (tile + 1) * per_tile)
        ]
        pltpu.matmul_push_rhs(jnp.concatenate(parts, axis=0), reg, unit)

    def mix(h, unit, tile, reg):
        rows = v_s[slot, h, :, tile * LANES : (tile + 1) * LANES]
        if there is not None:
            rows = jnp.where(there, rows, jnp.zeros_like(rows))
        pltpu.matmul_acc_lhs(value_acc[unit][h], rows, load_staged_rhs=reg)

    for u in units:
        stage_queries(0, u, 0)
    for u in units:
        score(0, u, range(per_head), 0)
    for u in units:
        stage_queries(1, u, 1)
    reg = 1
    for h in range(HEADS):
        if h + 1 < HEADS:
            for u in units:
                score(h + 1, u, range(per_tile), reg)
        for u in units:
            stage_weights(h, u, 0, 1 - reg)
        if h + 1 < HEADS:
            for u in units:
                score(h + 1, u, range(per_tile, per_head), None)
        for u in units:
            stage_weights(h, u, 1, reg)
        for u in units:
            mix(h, u, 0, 1 - reg)
        if h + 2 < HEADS:
            for u in units:
                stage_queries(h + 2, u, 1 - reg)
        for u in units:
            mix(h, u, 1, reg)
        reg = 1 - reg


def add_pairs(visit, store):
    ring = 6

    def inner(*accs):
        score_acc = [accs[:ring], accs[ring : 2 * ring]]
        value_acc = [accs[2 * ring : 2 * ring + HEADS], accs[2 * ring + HEADS :]]
        visit(lambda slot, q_s, k_s, v_s, there=None: add_pair(slot, q_s, k_s, v_s, score_acc, value_acc, there))
        for h in range(HEADS):
            for u in range(2):
                store(h, slice(u * LANES, (u + 1) * LANES), pltpu.matmul_pop(value_acc[u][h]))

    scores = [pltpu.ACC(u)((ROWS, LANES), F32) for u in range(2) for _ in range(ring)]
    values = [pltpu.ACC(u)((VALUE_ROWS, LANES), F32) for u in range(2) for _ in range(HEADS)]
    pl.run_scoped(inner, *scores, *values)


def add_pair_running(slot, q_s, k_s, v_s, o_s, m_s):
    for h in range(HEADS):
        scores = product(k_s[slot], q_s[h])
        old = m_s[h]
        new = jnp.maximum(old, jnp.max(scores, axis=0, keepdims=True))
        weights = jnp.exp2(scores - new).astype(BF16)
        o_s[h] = o_s[h] * jnp.exp2(old - new) + product(v_s[slot, h], weights)
        m_s[h] = new


def front_kernel(
    sizes, nb_ref, vox_ref, cube_ref, cw_ref, w_ref,
    mixed_ref, q_ref, k_ref, v_ref, sum_ref, den_ref, wt_ref, qn_ref, kn_ref, pick_ref, got0, got1, got2, got3,
    w_s, a_s, b_s, normed_s, face_s, q_s, k_s, v_s, face_out, face_in, send_sem, recv_sem
):
    gx, gy = lax.axis_index("gx"), lax.axis_index("gy")
    n_gx, n_gy = sizes
    blocks, _, ch = vox_ref.shape
    width = ch // HEADS
    got = (got0, got1, got2, got3)
    up_x, down_x = lax.rem(gx + 1, n_gx), lax.rem(gx + n_gx - 1, n_gx)
    up_y, down_y = lax.rem(gy + 1, n_gy), lax.rem(gy + n_gy - 1, n_gy)
    peers = [(up_x, gy), (down_x, gy), (gx, up_y), (gx, down_y)]
    layers = [cube_ref.at[:, SIDE - 1], cube_ref.at[:, 0], cube_ref.at[:, :, SIDE - 1], cube_ref.at[:, :, 0]]

    barrier = pltpu.get_barrier_semaphore()
    for peer in peers:
        pl.semaphore_signal(barrier, inc=1, device_id=peer, device_id_type=MESH)
    pl.semaphore_wait(barrier, 4)

    copies = [
        pltpu.make_async_remote_copy(
            src_ref=layer, dst_ref=face_s.at[f], send_sem=face_out.at[f], recv_sem=face_in.at[f],
            device_id=peers[f], device_id_type=MESH,
        )
        for f, layer in enumerate(layers)
    ]
    for f in (2, 3, 0, 1):
        copies[f].start()

    def passing(b, side):
        return pltpu.make_async_remote_copy(
            src_ref=normed_s.at[b], dst_ref=got[side].at[b],
            send_sem=send_sem.at[side, b], recv_sem=recv_sem.at[side, b],
            device_id=peers[side], device_id_type=MESH,
        )

    def pass_on(b):
        for side in (2, 3, 0, 1):
            passing(b, side).start()

    pair_weights(cw_ref, w_s)
    clear_operands(q_s, k_s, v_s)
    wt_ref[...] = w_ref[...].astype(F32).T.astype(BF16)
    for copy in copies:
        copy.wait()
    faces = [face_s.at[f] for f in range(4)]

    @pl.loop(0, blocks)
    def _(b):
        def between():
            @pl.when(b > 0)
            def _():
                pass_on(b - 1)

        conv_block(b, nb_ref, vox_ref, faces, w_s, a_s, b_s, mixed_ref, normed_s, between)

    pass_on(blocks - 1)

    @pl.loop(0, blocks)
    def _(b):
        factor = math.log2(math.e) / math.sqrt(width)
        normed = normed_s[b]
        normed = padded(normed, 0, LANES)
        keys = product(normed, padded(w_ref[:, ch : 2 * ch], LANES, LANES))[:, :ch].astype(BF16)
        turned = product(padded(wt_ref[...], 0, LANES), normed, transpose=True)
        queries = (turned[:ch] * factor).astype(BF16)
        values = turned[2 * ch :].astype(BF16)
        q_ref[b], k_ref[b], v_ref[b] = queries, keys, values
        qn_ref[b] = largest_norm(queries, width)
        kn_ref[b] = largest_norm(turned[ch : 2 * ch], width)
        put_key_set(keys, values, k_s, v_s, b, width)

    @pl.loop(0, blocks)
    def _(b):
        put_queries(q_ref[b], q_s, width)

        def visit(add):
            @pl.loop(0, 3)
            def _(i):
                near = nb_ref[b, i + 3]
                there = jnp.logical_or(i == 0, near >= 0)
                slot = jnp.where(jnp.logical_and(i > 0, near >= 0), near, b)

                @pl.when(jnp.logical_and(jnp.logical_or(i != 1, b > 0), jnp.logical_or(i != 2, b < blocks - 1)))
                def _():
                    add(slot, q_s, k_s, v_s, there)

        def store(h, lanes, value):
            sum_ref[b, h * width : (h + 1) * width, lanes] = value[:width]
            den_ref[b, h : h + 1, lanes] = value[width : width + 1]

        add_pairs(visit, store)

    for side in range(4):
        last = jnp.int32(0)
        for b in range(blocks):
            slot = nb_ref[b, side]
            last = jnp.where(slot >= 0, slot, last)
            pick_ref[b, side] = last

    @pl.loop(0, blocks)
    def _(b):
        for side in range(4):
            passing(b, side).wait()


def back_kernel(
    nb_ref, cnt_ref, pick_ref, qn_ref, kn_ref, mixed_ref, q_ref, sum_ref, den_ref, k_any, v_any,
    r0, r1, r2, r3, w_ref, wt_ref, wo_ref, out_ref, q_s, k_s, v_s, o_s, m_s, key_s, value_s
):
    b = pl.program_id(0)
    ch = mixed_ref.shape[-1]
    width = ch // HEADS

    @pl.when(b == 0)
    def _():
        clear_operands(q_s, k_s, v_s)

    @pl.when(b >= cnt_ref[0])
    def _():
        out_ref[0] = jnp.zeros(out_ref.shape[1:], out_ref.dtype)

    @pl.when(b < cnt_ref[0])
    def _():
        n = jnp.int32(0)
        kn = kn_ref[b]
        for face in (4, 5):
            slot = nb_ref[b, face]
            kn = jnp.where(slot >= 0, jnp.maximum(kn, kn_ref[jnp.maximum(slot, 0)]), kn)
        for face, ref in enumerate((r0, r1, r2, r3)):
            there = nb_ref[b, face] >= 0

            def put(ref=ref, n=n, kn=kn):
                normed = padded(ref[0], 0, LANES)
                keys = product(normed, padded(w_ref[:, ch : 2 * ch], LANES, LANES))[:, :ch].astype(BF16)
                turned = product(padded(wt_ref[ch:], 0, LANES), normed, transpose=True)
                put_key_set(keys, turned[ch:].astype(BF16), k_s, v_s, n, width)
                return jnp.maximum(kn, largest_norm(turned[:ch], width))

            kn = lax.cond(there, put, lambda kn=kn: kn)
            n = jnp.where(there, n + 1, n)
        fast = qn_ref[b] * kn <= LIMIT * LIMIT

        def finish(take):
            parts = []
            for h in range(HEADS):
                total, weight = take(h)
                parts.append(total / weight)
            attended = jnp.concatenate(parts, axis=0).T.astype(BF16)
            moved = product(padded(attended, 0, LANES), padded(wo_ref[...], LANES, LANES))[:, :ch]
            out_ref[0] = (mixed_ref[0].astype(F32) + moved).astype(out_ref.dtype)

        @pl.when(fast)
        def _():
            @pl.when(n == 0)
            def _():
                o_s[...] = jnp.zeros(o_s.shape, F32)

            @pl.when(n > 0)
            def _():
                put_queries(q_ref[0], q_s, width)

                def store(h, lanes, value):
                    o_s[h, :, lanes] = value

                def visit(add):
                    @pl.loop(0, n)
                    def _(i):
                        add(i, q_s, k_s, v_s)

                add_pairs(visit, store)

            for h in range(HEADS):
                o_s[h, :width] += sum_ref[0, h * width : (h + 1) * width]
                o_s[h, width : width + 1] += den_ref[0, h : h + 1]

        @pl.when(jnp.logical_not(fast))
        def _():
            put_queries(q_ref[0], q_s, width)
            count = n
            for slot in (b, nb_ref[b, 4], nb_ref[b, 5]):

                @pl.when(slot >= 0)
                def _(slot=slot, count=count):
                    pltpu.sync_copy(k_any.at[slot], key_s)
                    pltpu.sync_copy(v_any.at[slot], value_s)
                    put_key_set(key_s[...], value_s[...], k_s, v_s, count, width)

                count = jnp.where(slot >= 0, count + 1, count)
            o_s[...] = jnp.zeros(o_s.shape, F32)
            m_s[...] = jnp.full(m_s.shape, -1e30, F32)

            @pl.loop(0, count)
            def _(i):
                add_pair_running(i, q_s, k_s, v_s, o_s, m_s)

        finish(lambda h: (o_s[h, :width], o_s[h, width : width + 1]))


def body(voxels, neighbours, block_count, conv_weight, qkv_weight, out_weight):
    blocks, vox, ch = voxels.shape
    cubes = voxels.reshape(blocks, SIDE, SIDE, SIDE, ch)
    vmem = pl.BlockSpec(memory_space=pltpu.VMEM)
    smem = pl.BlockSpec(memory_space=pltpu.SMEM)
    hbm = pl.BlockSpec(memory_space=pl.ANY)
    like = jax.ShapeDtypeStruct(voxels.shape, BF16)
    turned = jax.ShapeDtypeStruct((blocks, ch, vox), BF16)
    scalars = jax.ShapeDtypeStruct((blocks,), F32)
    n_gx, n_gy = lax.axis_size("gx"), lax.axis_size("gy")

    def operands(slots):
        return [
            pltpu.VMEM((HEADS, 2 * ch, vox), BF16),
            pltpu.VMEM((slots, vox, 2 * ch), BF16),
            pltpu.VMEM((slots, HEADS, VALUE_ROWS, vox), BF16),
        ]

    mixed, q, k, v, total, weight, wt, qn, kn, pick, *got = pl.pallas_call(
        functools.partial(front_kernel, (n_gx, n_gy)),
        out_shape=[
            like, turned, like, turned,
            jax.ShapeDtypeStruct((blocks, ch, vox), F32),
            jax.ShapeDtypeStruct((blocks, HEADS, vox), F32),
            jax.ShapeDtypeStruct((3 * ch, ch), BF16),
            scalars, scalars, jax.ShapeDtypeStruct((blocks, 4), jnp.int32),
        ] + [like] * 4,
        in_specs=[smem, vmem, hbm, vmem, vmem],
        out_specs=[vmem] * 7 + [smem] * 3 + [hbm] * 4,
        scratch_shapes=[
            pltpu.VMEM((36 * ch, 2 * ch), BF16),
            pltpu.VMEM((3, SIDE + 2, SIDE * SIDE + 2 * SIDE, ch), BF16),
            pltpu.VMEM((3, SIDE + 2, SIDE * SIDE, ch), BF16),
            pltpu.VMEM(voxels.shape, BF16),
            pltpu.VMEM((4, blocks, SIDE, SIDE, ch), BF16),
            *operands(blocks),
            pltpu.SemaphoreType.DMA((4,)),
            pltpu.SemaphoreType.DMA((4,)),
            pltpu.SemaphoreType.DMA((4, blocks)),
            pltpu.SemaphoreType.DMA((4, blocks)),
        ],
        compiler_params=pltpu.CompilerParams(collective_id=0, has_side_effects=True),
        name="front",
    )(neighbours, voxels, cubes, conv_weight, qkv_weight)

    def block(*tail):
        return pl.BlockSpec((1,) + tail, lambda b, *_: (b,) + (0,) * len(tail))

    def whole(*shape):
        return pl.BlockSpec(shape, lambda b, *_: (0,) * len(shape))

    def across(face, *tail):
        return pl.BlockSpec((1,) + tail, lambda b, nb, cnt, pick: (pick[b, face],) + (0,) * len(tail))

    return pl.pallas_call(
        back_kernel,
        out_shape=like,
        grid_spec=pltpu.PrefetchScalarGridSpec(
            num_scalar_prefetch=3,
            grid=(blocks,),
            in_specs=[smem, smem, block(vox, ch), block(ch, vox), block(ch, vox), block(HEADS, vox), hbm, hbm]
            + [across(f, vox, ch) for f in range(4)]
            + [whole(ch, 3 * ch), whole(3 * ch, ch), whole(ch, ch)],
            out_specs=block(vox, ch),
            scratch_shapes=[
                *operands(7),
                pltpu.VMEM((HEADS, VALUE_ROWS, vox), F32),
                pltpu.VMEM((HEADS, 1, vox), F32),
                pltpu.VMEM((vox, ch), BF16),
                pltpu.VMEM((ch, vox), BF16),
            ],
        ),
        name="back",
    )(neighbours, block_count, pick, qn, kn, mixed, q, total, weight, k, v, *got, qkv_weight, wt, out_weight)


def solution(mesh):
    placed = (P(("gx", "gy"), None, None), P(("gx", "gy"), None), P(("gx", "gy")), P(), P(), P())
    return jax.shard_map(
        body, mesh=mesh, in_specs=placed, out_specs=P(("gx", "gy"), None, None), check_vma=False
    )
```

```python
import functools
import math

import jax
import jax.numpy as jnp
from jax import lax
from jax.experimental import pallas as pl
from jax.experimental.pallas import tpu as pltpu
from jax.sharding import PartitionSpec as P

HEADS = 4
SIDE = 8
LIMIT = 90.0
F32 = jnp.float32
BF16 = jnp.bfloat16
NT = (((1,), (1,)), ((), ()))
ROWS = 128
LANES = 256
VALUE_ROWS = 48
MESH = pl.DeviceIdType.MESH


def shifted_z(x, below, above):
    at = lax.broadcasted_iota(jnp.int32, x.shape, 1)
    down = pltpu.roll(jnp.where(at == SIDE - 1, below, x), 1, 1)
    up = pltpu.roll(jnp.where(at == 0, above, x), SIDE - 1, 1)
    return [down, x, up]


def picked(ref, slot, ch):
    value = ref[jnp.maximum(slot, 0)].astype(F32).reshape(-1, SIDE, ch)
    return jnp.where(slot >= 0, value, 0.0)


def lay_interior(b, nb_ref, vox_s, a_s, b_s):
    rows, ch = SIDE * SIDE, vox_s.shape[-1]
    own = vox_s[b].astype(F32).reshape(rows, SIDE, ch)
    inner = shifted_z(own, picked(vox_s, nb_ref[b, 4], ch), picked(vox_s, nb_ref[b, 5], ch))
    blank = jnp.zeros((SIDE, ch), F32)
    for e in range(3):
        for s in range(1, SIDE + 1):
            mid = inner[e][(s - 1) * SIDE : s * SIDE].reshape(rows, ch)
            a_s[b, e, s] = jnp.concatenate([blank, mid, blank], axis=0).astype(BF16)
            b_s[b, e, s] = mid.astype(BF16)


def lay_faces(b, nb_ref, faces, a_s, b_s):
    rows, ch = SIDE * SIDE, a_s.shape[-1]
    xm, xp, ym, yp = [shifted_z(picked(ref, nb_ref[b, f], ch), 0.0, 0.0) for f, ref in enumerate(faces)]
    blank = jnp.zeros((SIDE, ch), F32)
    end = rows + 2 * SIDE
    for e in range(3):
        for s, face in ((0, xm), (SIDE + 1, xp)):
            mid = face[e].reshape(rows, ch)
            a_s[b, e, s] = jnp.concatenate([blank, mid, blank], axis=0).astype(BF16)
            b_s[b, e, s] = mid.astype(BF16)
        for s in range(1, SIDE + 1):
            first = a_s[b, e, s, : 2 * SIDE].astype(F32)
            last = a_s[b, e, s, end - 2 * SIDE :].astype(F32)
            a_s[b, e, s, : 2 * SIDE] = jnp.concatenate([ym[e][s - 1], first[SIDE:]], axis=0).astype(BF16)
            a_s[b, e, s, end - 2 * SIDE :] = jnp.concatenate([last[:SIDE], yp[e][s - 1]], axis=0).astype(BF16)


def conv_block(b, vox_s, w_s, a_s, b_s, mixed_ref, normed_ref):
    rows, ch = SIDE * SIDE, vox_s.shape[-1]
    own = vox_s[b].astype(F32).reshape(rows, SIDE, ch)

    def tile(c, e, unit):
        def slab(x):
            return b_s[b, e, x] if c == 1 else a_s[b, e, x, c * SIDE : c * SIDE + rows]

        pairs = [2 * k + 2 * unit for k in range(4)]
        return jnp.concatenate([jnp.concatenate([slab(x), slab(x + 1)], axis=1) for x in pairs], axis=0)

    def inner(*accs):
        for c in range(3):
            for e in range(3):
                for unit in range(2):
                    reg = (c * 3 + e) % 2
                    at = ((c * 3 + e) * 2 + unit) * LANES
                    pltpu.matmul_push_rhs(w_s[at : at + LANES], reg, unit)
                    pltpu.matmul_acc_lhs(accs[unit], tile(c, e, unit), load_staged_rhs=reg)
        return pltpu.matmul_pop(accs[0]) + pltpu.matmul_pop(accs[1])

    acc = pl.run_scoped(inner, *[pltpu.ACC(u)((4 * rows, LANES), F32) for u in range(2)])
    for k in range(4):
        for o in range(2):
            x = 2 * k + o
            here = own[x * SIDE : (x + 1) * SIDE].reshape(rows, ch)
            mixed = (here + acc[k * rows : (k + 1) * rows, o * ch : (o + 1) * ch]).astype(BF16)
            mixed_ref[b, x * rows : (x + 1) * rows] = mixed
            wide = mixed.astype(F32)
            square = jnp.mean(wide * wide, axis=-1, keepdims=True)
            normed_ref[b, x * rows : (x + 1) * rows] = (wide * lax.rsqrt(square + 1e-06)).astype(BF16)


def pair_weights(cw_ref, w_s):
    ch = cw_ref.shape[-1]
    for ce in range(9):
        for r in range(4):
            for o in range(2):
                row = (ce * 4 + r) * ch
                tap = r - o
                value = cw_ref[tap * 9 + ce] if 0 <= tap <= 2 else jnp.zeros((ch, ch), BF16)
                w_s[row : row + ch, o * ch : (o + 1) * ch] = value


def clear_operands(q_s, k_s, v_s):
    q_s[...] = jnp.zeros(q_s.shape, q_s.dtype)
    k_s[...] = jnp.zeros(k_s.shape, k_s.dtype)
    v_s[...] = jnp.ones(v_s.shape, v_s.dtype)


def put_queries(queries, q_s, width):
    for h in range(HEADS):
        q_s[h, h * width : (h + 1) * width] = queries[h * width : (h + 1) * width]


def put_key_set(keys, values, k_s, v_s, slot, width):
    k_s[slot, :, : HEADS * width] = keys
    for h in range(HEADS):
        v_s[slot, h, :width] = values[h * width : (h + 1) * width]


def largest_norm(x, width):
    wide = x.astype(F32)
    return jnp.max(jnp.sum((wide * wide).reshape(HEADS, width, -1), axis=1)) * 1.02


def product(lhs, rhs, transpose=False):
    m, depth = lhs.shape
    n = rhs.shape[0 if transpose else 1]
    halves = n // LANES == 1
    rows = m // 2 if halves else m

    def inner(*accs):
        for u in range(2):
            part = lhs[u * rows : (u + 1) * rows] if halves else lhs
            for t in range(depth // LANES):
                deep = slice(t * LANES, (t + 1) * LANES)
                wide = slice(0, LANES) if halves else slice(u * LANES, (u + 1) * LANES)
                tile = rhs[wide, deep] if transpose else rhs[deep, wide]
                pltpu.matmul_push_rhs(tile, t % 2, u, transpose=transpose)
                pltpu.matmul_acc_lhs(accs[u], part[:, deep], load_staged_rhs=t % 2)
        return jnp.concatenate([pltpu.matmul_pop(acc) for acc in accs], axis=0 if halves else 1)

    return pl.run_scoped(inner, *[pltpu.ACC(u)((rows, LANES), F32) for u in range(2)])


def padded(x, rows, cols):
    if x.shape[1] < cols:
        x = jnp.concatenate([x, jnp.zeros((x.shape[0], cols - x.shape[1]), x.dtype)], axis=1)
    if x.shape[0] < rows:
        x = jnp.concatenate([x, jnp.zeros((rows - x.shape[0], x.shape[1]), x.dtype)], axis=0)
    return x


def add_pair(slot, q_s, k_s, v_s, score_acc, value_acc, there=None):
    per_tile, per_head = LANES // ROWS, k_s.shape[1] // ROWS
    ring = len(score_acc[0])
    units = range(2)

    def chunk(unit, h, c):
        return score_acc[unit][(per_head * h + c) % ring]

    def stage_queries(h, unit, reg):
        pltpu.matmul_push_rhs(q_s[h, :, unit * LANES : (unit + 1) * LANES], reg, unit)

    def score(h, unit, chunks, reg):
        for c in chunks:
            rows = k_s[slot, c * ROWS : (c + 1) * ROWS]
            pltpu.matmul_acc_lhs(chunk(unit, h, c), rows, load_staged_rhs=reg if c == 0 else None)

    def stage_weights(h, unit, tile, reg):
        parts = [
            jnp.exp2(pltpu.matmul_pop(chunk(unit, h, c))).astype(BF16)
            for c in range(tile * per_tile, (tile + 1) * per_tile)
        ]
        pltpu.matmul_push_rhs(jnp.concatenate(parts, axis=0), reg, unit)

    def mix(h, unit, tile, reg):
        rows = v_s[slot, h, :, tile * LANES : (tile + 1) * LANES]
        if there is not None:
            rows = jnp.where(there, rows, jnp.zeros_like(rows))
        pltpu.matmul_acc_lhs(value_acc[unit][h], rows, load_staged_rhs=reg)

    for u in units:
        stage_queries(0, u, 0)
    for u in units:
        score(0, u, range(per_head), 0)
    for u in units:
        stage_queries(1, u, 1)
    reg = 1
    for h in range(HEADS):
        if h + 1 < HEADS:
            for u in units:
                score(h + 1, u, range(per_tile), reg)
        for u in units:
            stage_weights(h, u, 0, 1 - reg)
        if h + 1 < HEADS:
            for u in units:
                score(h + 1, u, range(per_tile, per_head), None)
        for u in units:
            stage_weights(h, u, 1, reg)
        for u in units:
            mix(h, u, 0, 1 - reg)
        if h + 2 < HEADS:
            for u in units:
                stage_queries(h + 2, u, 1 - reg)
        for u in units:
            mix(h, u, 1, reg)
        reg = 1 - reg


def add_pairs(visit, store):
    ring = 6

    def inner(*accs):
        score_acc = [accs[:ring], accs[ring : 2 * ring]]
        value_acc = [accs[2 * ring : 2 * ring + HEADS], accs[2 * ring + HEADS :]]
        visit(lambda slot, q_s, k_s, v_s, there=None: add_pair(slot, q_s, k_s, v_s, score_acc, value_acc, there))
        for h in range(HEADS):
            for u in range(2):
                store(h, slice(u * LANES, (u + 1) * LANES), pltpu.matmul_pop(value_acc[u][h]))

    scores = [pltpu.ACC(u)((ROWS, LANES), F32) for u in range(2) for _ in range(ring)]
    values = [pltpu.ACC(u)((VALUE_ROWS, LANES), F32) for u in range(2) for _ in range(HEADS)]
    pl.run_scoped(inner, *scores, *values)


def add_pair_running(slot, q_s, k_s, v_s, o_s, m_s):
    for h in range(HEADS):
        scores = product(k_s[slot], q_s[h])
        old = m_s[h]
        new = jnp.maximum(old, jnp.max(scores, axis=0, keepdims=True))
        weights = jnp.exp2(scores - new).astype(BF16)
        o_s[h] = o_s[h] * jnp.exp2(old - new) + product(v_s[slot, h], weights)
        m_s[h] = new


def front_kernel(
    sizes, nb_ref, vox_ref, cube_ref, cw_ref, w_ref,
    mixed_ref, q_ref, k_ref, v_ref, sum_ref, den_ref, wt_ref, qn_ref, kn_ref, pick_ref, got0, got1, got2, got3,
    w_s, a_s, b_s, normed_s, face_s, q_s, k_s, v_s, vox_s, cw_s, mixed_s, queries_s, keys_s, values_s, sum_s, den_s,
    face_out, face_in, send_sem, recv_sem, load_sem, save_sem
):
    gx, gy = lax.axis_index("gx"), lax.axis_index("gy")
    n_gx, n_gy = sizes
    blocks, _, ch = vox_s.shape
    width = ch // HEADS
    got = (got0, got1, got2, got3)
    up_x, down_x = lax.rem(gx + 1, n_gx), lax.rem(gx + n_gx - 1, n_gx)
    up_y, down_y = lax.rem(gy + 1, n_gy), lax.rem(gy + n_gy - 1, n_gy)
    peers = [(up_x, gy), (down_x, gy), (gx, up_y), (gx, down_y)]
    to = [gx < n_gx - 1, gx > 0, gy < n_gy - 1, gy > 0]
    since = [to[1], to[0], to[3], to[2]]
    order = (2, 3, 0, 1)
    layers = [cube_ref.at[:, SIDE - 1], cube_ref.at[:, 0], cube_ref.at[:, :, SIDE - 1], cube_ref.at[:, :, 0]]

    loads = [
        pltpu.make_async_copy(vox_ref, vox_s, load_sem.at[0]),
        pltpu.make_async_copy(cw_ref, cw_s, load_sem.at[1]),
    ]
    for load in loads:
        load.start()

    barrier = pltpu.get_barrier_semaphore()
    for side in order:

        @pl.when(to[side])
        def _(side=side):
            pl.semaphore_signal(barrier, inc=1, device_id=peers[side], device_id_type=MESH)

    pl.semaphore_wait(barrier, sum(there.astype(jnp.int32) for there in to))

    def face_copy(f):
        return pltpu.make_async_remote_copy(
            src_ref=layers[f], dst_ref=face_s.at[f], send_sem=face_out.at[f], recv_sem=face_in.at[f],
            device_id=peers[f], device_id_type=MESH,
        )

    def passing(b, side):
        return pltpu.make_async_remote_copy(
            src_ref=normed_s.at[b], dst_ref=got[side].at[b],
            send_sem=send_sem.at[side, b], recv_sem=recv_sem.at[side, b],
            device_id=peers[side], device_id_type=MESH,
        )

    def saves(b):
        pairs = (
            (mixed_s, mixed_ref), (queries_s, q_ref), (keys_s, k_ref), (values_s, v_ref), (sum_s, sum_ref), (den_s, den_ref)
        )
        return [
            pltpu.make_async_copy(here.at[b], there.at[b], save_sem.at[i, b]) for i, (here, there) in enumerate(pairs)
        ]

    def start_where(conditions, copy):
        for side in order:

            @pl.when(conditions[side])
            def _(side=side):
                copy(side).start()

    def wait_for(copy):
        for side in order:

            @pl.when(to[side])
            def _(side=side):
                copy(side).wait_send()

            @pl.when(since[side])
            def _(side=side):
                copy(side).wait_recv()

    start_where(to, face_copy)
    clear_operands(q_s, k_s, v_s)
    wt_ref[...] = w_ref[...].astype(F32).T.astype(BF16)
    loads[0].wait()

    @pl.loop(0, blocks)
    def _(b):
        lay_interior(b, nb_ref, vox_s, a_s, b_s)

    loads[1].wait()
    pair_weights(cw_s, w_s)
    wait_for(face_copy)
    faces = [face_s.at[f] for f in range(4)]

    @pl.loop(0, blocks)
    def _(b):
        lay_faces(b, nb_ref, faces, a_s, b_s)

        @pl.when(b > 0)
        def _():
            start_where(to, functools.partial(passing, b - 1))

        conv_block(b, vox_s, w_s, a_s, b_s, mixed_s, normed_s)

    start_where(to, functools.partial(passing, blocks - 1))

    @pl.loop(0, blocks)
    def _(b):
        factor = math.log2(math.e) / math.sqrt(width)
        normed = padded(normed_s[b], 0, LANES)
        keys = product(normed, padded(w_ref[:, ch : 2 * ch], LANES, LANES))[:, :ch].astype(BF16)
        turned = product(padded(wt_ref[...], 0, LANES), normed, transpose=True)
        queries = (turned[:ch] * factor).astype(BF16)
        values = turned[2 * ch :].astype(BF16)
        queries_s[b], keys_s[b], values_s[b] = queries, keys, values
        qn_ref[b] = largest_norm(queries, width)
        kn_ref[b] = largest_norm(turned[ch : 2 * ch], width)
        put_key_set(keys, values, k_s, v_s, b, width)

    @pl.loop(0, blocks)
    def _(b):
        put_queries(queries_s[b], q_s, width)

        def visit(add):
            @pl.loop(0, 3)
            def _(i):
                near = nb_ref[b, i + 3]
                there = jnp.logical_or(i == 0, near >= 0)
                slot = jnp.where(jnp.logical_and(i > 0, near >= 0), near, b)

                @pl.when(jnp.logical_and(jnp.logical_or(i != 1, b > 0), jnp.logical_or(i != 2, b < blocks - 1)))
                def _():
                    add(slot, q_s, k_s, v_s, there)

        def store(h, lanes, value):
            sum_s[b, h * width : (h + 1) * width, lanes] = value[:width]
            den_s[b, h : h + 1, lanes] = value[width : width + 1]

        add_pairs(visit, store)

        @pl.when(b > 0)
        def _():
            for save in saves(b - 1):
                save.start()

    for save in saves(blocks - 1):
        save.start()

    for side in range(4):
        last = jnp.int32(0)
        for b in range(blocks):
            slot = nb_ref[b, side]
            last = jnp.where(slot >= 0, slot, last)
            pick_ref[b, side] = last

    @pl.loop(0, blocks)
    def _(b):
        for save in saves(b):
            save.wait()
        wait_for(functools.partial(passing, b))


def back_kernel(
    nb_ref, cnt_ref, pick_ref, qn_ref, kn_ref, mixed_ref, q_ref, sum_ref, den_ref, k_any, v_any,
    r0, r1, r2, r3, w_ref, wt_ref, wo_ref, out_ref, q_s, k_s, v_s, o_s, m_s, key_s, value_s
):
    b = pl.program_id(0)
    ch = mixed_ref.shape[-1]
    width = ch // HEADS

    @pl.when(b == 0)
    def _():
        clear_operands(q_s, k_s, v_s)

    @pl.when(b >= cnt_ref[0])
    def _():
        out_ref[0] = jnp.zeros(out_ref.shape[1:], out_ref.dtype)

    @pl.when(b < cnt_ref[0])
    def _():
        n = jnp.int32(0)
        kn = kn_ref[b]
        for face in (4, 5):
            slot = nb_ref[b, face]
            kn = jnp.where(slot >= 0, jnp.maximum(kn, kn_ref[jnp.maximum(slot, 0)]), kn)
        for face, ref in enumerate((r0, r1, r2, r3)):
            there = nb_ref[b, face] >= 0

            def put(ref=ref, n=n, kn=kn):
                normed = padded(ref[0], 0, LANES)
                keys = product(normed, padded(w_ref[:, ch : 2 * ch], LANES, LANES))[:, :ch].astype(BF16)
                turned = product(padded(wt_ref[ch:], 0, LANES), normed, transpose=True)
                put_key_set(keys, turned[ch:].astype(BF16), k_s, v_s, n, width)
                return jnp.maximum(kn, largest_norm(turned[:ch], width))

            kn = lax.cond(there, put, lambda kn=kn: kn)
            n = jnp.where(there, n + 1, n)
        fast = qn_ref[b] * kn <= LIMIT * LIMIT

        def finish(take):
            parts = []
            for h in range(HEADS):
                total, weight = take(h)
                parts.append(total / weight)
            attended = jnp.concatenate(parts, axis=0).T.astype(BF16)
            moved = product(padded(attended, 0, LANES), padded(wo_ref[...], LANES, LANES))[:, :ch]
            out_ref[0] = (mixed_ref[0].astype(F32) + moved).astype(out_ref.dtype)

        @pl.when(fast)
        def _():
            @pl.when(n == 0)
            def _():
                o_s[...] = jnp.zeros(o_s.shape, F32)

            @pl.when(n > 0)
            def _():
                put_queries(q_ref[0], q_s, width)

                def store(h, lanes, value):
                    o_s[h, :, lanes] = value

                def visit(add):
                    @pl.loop(0, n)
                    def _(i):
                        add(i, q_s, k_s, v_s)

                add_pairs(visit, store)

            for h in range(HEADS):
                o_s[h, :width] += sum_ref[0, h * width : (h + 1) * width]
                o_s[h, width : width + 1] += den_ref[0, h : h + 1]

        @pl.when(jnp.logical_not(fast))
        def _():
            put_queries(q_ref[0], q_s, width)
            count = n
            for slot in (b, nb_ref[b, 4], nb_ref[b, 5]):

                @pl.when(slot >= 0)
                def _(slot=slot, count=count):
                    pltpu.sync_copy(k_any.at[slot], key_s)
                    pltpu.sync_copy(v_any.at[slot], value_s)
                    put_key_set(key_s[...], value_s[...], k_s, v_s, count, width)

                count = jnp.where(slot >= 0, count + 1, count)
            o_s[...] = jnp.zeros(o_s.shape, F32)
            m_s[...] = jnp.full(m_s.shape, -1e30, F32)

            @pl.loop(0, count)
            def _(i):
                add_pair_running(i, q_s, k_s, v_s, o_s, m_s)

        finish(lambda h: (o_s[h, :width], o_s[h, width : width + 1]))


def body(voxels, neighbours, block_count, conv_weight, qkv_weight, out_weight):
    blocks, vox, ch = voxels.shape
    cubes = voxels.reshape(blocks, SIDE, SIDE, SIDE, ch)
    vmem = pl.BlockSpec(memory_space=pltpu.VMEM)
    smem = pl.BlockSpec(memory_space=pltpu.SMEM)
    hbm = pl.BlockSpec(memory_space=pl.ANY)
    like = jax.ShapeDtypeStruct(voxels.shape, BF16)
    turned = jax.ShapeDtypeStruct((blocks, ch, vox), BF16)
    scalars = jax.ShapeDtypeStruct((blocks,), F32)
    n_gx, n_gy = lax.axis_size("gx"), lax.axis_size("gy")

    def operands(slots):
        return [
            pltpu.VMEM((HEADS, 2 * ch, vox), BF16),
            pltpu.VMEM((slots, vox, 2 * ch), BF16),
            pltpu.VMEM((slots, HEADS, VALUE_ROWS, vox), BF16),
        ]

    mixed, q, k, v, total, weight, wt, qn, kn, pick, *got = pl.pallas_call(
        functools.partial(front_kernel, (n_gx, n_gy)),
        out_shape=[
            like, turned, like, turned,
            jax.ShapeDtypeStruct((blocks, ch, vox), F32),
            jax.ShapeDtypeStruct((blocks, HEADS, vox), F32),
            jax.ShapeDtypeStruct((3 * ch, ch), BF16),
            scalars, scalars, jax.ShapeDtypeStruct((blocks, 4), jnp.int32),
        ] + [like] * 4,
        in_specs=[smem, hbm, hbm, hbm, vmem],
        out_specs=[hbm] * 6 + [vmem] + [smem] * 3 + [hbm] * 4,
        scratch_shapes=[
            pltpu.VMEM((36 * ch, 2 * ch), BF16),
            pltpu.VMEM((blocks, 3, SIDE + 2, SIDE * SIDE + 2 * SIDE, ch), BF16),
            pltpu.VMEM((blocks, 3, SIDE + 2, SIDE * SIDE, ch), BF16),
            pltpu.VMEM(voxels.shape, BF16),
            pltpu.VMEM((4, blocks, SIDE, SIDE, ch), BF16),
            *operands(blocks),
            pltpu.VMEM(voxels.shape, BF16),
            pltpu.VMEM(conv_weight.shape, BF16),
            pltpu.VMEM(voxels.shape, BF16),
            pltpu.VMEM((blocks, ch, vox), BF16),
            pltpu.VMEM(voxels.shape, BF16),
            pltpu.VMEM((blocks, ch, vox), BF16),
            pltpu.VMEM((blocks, ch, vox), F32),
            pltpu.VMEM((blocks, HEADS, vox), F32),
            pltpu.SemaphoreType.DMA((4,)),
            pltpu.SemaphoreType.DMA((4,)),
            pltpu.SemaphoreType.DMA((4, blocks)),
            pltpu.SemaphoreType.DMA((4, blocks)),
            pltpu.SemaphoreType.DMA((2,)),
            pltpu.SemaphoreType.DMA((6, blocks)),
        ],
        compiler_params=pltpu.CompilerParams(collective_id=0, has_side_effects=True),
        name="front",
    )(neighbours, voxels, cubes, conv_weight, qkv_weight)

    def block(*tail):
        return pl.BlockSpec((1,) + tail, lambda b, *_: (b,) + (0,) * len(tail))

    def whole(*shape):
        return pl.BlockSpec(shape, lambda b, *_: (0,) * len(shape))

    def across(face, *tail):
        return pl.BlockSpec((1,) + tail, lambda b, nb, cnt, pick: (pick[b, face],) + (0,) * len(tail))

    return pl.pallas_call(
        back_kernel,
        out_shape=like,
        grid_spec=pltpu.PrefetchScalarGridSpec(
            num_scalar_prefetch=3,
            grid=(blocks,),
            in_specs=[smem, smem, block(vox, ch), block(ch, vox), block(ch, vox), block(HEADS, vox), hbm, hbm]
            + [across(f, vox, ch) for f in range(4)]
            + [whole(ch, 3 * ch), whole(3 * ch, ch), whole(ch, ch)],
            out_specs=block(vox, ch),
            scratch_shapes=[
                *operands(7),
                pltpu.VMEM((HEADS, VALUE_ROWS, vox), F32),
                pltpu.VMEM((HEADS, 1, vox), F32),
                pltpu.VMEM((vox, ch), BF16),
                pltpu.VMEM((ch, vox), BF16),
            ],
        ),
        name="back",
    )(neighbours, block_count, pick, qn, kn, mixed, q, total, weight, k, v, *got, qkv_weight, wt, out_weight)


def solution(mesh):
    placed = (P(("gx", "gy"), None, None), P(("gx", "gy"), None), P(("gx", "gy")), P(), P(), P())
    return jax.shard_map(
        body, mesh=mesh, in_specs=placed, out_specs=P(("gx", "gy"), None, None), check_vma=False
    )
```

```python
import functools
import math

import jax
import jax.numpy as jnp
from jax import lax
from jax.experimental import pallas as pl
from jax.experimental.pallas import tpu as pltpu
from jax.sharding import PartitionSpec as P

HEADS = 4
SIDE = 8
LIMIT = 90.0
F32 = jnp.float32
BF16 = jnp.bfloat16
NT = (((1,), (1,)), ((), ()))
ROWS = 128
LANES = 256
VALUE_ROWS = 48
MESH = pl.DeviceIdType.MESH


def shifted_z(x, below, above):
    at = lax.broadcasted_iota(jnp.int32, x.shape, 1)
    down = pltpu.roll(jnp.where(at == SIDE - 1, below, x), 1, 1)
    up = pltpu.roll(jnp.where(at == 0, above, x), SIDE - 1, 1)
    return [down, x, up]


def picked(ref, slot, ch):
    value = ref[jnp.maximum(slot, 0)].astype(F32).reshape(-1, SIDE, ch)
    return jnp.where(slot >= 0, value, 0.0)


def lay_interior(b, nb_ref, vox_s, a_s, b_s):
    rows, ch = SIDE * SIDE, vox_s.shape[-1]
    own = vox_s[b].astype(F32).reshape(rows, SIDE, ch)
    inner = shifted_z(own, picked(vox_s, nb_ref[b, 4], ch), picked(vox_s, nb_ref[b, 5], ch))
    blank = jnp.zeros((SIDE, ch), F32)
    for e in range(3):
        for s in range(1, SIDE + 1):
            mid = inner[e][(s - 1) * SIDE : s * SIDE].reshape(rows, ch)
            a_s[b, e, s] = jnp.concatenate([blank, mid, blank], axis=0).astype(BF16)
            b_s[b, e, s] = mid.astype(BF16)


def lay_faces(b, nb_ref, faces, a_s, b_s):
    rows, ch = SIDE * SIDE, a_s.shape[-1]
    xm, xp, ym, yp = [shifted_z(picked(ref, nb_ref[b, f], ch), 0.0, 0.0) for f, ref in enumerate(faces)]
    blank = jnp.zeros((SIDE, ch), F32)
    end = rows + 2 * SIDE
    for e in range(3):
        for s, face in ((0, xm), (SIDE + 1, xp)):
            mid = face[e].reshape(rows, ch)
            a_s[b, e, s] = jnp.concatenate([blank, mid, blank], axis=0).astype(BF16)
            b_s[b, e, s] = mid.astype(BF16)
        for s in range(1, SIDE + 1):
            first = a_s[b, e, s, : 2 * SIDE].astype(F32)
            last = a_s[b, e, s, end - 2 * SIDE :].astype(F32)
            a_s[b, e, s, : 2 * SIDE] = jnp.concatenate([ym[e][s - 1], first[SIDE:]], axis=0).astype(BF16)
            a_s[b, e, s, end - 2 * SIDE :] = jnp.concatenate([last[:SIDE], yp[e][s - 1]], axis=0).astype(BF16)


def conv_block(b, vox_s, w_s, a_s, b_s, mixed_ref, normed_ref):
    rows, ch = SIDE * SIDE, vox_s.shape[-1]
    own = vox_s[b].astype(F32).reshape(rows, SIDE, ch)

    def tile(c, e, unit):
        def slab(x):
            return b_s[b, e, x] if c == 1 else a_s[b, e, x, c * SIDE : c * SIDE + rows]

        pairs = [2 * k + 2 * unit for k in range(4)]
        return jnp.concatenate([jnp.concatenate([slab(x), slab(x + 1)], axis=1) for x in pairs], axis=0)

    def inner(*accs):
        for c in range(3):
            for e in range(3):
                for unit in range(2):
                    reg = (c * 3 + e) % 2
                    at = ((c * 3 + e) * 2 + unit) * LANES
                    pltpu.matmul_push_rhs(w_s[at : at + LANES], reg, unit)
                    pltpu.matmul_acc_lhs(accs[unit], tile(c, e, unit), load_staged_rhs=reg)
        return pltpu.matmul_pop(accs[0]) + pltpu.matmul_pop(accs[1])

    acc = pl.run_scoped(inner, *[pltpu.ACC(u)((4 * rows, LANES), F32) for u in range(2)])
    for k in range(4):
        for o in range(2):
            x = 2 * k + o
            here = own[x * SIDE : (x + 1) * SIDE].reshape(rows, ch)
            mixed = (here + acc[k * rows : (k + 1) * rows, o * ch : (o + 1) * ch]).astype(BF16)
            mixed_ref[b, x * rows : (x + 1) * rows] = mixed
            wide = mixed.astype(F32)
            square = jnp.mean(wide * wide, axis=-1, keepdims=True)
            normed_ref[b, x * rows : (x + 1) * rows] = (wide * lax.rsqrt(square + 1e-06)).astype(BF16)


def pair_weights(cw_ref, w_s):
    ch = cw_ref.shape[-1]
    for ce in range(9):
        for r in range(4):
            for o in range(2):
                row = (ce * 4 + r) * ch
                tap = r - o
                value = cw_ref[tap * 9 + ce] if 0 <= tap <= 2 else jnp.zeros((ch, ch), BF16)
                w_s[row : row + ch, o * ch : (o + 1) * ch] = value


def clear_operands(q_s, k_s, v_s):
    q_s[...] = jnp.zeros(q_s.shape, q_s.dtype)
    k_s[...] = jnp.zeros(k_s.shape, k_s.dtype)
    v_s[...] = jnp.ones(v_s.shape, v_s.dtype)


def put_queries(queries, q_s, width):
    for h in range(HEADS):
        q_s[h, h * width : (h + 1) * width] = queries[h * width : (h + 1) * width]


def put_key_set(keys, values, k_s, v_s, slot, width):
    k_s[slot, :, : HEADS * width] = keys
    for h in range(HEADS):
        v_s[slot, h, :width] = values[h * width : (h + 1) * width]


def largest_norm(x, width):
    wide = x.astype(F32)
    return jnp.max(jnp.sum((wide * wide).reshape(HEADS, width, -1), axis=1)) * 1.02


def products(*terms):
    plans = []
    for lhs, rhs, transpose in terms:
        halves = rhs.shape[0 if transpose else 1] == LANES
        plans.append((lhs, rhs, transpose, halves, lhs.shape[0] // 2 if halves else lhs.shape[0]))

    def inner(*accs):
        reg = 0
        for p, (lhs, rhs, transpose, halves, rows) in enumerate(plans):
            for t in range(lhs.shape[1] // LANES):
                deep = slice(t * LANES, (t + 1) * LANES)
                for u in range(2):
                    part = lhs[u * rows : (u + 1) * rows] if halves else lhs
                    wide = slice(0, LANES) if halves else slice(u * LANES, (u + 1) * LANES)
                    tile = rhs[wide, deep] if transpose else rhs[deep, wide]
                    pltpu.matmul_push_rhs(tile, reg, u, transpose=transpose)
                    pltpu.matmul_acc_lhs(accs[2 * p + u], part[:, deep], load_staged_rhs=reg)
                reg = 1 - reg
        return [
            jnp.concatenate([pltpu.matmul_pop(acc) for acc in accs[2 * p : 2 * p + 2]], axis=0 if plan[3] else 1)
            for p, plan in enumerate(plans)
        ]

    return pl.run_scoped(inner, *[pltpu.ACC(u)((plan[4], LANES), F32) for plan in plans for u in range(2)])


def product(lhs, rhs, transpose=False):
    return products((lhs, rhs, transpose))[0]


def padded(x, rows, cols):
    if x.shape[1] < cols:
        x = jnp.concatenate([x, jnp.zeros((x.shape[0], cols - x.shape[1]), x.dtype)], axis=1)
    if x.shape[0] < rows:
        x = jnp.concatenate([x, jnp.zeros((rows - x.shape[0], x.shape[1]), x.dtype)], axis=0)
    return x


def add_pair(slot, q_s, k_s, v_s, score_acc, value_acc, there=None):
    per_tile, per_head = LANES // ROWS, k_s.shape[1] // ROWS
    ring = len(score_acc[0])
    units = range(2)

    def chunk(unit, h, c):
        return score_acc[unit][(per_head * h + c) % ring]

    def stage_queries(h, unit, reg):
        pltpu.matmul_push_rhs(q_s[h, :, unit * LANES : (unit + 1) * LANES], reg, unit)

    def score(h, unit, chunks, reg):
        for c in chunks:
            rows = k_s[slot, c * ROWS : (c + 1) * ROWS]
            pltpu.matmul_acc_lhs(chunk(unit, h, c), rows, load_staged_rhs=reg if c == 0 else None)

    def stage_weights(h, unit, tile, reg):
        parts = [
            jnp.exp2(pltpu.matmul_pop(chunk(unit, h, c))).astype(BF16)
            for c in range(tile * per_tile, (tile + 1) * per_tile)
        ]
        pltpu.matmul_push_rhs(jnp.concatenate(parts, axis=0), reg, unit)

    def mix(h, unit, tile, reg):
        rows = v_s[slot, h, :, tile * LANES : (tile + 1) * LANES]
        if there is not None:
            rows = jnp.where(there, rows, jnp.zeros_like(rows))
        pltpu.matmul_acc_lhs(value_acc[unit][h], rows, load_staged_rhs=reg)

    for u in units:
        stage_queries(0, u, 0)
    for u in units:
        score(0, u, range(per_head), 0)
    for u in units:
        stage_queries(1, u, 1)
    reg = 1
    for h in range(HEADS):
        if h + 1 < HEADS:
            for u in units:
                score(h + 1, u, range(per_tile), reg)
        for u in units:
            stage_weights(h, u, 0, 1 - reg)
        if h + 1 < HEADS:
            for u in units:
                score(h + 1, u, range(per_tile, per_head), None)
        for u in units:
            stage_weights(h, u, 1, reg)
        for u in units:
            mix(h, u, 0, 1 - reg)
        if h + 2 < HEADS:
            for u in units:
                stage_queries(h + 2, u, 1 - reg)
        for u in units:
            mix(h, u, 1, reg)
        reg = 1 - reg


def add_pairs(visit, store):
    ring = 6

    def inner(*accs):
        score_acc = [accs[:ring], accs[ring : 2 * ring]]
        value_acc = [accs[2 * ring : 2 * ring + HEADS], accs[2 * ring + HEADS :]]
        visit(lambda slot, q_s, k_s, v_s, there=None: add_pair(slot, q_s, k_s, v_s, score_acc, value_acc, there))
        for h in range(HEADS):
            for u in range(2):
                store(h, slice(u * LANES, (u + 1) * LANES), pltpu.matmul_pop(value_acc[u][h]))

    scores = [pltpu.ACC(u)((ROWS, LANES), F32) for u in range(2) for _ in range(ring)]
    values = [pltpu.ACC(u)((VALUE_ROWS, LANES), F32) for u in range(2) for _ in range(HEADS)]
    pl.run_scoped(inner, *scores, *values)


def add_pair_running(slot, q_s, k_s, v_s, o_s, m_s):
    for h in range(HEADS):
        scores = product(k_s[slot], q_s[h])
        old = m_s[h]
        new = jnp.maximum(old, jnp.max(scores, axis=0, keepdims=True))
        weights = jnp.exp2(scores - new).astype(BF16)
        o_s[h] = o_s[h] * jnp.exp2(old - new) + product(v_s[slot, h], weights)
        m_s[h] = new


def front_kernel(
    sizes, nb_ref, vox_ref, cube_ref, cw_ref, w_ref,
    mixed_ref, q_ref, k_ref, v_ref, sum_ref, den_ref, wt_ref, qn_ref, kn_ref, got0, got1, got2, got3,
    w_s, a_s, b_s, normed_s, face_s, q_s, k_s, v_s, vox_s, cw_s, mixed_s, queries_s, keys_s, values_s, sum_s, den_s,
    face_out, face_in, send_sem, recv_sem, load_sem, save_sem
):
    gx, gy = lax.axis_index("gx"), lax.axis_index("gy")
    n_gx, n_gy = sizes
    blocks, _, ch = vox_s.shape
    width = ch // HEADS
    got = (got0, got1, got2, got3)
    up_x, down_x = lax.rem(gx + 1, n_gx), lax.rem(gx + n_gx - 1, n_gx)
    up_y, down_y = lax.rem(gy + 1, n_gy), lax.rem(gy + n_gy - 1, n_gy)
    peers = [(up_x, gy), (down_x, gy), (gx, up_y), (gx, down_y)]
    to = [gx < n_gx - 1, gx > 0, gy < n_gy - 1, gy > 0]
    since = [to[1], to[0], to[3], to[2]]
    order = (2, 3, 0, 1)
    layers = [cube_ref.at[:, SIDE - 1], cube_ref.at[:, 0], cube_ref.at[:, :, SIDE - 1], cube_ref.at[:, :, 0]]

    loads = [
        pltpu.make_async_copy(vox_ref, vox_s, load_sem.at[0]),
        pltpu.make_async_copy(cw_ref, cw_s, load_sem.at[1]),
    ]
    for load in loads:
        load.start()

    barrier = pltpu.get_barrier_semaphore()
    for side in order:

        @pl.when(to[side])
        def _(side=side):
            pl.semaphore_signal(barrier, inc=1, device_id=peers[side], device_id_type=MESH)

    pl.semaphore_wait(barrier, sum(there.astype(jnp.int32) for there in to))

    def face_copy(f):
        return pltpu.make_async_remote_copy(
            src_ref=layers[f], dst_ref=face_s.at[f], send_sem=face_out.at[f], recv_sem=face_in.at[f],
            device_id=peers[f], device_id_type=MESH,
        )

    def passing(b, side):
        return pltpu.make_async_remote_copy(
            src_ref=normed_s.at[b], dst_ref=got[side].at[b],
            send_sem=send_sem.at[side, b], recv_sem=recv_sem.at[side, b],
            device_id=peers[side], device_id_type=MESH,
        )

    def saves(b):
        pairs = (
            (mixed_s, mixed_ref), (queries_s, q_ref), (keys_s, k_ref), (values_s, v_ref), (sum_s, sum_ref), (den_s, den_ref)
        )
        return [
            pltpu.make_async_copy(here.at[b], there.at[b], save_sem.at[i, b]) for i, (here, there) in enumerate(pairs)
        ]

    def start_where(conditions, copy):
        for side in order:

            @pl.when(conditions[side])
            def _(side=side):
                copy(side).start()

    def wait_for(copy):
        for side in order:

            @pl.when(to[side])
            def _(side=side):
                copy(side).wait_send()

            @pl.when(since[side])
            def _(side=side):
                copy(side).wait_recv()

    start_where(to, face_copy)
    clear_operands(q_s, k_s, v_s)
    wt_ref[...] = w_ref[...].astype(F32).T.astype(BF16)
    loads[0].wait()

    @pl.loop(0, blocks)
    def _(b):
        lay_interior(b, nb_ref, vox_s, a_s, b_s)

    loads[1].wait()
    pair_weights(cw_s, w_s)
    wait_for(face_copy)
    faces = [face_s.at[f] for f in range(4)]

    @pl.loop(0, blocks)
    def _(b):
        lay_faces(b, nb_ref, faces, a_s, b_s)

        @pl.when(b > 0)
        def _():
            start_where(to, functools.partial(passing, b - 1))

        conv_block(b, vox_s, w_s, a_s, b_s, mixed_s, normed_s)

    start_where(to, functools.partial(passing, blocks - 1))

    @pl.loop(0, blocks)
    def _(b):
        factor = math.log2(math.e) / math.sqrt(width)
        normed = padded(normed_s[b], 0, LANES)
        keys, turned = products(
            (normed, padded(w_ref[:, ch : 2 * ch], LANES, LANES), False), (padded(wt_ref[...], 0, LANES), normed, True)
        )
        keys = keys[:, :ch].astype(BF16)
        queries = (turned[:ch] * factor).astype(BF16)
        values = turned[2 * ch :].astype(BF16)
        queries_s[b], keys_s[b], values_s[b] = queries, keys, values
        qn_ref[b] = largest_norm(queries, width)
        kn_ref[b] = largest_norm(turned[ch : 2 * ch], width)
        put_key_set(keys, values, k_s, v_s, b, width)

    @pl.loop(0, blocks)
    def _(b):
        put_queries(queries_s[b], q_s, width)

        def visit(add):
            @pl.loop(0, 3)
            def _(i):
                near = nb_ref[b, i + 3]
                there = jnp.logical_or(i == 0, near >= 0)
                slot = jnp.where(jnp.logical_and(i > 0, near >= 0), near, b)

                @pl.when(jnp.logical_and(jnp.logical_or(i != 1, b > 0), jnp.logical_or(i != 2, b < blocks - 1)))
                def _():
                    add(slot, q_s, k_s, v_s, there)

        def store(h, lanes, value):
            sum_s[b, h * width : (h + 1) * width, lanes] = value[:width]
            den_s[b, h : h + 1, lanes] = value[width : width + 1]

        add_pairs(visit, store)

        @pl.when(b > 0)
        def _():
            for save in saves(b - 1):
                save.start()

    for save in saves(blocks - 1):
        save.start()

    @pl.loop(0, blocks)
    def _(b):
        for save in saves(b):
            save.wait()
        wait_for(functools.partial(passing, b))


def back_kernel(
    nb_ref, cnt_ref, qn_ref, kn_ref, mixed_ref, q_ref, sum_ref, den_ref, k_ref, v_ref, r0, r1, r2, r3,
    w_ref, wt_ref, wo_ref, out_ref,
    q_s, k_s, v_s, o_s, m_s, key_s, value_s, mixed_s, queries_s, sum_s, den_s, got_s, out_s, blank_s,
    load_sem, got_sem, out_sem
):
    blocks, _, ch = mixed_s.shape
    width = ch // HEADS
    count = cnt_ref[0]
    got = (r0, r1, r2, r3)

    def loads(b):
        pairs = ((mixed_ref, mixed_s), (q_ref, queries_s), (sum_ref, sum_s), (den_ref, den_s))
        return [
            pltpu.make_async_copy(there.at[b], here.at[b], load_sem.at[i, b]) for i, (there, here) in enumerate(pairs)
        ]

    def fetch(b, face):
        slot = jnp.maximum(nb_ref[b, face], 0)
        return pltpu.make_async_copy(got[face].at[slot], got_s.at[face, b], got_sem.at[face, b])

    def save(b, source):
        return pltpu.make_async_copy(source, out_ref.at[b], out_sem.at[b])

    @pl.loop(0, count)
    def _(b):
        for face in range(4):

            @pl.when(nb_ref[b, face] >= 0)
            def _(face=face):
                fetch(b, face).start()

        for load in loads(b):
            load.start()

    blank_s[...] = jnp.zeros(blank_s.shape, blank_s.dtype)
    clear_operands(q_s, k_s, v_s)

    @pl.loop(count, blocks)
    def _(b):
        save(b, blank_s).start()

    @pl.loop(0, count)
    def _(b):
        n = jnp.int32(0)
        kn = kn_ref[b]
        for face in (4, 5):
            slot = nb_ref[b, face]
            kn = jnp.where(slot >= 0, jnp.maximum(kn, kn_ref[jnp.maximum(slot, 0)]), kn)
        for face in range(4):
            there = nb_ref[b, face] >= 0

            def put(face=face, n=n, kn=kn):
                fetch(b, face).wait()
                normed = padded(got_s[face, b], 0, LANES)
                keys, turned = products(
                    (normed, padded(w_ref[:, ch : 2 * ch], LANES, LANES), False),
                    (padded(wt_ref[ch:], 0, LANES), normed, True),
                )
                put_key_set(keys[:, :ch].astype(BF16), turned[ch:].astype(BF16), k_s, v_s, n, width)
                return jnp.maximum(kn, largest_norm(turned[:ch], width))

            kn = lax.cond(there, put, lambda kn=kn: kn)
            n = jnp.where(there, n + 1, n)
        for load in loads(b):
            load.wait()
        fast = qn_ref[b] * kn <= LIMIT * LIMIT

        def finish(take):
            parts = []
            for h in range(HEADS):
                total, weight = take(h)
                parts.append(total * (1.0 / weight))
            attended = jnp.concatenate(parts, axis=0).T.astype(BF16)
            moved = product(padded(attended, 0, LANES), padded(wo_ref[...], LANES, LANES))[:, :ch]
            out_s[b] = (mixed_s[b].astype(F32) + moved).astype(BF16)

        def own(h):
            return sum_s[b, h * width : (h + 1) * width], den_s[b, h : h + 1]

        @pl.when(jnp.logical_and(fast, n == 0))
        def _():
            finish(own)

        @pl.when(jnp.logical_and(fast, n > 0))
        def _():
            put_queries(queries_s[b], q_s, width)

            def visit(add):
                @pl.loop(0, n)
                def _(i):
                    add(i, q_s, k_s, v_s)

            def store(h, lanes, value):
                o_s[h, :, lanes] = value

            add_pairs(visit, store)

            def both(h):
                total, weight = own(h)
                return total + o_s[h, :width], weight + o_s[h, width : width + 1]

            finish(both)

        @pl.when(jnp.logical_not(fast))
        def _():
            put_queries(queries_s[b], q_s, width)
            sets = n
            for slot in (b, nb_ref[b, 4], nb_ref[b, 5]):

                @pl.when(slot >= 0)
                def _(slot=slot, sets=sets):
                    pltpu.sync_copy(k_ref.at[slot], key_s)
                    pltpu.sync_copy(v_ref.at[slot], value_s)
                    put_key_set(key_s[...], value_s[...], k_s, v_s, sets, width)

                sets = jnp.where(slot >= 0, sets + 1, sets)
            o_s[...] = jnp.zeros(o_s.shape, F32)
            m_s[...] = jnp.full(m_s.shape, -1e30, F32)

            @pl.loop(0, sets)
            def _(i):
                add_pair_running(i, q_s, k_s, v_s, o_s, m_s)

            finish(lambda h: (o_s[h, :width], o_s[h, width : width + 1]))

        save(b, out_s.at[b]).start()

    @pl.loop(0, count)
    def _(b):
        save(b, out_s.at[b]).wait()

    @pl.loop(count, blocks)
    def _(b):
        save(b, blank_s).wait()


def body(voxels, neighbours, block_count, conv_weight, qkv_weight, out_weight):
    blocks, vox, ch = voxels.shape
    cubes = voxels.reshape(blocks, SIDE, SIDE, SIDE, ch)
    vmem = pl.BlockSpec(memory_space=pltpu.VMEM)
    smem = pl.BlockSpec(memory_space=pltpu.SMEM)
    hbm = pl.BlockSpec(memory_space=pl.ANY)
    like = jax.ShapeDtypeStruct(voxels.shape, BF16)
    turned = jax.ShapeDtypeStruct((blocks, ch, vox), BF16)
    scalars = jax.ShapeDtypeStruct((blocks,), F32)
    n_gx, n_gy = lax.axis_size("gx"), lax.axis_size("gy")

    def operands(slots):
        return [
            pltpu.VMEM((HEADS, 2 * ch, vox), BF16),
            pltpu.VMEM((slots, vox, 2 * ch), BF16),
            pltpu.VMEM((slots, HEADS, VALUE_ROWS, vox), BF16),
        ]

    mixed, q, k, v, total, weight, wt, qn, kn, *got = pl.pallas_call(
        functools.partial(front_kernel, (n_gx, n_gy)),
        out_shape=[
            like, turned, like, turned,
            jax.ShapeDtypeStruct((blocks, ch, vox), F32),
            jax.ShapeDtypeStruct((blocks, HEADS, vox), F32),
            jax.ShapeDtypeStruct((3 * ch, ch), BF16),
            scalars, scalars,
        ] + [like] * 4,
        in_specs=[smem, hbm, hbm, hbm, vmem],
        out_specs=[hbm] * 6 + [vmem] + [smem] * 2 + [hbm] * 4,
        scratch_shapes=[
            pltpu.VMEM((36 * ch, 2 * ch), BF16),
            pltpu.VMEM((blocks, 3, SIDE + 2, SIDE * SIDE + 2 * SIDE, ch), BF16),
            pltpu.VMEM((blocks, 3, SIDE + 2, SIDE * SIDE, ch), BF16),
            pltpu.VMEM(voxels.shape, BF16),
            pltpu.VMEM((4, blocks, SIDE, SIDE, ch), BF16),
            *operands(blocks),
            pltpu.VMEM(voxels.shape, BF16),
            pltpu.VMEM(conv_weight.shape, BF16),
            pltpu.VMEM(voxels.shape, BF16),
            pltpu.VMEM((blocks, ch, vox), BF16),
            pltpu.VMEM(voxels.shape, BF16),
            pltpu.VMEM((blocks, ch, vox), BF16),
            pltpu.VMEM((blocks, ch, vox), F32),
            pltpu.VMEM((blocks, HEADS, vox), F32),
            pltpu.SemaphoreType.DMA((4,)),
            pltpu.SemaphoreType.DMA((4,)),
            pltpu.SemaphoreType.DMA((4, blocks)),
            pltpu.SemaphoreType.DMA((4, blocks)),
            pltpu.SemaphoreType.DMA((2,)),
            pltpu.SemaphoreType.DMA((6, blocks)),
        ],
        compiler_params=pltpu.CompilerParams(collective_id=0, has_side_effects=True),
        name="front",
    )(neighbours, voxels, cubes, conv_weight, qkv_weight)

    return pl.pallas_call(
        back_kernel,
        out_shape=like,
        in_specs=[smem] * 4 + [hbm] * 10 + [vmem] * 3,
        out_specs=hbm,
        scratch_shapes=[
            *operands(7),
            pltpu.VMEM((HEADS, VALUE_ROWS, vox), F32),
            pltpu.VMEM((HEADS, 1, vox), F32),
            pltpu.VMEM((vox, ch), BF16),
            pltpu.VMEM((ch, vox), BF16),
            pltpu.VMEM(voxels.shape, BF16),
            pltpu.VMEM((blocks, ch, vox), BF16),
            pltpu.VMEM((blocks, ch, vox), F32),
            pltpu.VMEM((blocks, HEADS, vox), F32),
            pltpu.VMEM((4,) + voxels.shape, BF16),
            pltpu.VMEM(voxels.shape, BF16),
            pltpu.VMEM((vox, ch), BF16),
            pltpu.SemaphoreType.DMA((4, blocks)),
            pltpu.SemaphoreType.DMA((4, blocks)),
            pltpu.SemaphoreType.DMA((blocks,)),
        ],
        name="back",
    )(neighbours, block_count, qn, kn, mixed, q, total, weight, k, v, *got, qkv_weight, wt, out_weight)


def solution(mesh):
    placed = (P(("gx", "gy"), None, None), P(("gx", "gy"), None), P(("gx", "gy")), P(), P(), P())
    return jax.shard_map(
        body, mesh=mesh, in_specs=placed, out_specs=P(("gx", "gy"), None, None), check_vma=False
    )
```

```python
import functools
import math

import jax
import jax.numpy as jnp
from jax import lax
from jax.experimental import pallas as pl
from jax.experimental.pallas import tpu as pltpu
from jax.sharding import PartitionSpec as P

HEADS = 4
SIDE = 8
LIMIT = 90.0
F32 = jnp.float32
BF16 = jnp.bfloat16
NT = (((1,), (1,)), ((), ()))
ROWS = 128
LANES = 256
VALUE_ROWS = 48
MESH = pl.DeviceIdType.MESH


def shifted_z(x, below, above):
    at = lax.broadcasted_iota(jnp.int32, x.shape, 1)
    down = pltpu.roll(jnp.where(at == SIDE - 1, below, x), 1, 1)
    up = pltpu.roll(jnp.where(at == 0, above, x), SIDE - 1, 1)
    return [down, x, up]


def picked(ref, slot, ch):
    value = ref[jnp.maximum(slot, 0)].astype(F32).reshape(-1, SIDE, ch)
    return jnp.where(slot >= 0, value, 0.0)


def lay_interior(b, nb_ref, vox_s, a_s, b_s):
    rows, ch = SIDE * SIDE, vox_s.shape[-1]
    own = vox_s[b].astype(F32).reshape(rows, SIDE, ch)
    inner = shifted_z(own, picked(vox_s, nb_ref[b, 4], ch), picked(vox_s, nb_ref[b, 5], ch))
    blank = jnp.zeros((SIDE, ch), F32)
    for e in range(3):
        for s in range(1, SIDE + 1):
            mid = inner[e][(s - 1) * SIDE : s * SIDE].reshape(rows, ch)
            a_s[b, e, s] = jnp.concatenate([blank, mid, blank], axis=0).astype(BF16)
            b_s[b, e, s] = mid.astype(BF16)


def lay_faces(b, nb_ref, faces, a_s, b_s):
    rows, ch = SIDE * SIDE, a_s.shape[-1]
    xm, xp, ym, yp = [shifted_z(picked(ref, nb_ref[b, f], ch), 0.0, 0.0) for f, ref in enumerate(faces)]
    blank = jnp.zeros((SIDE, ch), F32)
    end = rows + 2 * SIDE
    for e in range(3):
        for s, face in ((0, xm), (SIDE + 1, xp)):
            mid = face[e].reshape(rows, ch)
            a_s[b, e, s] = jnp.concatenate([blank, mid, blank], axis=0).astype(BF16)
            b_s[b, e, s] = mid.astype(BF16)
        for s in range(1, SIDE + 1):
            first = a_s[b, e, s, : 2 * SIDE].astype(F32)
            last = a_s[b, e, s, end - 2 * SIDE :].astype(F32)
            a_s[b, e, s, : 2 * SIDE] = jnp.concatenate([ym[e][s - 1], first[SIDE:]], axis=0).astype(BF16)
            a_s[b, e, s, end - 2 * SIDE :] = jnp.concatenate([last[:SIDE], yp[e][s - 1]], axis=0).astype(BF16)


def conv_block(b, vox_s, w_s, a_s, b_s, mixed_ref, normed_ref):
    rows, ch = SIDE * SIDE, vox_s.shape[-1]
    own = vox_s[b].astype(F32).reshape(rows, SIDE, ch)

    def tile(c, e, unit):
        def slab(x):
            return b_s[b, e, x] if c == 1 else a_s[b, e, x, c * SIDE : c * SIDE + rows]

        pairs = [2 * k + 2 * unit for k in range(4)]
        return jnp.concatenate([jnp.concatenate([slab(x), slab(x + 1)], axis=1) for x in pairs], axis=0)

    def inner(*accs):
        for c in range(3):
            for e in range(3):
                for unit in range(2):
                    reg = (c * 3 + e) % 2
                    at = ((c * 3 + e) * 2 + unit) * LANES
                    pltpu.matmul_push_rhs(w_s[at : at + LANES], reg, unit)
                    pltpu.matmul_acc_lhs(accs[unit], tile(c, e, unit), load_staged_rhs=reg)
        return pltpu.matmul_pop(accs[0]) + pltpu.matmul_pop(accs[1])

    acc = pl.run_scoped(inner, *[pltpu.ACC(u)((4 * rows, LANES), F32) for u in range(2)])
    for k in range(4):
        for o in range(2):
            x = 2 * k + o
            here = own[x * SIDE : (x + 1) * SIDE].reshape(rows, ch)
            mixed = (here + acc[k * rows : (k + 1) * rows, o * ch : (o + 1) * ch]).astype(BF16)
            mixed_ref[b, x * rows : (x + 1) * rows] = mixed
            wide = mixed.astype(F32)
            square = jnp.mean(wide * wide, axis=-1, keepdims=True)
            normed_ref[b, x * rows : (x + 1) * rows] = (wide * lax.rsqrt(square + 1e-06)).astype(BF16)


def pair_weights(cw_ref, w_s):
    ch = cw_ref.shape[-1]
    for ce in range(9):
        for r in range(4):
            for o in range(2):
                row = (ce * 4 + r) * ch
                tap = r - o
                value = cw_ref[tap * 9 + ce] if 0 <= tap <= 2 else jnp.zeros((ch, ch), BF16)
                w_s[row : row + ch, o * ch : (o + 1) * ch] = value


def clear_operands(q_s, k_s, v_s):
    q_s[...] = jnp.zeros(q_s.shape, q_s.dtype)
    k_s[...] = jnp.zeros(k_s.shape, k_s.dtype)
    v_s[...] = jnp.ones(v_s.shape, v_s.dtype)


def put_queries(queries, q_s, width):
    for h in range(HEADS):
        q_s[h, h * width : (h + 1) * width] = queries[h * width : (h + 1) * width]


def put_key_set(keys, values, k_s, v_s, slot, width):
    k_s[slot, :, : HEADS * width] = keys
    for h in range(HEADS):
        v_s[slot, h, :width] = values[h * width : (h + 1) * width]


def largest_norm(x, width):
    wide = x.astype(F32)
    return jnp.max(jnp.sum((wide * wide).reshape(HEADS, width, -1), axis=1), axis=0, keepdims=True) * 1.02


def products(*terms):
    plans = []
    for lhs, rhs, transpose in terms:
        halves = rhs.shape[0 if transpose else 1] == LANES
        plans.append((lhs, rhs, transpose, halves, lhs.shape[0] // 2 if halves else lhs.shape[0]))

    def inner(*accs):
        reg = 0
        for p, (lhs, rhs, transpose, halves, rows) in enumerate(plans):
            for t in range(lhs.shape[1] // LANES):
                deep = slice(t * LANES, (t + 1) * LANES)
                for u in range(2):
                    part = lhs[u * rows : (u + 1) * rows] if halves else lhs
                    wide = slice(0, LANES) if halves else slice(u * LANES, (u + 1) * LANES)
                    tile = rhs[wide, deep] if transpose else rhs[deep, wide]
                    pltpu.matmul_push_rhs(tile, reg, u, transpose=transpose)
                    pltpu.matmul_acc_lhs(accs[2 * p + u], part[:, deep], load_staged_rhs=reg)
                reg = 1 - reg
        return [
            jnp.concatenate([pltpu.matmul_pop(acc) for acc in accs[2 * p : 2 * p + 2]], axis=0 if plan[3] else 1)
            for p, plan in enumerate(plans)
        ]

    return pl.run_scoped(inner, *[pltpu.ACC(u)((plan[4], LANES), F32) for plan in plans for u in range(2)])


def product(lhs, rhs, transpose=False):
    return products((lhs, rhs, transpose))[0]


def padded(x, rows, cols):
    if x.shape[1] < cols:
        x = jnp.concatenate([x, jnp.zeros((x.shape[0], cols - x.shape[1]), x.dtype)], axis=1)
    if x.shape[0] < rows:
        x = jnp.concatenate([x, jnp.zeros((rows - x.shape[0], x.shape[1]), x.dtype)], axis=0)
    return x


def add_pair(slot, q_s, k_s, v_s, score_acc, value_acc, there=None):
    per_tile, per_head = LANES // ROWS, k_s.shape[1] // ROWS
    ring = len(score_acc[0])
    units = range(2)

    def chunk(unit, h, c):
        return score_acc[unit][(per_head * h + c) % ring]

    def stage_queries(h, unit, reg):
        pltpu.matmul_push_rhs(q_s[h, :, unit * LANES : (unit + 1) * LANES], reg, unit)

    def score(h, unit, chunks, reg):
        for c in chunks:
            rows = k_s[slot, c * ROWS : (c + 1) * ROWS]
            pltpu.matmul_acc_lhs(chunk(unit, h, c), rows, load_staged_rhs=reg if c == 0 else None)

    def stage_weights(h, unit, tile, reg):
        parts = [
            jnp.exp2(pltpu.matmul_pop(chunk(unit, h, c))).astype(BF16)
            for c in range(tile * per_tile, (tile + 1) * per_tile)
        ]
        pltpu.matmul_push_rhs(jnp.concatenate(parts, axis=0), reg, unit)

    def mix(h, unit, tile, reg):
        rows = v_s[slot, h, :, tile * LANES : (tile + 1) * LANES]
        if there is not None:
            rows = jnp.where(there, rows, jnp.zeros_like(rows))
        pltpu.matmul_acc_lhs(value_acc[unit][h], rows, load_staged_rhs=reg)

    for u in units:
        stage_queries(0, u, 0)
    for u in units:
        score(0, u, range(per_head), 0)
    for u in units:
        stage_queries(1, u, 1)
    reg = 1
    for h in range(HEADS):
        if h + 1 < HEADS:
            for u in units:
                score(h + 1, u, range(per_tile), reg)
        for u in units:
            stage_weights(h, u, 0, 1 - reg)
        if h + 1 < HEADS:
            for u in units:
                score(h + 1, u, range(per_tile, per_head), None)
        for u in units:
            stage_weights(h, u, 1, reg)
        for u in units:
            mix(h, u, 0, 1 - reg)
        if h + 2 < HEADS:
            for u in units:
                stage_queries(h + 2, u, 1 - reg)
        for u in units:
            mix(h, u, 1, reg)
        reg = 1 - reg


def add_pairs(visit, store):
    ring = 6

    def inner(*accs):
        score_acc = [accs[:ring], accs[ring : 2 * ring]]
        value_acc = [accs[2 * ring : 2 * ring + HEADS], accs[2 * ring + HEADS :]]
        visit(lambda slot, q_s, k_s, v_s, there=None: add_pair(slot, q_s, k_s, v_s, score_acc, value_acc, there))
        for h in range(HEADS):
            for u in range(2):
                store(h, slice(u * LANES, (u + 1) * LANES), pltpu.matmul_pop(value_acc[u][h]))

    scores = [pltpu.ACC(u)((ROWS, LANES), F32) for u in range(2) for _ in range(ring)]
    values = [pltpu.ACC(u)((VALUE_ROWS, LANES), F32) for u in range(2) for _ in range(HEADS)]
    pl.run_scoped(inner, *scores, *values)


def add_pair_running(slot, q_s, k_s, v_s, o_s, m_s):
    for h in range(HEADS):
        scores = product(k_s[slot], q_s[h])
        old = m_s[h]
        new = jnp.maximum(old, jnp.max(scores, axis=0, keepdims=True))
        weights = jnp.exp2(scores - new).astype(BF16)
        o_s[h] = o_s[h] * jnp.exp2(old - new) + product(v_s[slot, h], weights)
        m_s[h] = new


def front_kernel(
    sizes, nb_ref, vox_ref, cube_ref, cw_ref, w_ref,
    mixed_ref, q_ref, k_ref, v_ref, sum_ref, den_ref, wt_ref, qn_ref, kn_ref, got0, got1, got2, got3,
    w_s, a_s, b_s, normed_s, face_s, q_s, k_s, v_s, vox_s, cw_s, mixed_s, queries_s, keys_s, values_s, sum_s, den_s, norm_s,
    face_out, face_in, send_sem, recv_sem, load_sem, save_sem
):
    gx, gy = lax.axis_index("gx"), lax.axis_index("gy")
    n_gx, n_gy = sizes
    blocks, _, ch = vox_s.shape
    width = ch // HEADS
    got = (got0, got1, got2, got3)
    up_x, down_x = lax.rem(gx + 1, n_gx), lax.rem(gx + n_gx - 1, n_gx)
    up_y, down_y = lax.rem(gy + 1, n_gy), lax.rem(gy + n_gy - 1, n_gy)
    peers = [(up_x, gy), (down_x, gy), (gx, up_y), (gx, down_y)]
    to = [gx < n_gx - 1, gx > 0, gy < n_gy - 1, gy > 0]
    since = [to[1], to[0], to[3], to[2]]
    order = (2, 3, 0, 1)
    layers = [cube_ref.at[:, SIDE - 1], cube_ref.at[:, 0], cube_ref.at[:, :, SIDE - 1], cube_ref.at[:, :, 0]]

    loads = [
        pltpu.make_async_copy(vox_ref, vox_s, load_sem.at[0]),
        pltpu.make_async_copy(cw_ref, cw_s, load_sem.at[1]),
    ]
    for load in loads:
        load.start()

    barrier = pltpu.get_barrier_semaphore()
    for side in order:

        @pl.when(to[side])
        def _(side=side):
            pl.semaphore_signal(barrier, inc=1, device_id=peers[side], device_id_type=MESH)

    pl.semaphore_wait(barrier, sum(there.astype(jnp.int32) for there in to))

    def face_copy(f):
        return pltpu.make_async_remote_copy(
            src_ref=layers[f], dst_ref=face_s.at[f], send_sem=face_out.at[f], recv_sem=face_in.at[f],
            device_id=peers[f], device_id_type=MESH,
        )

    def passing(b, side):
        return pltpu.make_async_remote_copy(
            src_ref=normed_s.at[b], dst_ref=got[side].at[b],
            send_sem=send_sem.at[side, b], recv_sem=recv_sem.at[side, b],
            device_id=peers[side], device_id_type=MESH,
        )

    def saves(b):
        pairs = (
            (mixed_s, mixed_ref), (queries_s, q_ref), (keys_s, k_ref), (values_s, v_ref), (sum_s, sum_ref), (den_s, den_ref)
        )
        return [
            pltpu.make_async_copy(here.at[b], there.at[b], save_sem.at[i, b]) for i, (here, there) in enumerate(pairs)
        ]

    def start_where(conditions, copy):
        for side in order:

            @pl.when(conditions[side])
            def _(side=side):
                copy(side).start()

    def wait_for(copy):
        for side in order:

            @pl.when(to[side])
            def _(side=side):
                copy(side).wait_send()

            @pl.when(since[side])
            def _(side=side):
                copy(side).wait_recv()

    start_where(to, face_copy)
    clear_operands(q_s, k_s, v_s)
    wt_ref[...] = w_ref[...].astype(F32).T.astype(BF16)
    loads[0].wait()

    @pl.loop(0, blocks)
    def _(b):
        lay_interior(b, nb_ref, vox_s, a_s, b_s)

    loads[1].wait()
    pair_weights(cw_s, w_s)
    wait_for(face_copy)
    faces = [face_s.at[f] for f in range(4)]

    @pl.loop(0, blocks)
    def _(b):
        lay_faces(b, nb_ref, faces, a_s, b_s)

        @pl.when(b > 0)
        def _():
            start_where(to, functools.partial(passing, b - 1))

        conv_block(b, vox_s, w_s, a_s, b_s, mixed_s, normed_s)

    start_where(to, functools.partial(passing, blocks - 1))

    @pl.loop(0, blocks)
    def _(b):
        factor = math.log2(math.e) / math.sqrt(width)
        normed = padded(normed_s[b], 0, LANES)
        keys, turned = products(
            (normed, padded(w_ref[:, ch : 2 * ch], LANES, LANES), False), (padded(wt_ref[...], 0, LANES), normed, True)
        )
        keys = keys[:, :ch].astype(BF16)
        queries = (turned[:ch] * factor).astype(BF16)
        values = turned[2 * ch :].astype(BF16)
        queries_s[b], keys_s[b], values_s[b] = queries, keys, values
        norm_s[0, b] = largest_norm(queries, width)
        norm_s[1, b] = largest_norm(turned[ch : 2 * ch], width)
        put_key_set(keys, values, k_s, v_s, b, width)

    @pl.loop(0, blocks)
    def _(b):
        put_queries(queries_s[b], q_s, width)

        def visit(add):
            @pl.loop(0, 3)
            def _(i):
                near = nb_ref[b, i + 3]
                there = jnp.logical_or(i == 0, near >= 0)
                slot = jnp.where(jnp.logical_and(i > 0, near >= 0), near, b)

                @pl.when(jnp.logical_and(jnp.logical_or(i != 1, b > 0), jnp.logical_or(i != 2, b < blocks - 1)))
                def _():
                    add(slot, q_s, k_s, v_s, there)

        def store(h, lanes, value):
            sum_s[b, h * width : (h + 1) * width, lanes] = value[:width]
            den_s[b, h : h + 1, lanes] = value[width : width + 1]

        add_pairs(visit, store)

        @pl.when(b > 0)
        def _():
            for save in saves(b - 1):
                save.start()

    for save in saves(blocks - 1):
        save.start()
    for b in range(blocks):
        qn_ref[b] = jnp.max(norm_s[0, b])
        kn_ref[b] = jnp.max(norm_s[1, b])

    @pl.loop(0, blocks)
    def _(b):
        for save in saves(b):
            save.wait()
        wait_for(functools.partial(passing, b))


def back_kernel(
    nb_ref, cnt_ref, qn_ref, kn_ref, mixed_ref, q_ref, sum_ref, den_ref, k_ref, v_ref, r0, r1, r2, r3,
    w_ref, wt_ref, wo_ref, out_ref,
    q_s, k_s, v_s, o_s, m_s, key_s, value_s, mixed_s, queries_s, sum_s, den_s, got_s, out_s, blank_s, norm_s,
    load_sem, got_sem, out_sem
):
    blocks, _, ch = mixed_s.shape
    width = ch // HEADS
    count = cnt_ref[0]
    got = (r0, r1, r2, r3)

    def loads(b):
        pairs = ((mixed_ref, mixed_s), (q_ref, queries_s), (sum_ref, sum_s), (den_ref, den_s))
        return [
            pltpu.make_async_copy(there.at[b], here.at[b], load_sem.at[i, b]) for i, (there, here) in enumerate(pairs)
        ]

    def fetch(b, face):
        slot = jnp.maximum(nb_ref[b, face], 0)
        return pltpu.make_async_copy(got[face].at[slot], got_s.at[face, b], got_sem.at[face, b])

    def save(b, source):
        return pltpu.make_async_copy(source, out_ref.at[b], out_sem.at[b])

    @pl.loop(0, count)
    def _(b):
        for face in range(4):

            @pl.when(nb_ref[b, face] >= 0)
            def _(face=face):
                fetch(b, face).start()

        for load in loads(b):
            load.start()

    blank_s[...] = jnp.zeros(blank_s.shape, blank_s.dtype)
    clear_operands(q_s, k_s, v_s)

    @pl.loop(count, blocks)
    def _(b):
        save(b, blank_s).start()

    @pl.loop(0, count)
    def _(b):
        n = jnp.int32(0)
        kn = kn_ref[b]
        norm_s[...] = jnp.zeros(norm_s.shape, F32)
        for face in (4, 5):
            slot = nb_ref[b, face]
            kn = jnp.where(slot >= 0, jnp.maximum(kn, kn_ref[jnp.maximum(slot, 0)]), kn)
        for face in range(4):
            there = nb_ref[b, face] >= 0

            @pl.when(there)
            def _(face=face, n=n):
                fetch(b, face).wait()
                normed = padded(got_s[face, b], 0, LANES)
                keys, turned = products(
                    (normed, padded(w_ref[:, ch : 2 * ch], LANES, LANES), False),
                    (padded(wt_ref[ch:], 0, LANES), normed, True),
                )
                put_key_set(keys[:, :ch].astype(BF16), turned[ch:].astype(BF16), k_s, v_s, n, width)
                norm_s[...] = jnp.maximum(norm_s[...], largest_norm(turned[:ch], width))

            n = jnp.where(there, n + 1, n)
        kn = jnp.maximum(kn, jnp.max(norm_s[...]))
        for load in loads(b):
            load.wait()
        fast = qn_ref[b] * kn <= LIMIT * LIMIT

        def finish(take):
            parts = []
            for h in range(HEADS):
                total, weight = take(h)
                parts.append(total * (1.0 / weight))
            attended = jnp.concatenate(parts, axis=0).T.astype(BF16)
            moved = product(padded(attended, 0, LANES), padded(wo_ref[...], LANES, LANES))[:, :ch]
            out_s[b] = (mixed_s[b].astype(F32) + moved).astype(BF16)

        def own(h):
            return sum_s[b, h * width : (h + 1) * width], den_s[b, h : h + 1]

        @pl.when(jnp.logical_and(fast, n == 0))
        def _():
            finish(own)

        @pl.when(jnp.logical_and(fast, n > 0))
        def _():
            put_queries(queries_s[b], q_s, width)

            def visit(add):
                @pl.loop(0, n)
                def _(i):
                    add(i, q_s, k_s, v_s)

            def store(h, lanes, value):
                o_s[h, :, lanes] = value

            add_pairs(visit, store)

            def both(h):
                total, weight = own(h)
                return total + o_s[h, :width], weight + o_s[h, width : width + 1]

            finish(both)

        @pl.when(jnp.logical_not(fast))
        def _():
            put_queries(queries_s[b], q_s, width)
            sets = n
            for slot in (b, nb_ref[b, 4], nb_ref[b, 5]):

                @pl.when(slot >= 0)
                def _(slot=slot, sets=sets):
                    pltpu.sync_copy(k_ref.at[slot], key_s)
                    pltpu.sync_copy(v_ref.at[slot], value_s)
                    put_key_set(key_s[...], value_s[...], k_s, v_s, sets, width)

                sets = jnp.where(slot >= 0, sets + 1, sets)
            o_s[...] = jnp.zeros(o_s.shape, F32)
            m_s[...] = jnp.full(m_s.shape, -1e30, F32)

            @pl.loop(0, sets)
            def _(i):
                add_pair_running(i, q_s, k_s, v_s, o_s, m_s)

            finish(lambda h: (o_s[h, :width], o_s[h, width : width + 1]))

        save(b, out_s.at[b]).start()

    @pl.loop(0, count)
    def _(b):
        save(b, out_s.at[b]).wait()

    @pl.loop(count, blocks)
    def _(b):
        save(b, blank_s).wait()


def body(voxels, neighbours, block_count, conv_weight, qkv_weight, out_weight):
    blocks, vox, ch = voxels.shape
    cubes = voxels.reshape(blocks, SIDE, SIDE, SIDE, ch)
    vmem = pl.BlockSpec(memory_space=pltpu.VMEM)
    smem = pl.BlockSpec(memory_space=pltpu.SMEM)
    hbm = pl.BlockSpec(memory_space=pl.ANY)
    like = jax.ShapeDtypeStruct(voxels.shape, BF16)
    turned = jax.ShapeDtypeStruct((blocks, ch, vox), BF16)
    scalars = jax.ShapeDtypeStruct((blocks,), F32)
    n_gx, n_gy = lax.axis_size("gx"), lax.axis_size("gy")

    def operands(slots):
        return [
            pltpu.VMEM((HEADS, 2 * ch, vox), BF16),
            pltpu.VMEM((slots, vox, 2 * ch), BF16),
            pltpu.VMEM((slots, HEADS, VALUE_ROWS, vox), BF16),
        ]

    mixed, q, k, v, total, weight, wt, qn, kn, *got = pl.pallas_call(
        functools.partial(front_kernel, (n_gx, n_gy)),
        out_shape=[
            like, turned, like, turned,
            jax.ShapeDtypeStruct((blocks, ch, vox), F32),
            jax.ShapeDtypeStruct((blocks, HEADS, vox), F32),
            jax.ShapeDtypeStruct((3 * ch, ch), BF16),
            scalars, scalars,
        ] + [like] * 4,
        in_specs=[smem, hbm, hbm, hbm, vmem],
        out_specs=[hbm] * 6 + [vmem] + [smem] * 2 + [hbm] * 4,
        scratch_shapes=[
            pltpu.VMEM((36 * ch, 2 * ch), BF16),
            pltpu.VMEM((blocks, 3, SIDE + 2, SIDE * SIDE + 2 * SIDE, ch), BF16),
            pltpu.VMEM((blocks, 3, SIDE + 2, SIDE * SIDE, ch), BF16),
            pltpu.VMEM(voxels.shape, BF16),
            pltpu.VMEM((4, blocks, SIDE, SIDE, ch), BF16),
            *operands(blocks),
            pltpu.VMEM(voxels.shape, BF16),
            pltpu.VMEM(conv_weight.shape, BF16),
            pltpu.VMEM(voxels.shape, BF16),
            pltpu.VMEM((blocks, ch, vox), BF16),
            pltpu.VMEM(voxels.shape, BF16),
            pltpu.VMEM((blocks, ch, vox), BF16),
            pltpu.VMEM((blocks, ch, vox), F32),
            pltpu.VMEM((blocks, HEADS, vox), F32),
            pltpu.VMEM((2, blocks, 1, vox), F32),
            pltpu.SemaphoreType.DMA((4,)),
            pltpu.SemaphoreType.DMA((4,)),
            pltpu.SemaphoreType.DMA((4, blocks)),
            pltpu.SemaphoreType.DMA((4, blocks)),
            pltpu.SemaphoreType.DMA((2,)),
            pltpu.SemaphoreType.DMA((6, blocks)),
        ],
        compiler_params=pltpu.CompilerParams(collective_id=0, has_side_effects=True),
        name="front",
    )(neighbours, voxels, cubes, conv_weight, qkv_weight)

    return pl.pallas_call(
        back_kernel,
        out_shape=like,
        in_specs=[smem] * 4 + [hbm] * 10 + [vmem] * 3,
        out_specs=hbm,
        scratch_shapes=[
            *operands(7),
            pltpu.VMEM((HEADS, VALUE_ROWS, vox), F32),
            pltpu.VMEM((HEADS, 1, vox), F32),
            pltpu.VMEM((vox, ch), BF16),
            pltpu.VMEM((ch, vox), BF16),
            pltpu.VMEM(voxels.shape, BF16),
            pltpu.VMEM((blocks, ch, vox), BF16),
            pltpu.VMEM((blocks, ch, vox), F32),
            pltpu.VMEM((blocks, HEADS, vox), F32),
            pltpu.VMEM((4,) + voxels.shape, BF16),
            pltpu.VMEM(voxels.shape, BF16),
            pltpu.VMEM((vox, ch), BF16),
            pltpu.VMEM((1, vox), F32),
            pltpu.SemaphoreType.DMA((4, blocks)),
            pltpu.SemaphoreType.DMA((4, blocks)),
            pltpu.SemaphoreType.DMA((blocks,)),
        ],
        name="back",
    )(neighbours, block_count, qn, kn, mixed, q, total, weight, k, v, *got, qkv_weight, wt, out_weight)


def solution(mesh):
    placed = (P(("gx", "gy"), None, None), P(("gx", "gy"), None), P(("gx", "gy")), P(), P(), P())
    return jax.shard_map(
        body, mesh=mesh, in_specs=placed, out_specs=P(("gx", "gy"), None, None), check_vma=False
    )
```

```python
import functools
import math

import jax
import jax.numpy as jnp
from jax import lax
from jax.experimental import pallas as pl
from jax.experimental.pallas import tpu as pltpu
from jax.sharding import PartitionSpec as P

HEADS = 4
SIDE = 8
LIMIT = 90.0
F32 = jnp.float32
BF16 = jnp.bfloat16
NT = (((1,), (1,)), ((), ()))
ROWS = 128
LANES = 256
VALUE_ROWS = 48
MESH = pl.DeviceIdType.MESH


def shifted_z(x, below, above):
    at = lax.broadcasted_iota(jnp.int32, x.shape, 1)
    down = pltpu.roll(jnp.where(at == SIDE - 1, below, x), 1, 1)
    up = pltpu.roll(jnp.where(at == 0, above, x), SIDE - 1, 1)
    return [down, x, up]


def picked(ref, slot, ch):
    value = ref[jnp.maximum(slot, 0)].astype(F32).reshape(-1, SIDE, ch)
    return jnp.where(slot >= 0, value, 0.0)


def lay_interior(b, nb_ref, vox_s, a_s, b_s):
    rows, ch = SIDE * SIDE, vox_s.shape[-1]
    own = vox_s[b].astype(F32).reshape(rows, SIDE, ch)
    inner = shifted_z(own, picked(vox_s, nb_ref[b, 4], ch), picked(vox_s, nb_ref[b, 5], ch))
    blank = jnp.zeros((SIDE, ch), F32)
    for e in range(3):
        for s in range(1, SIDE + 1):
            mid = inner[e][(s - 1) * SIDE : s * SIDE].reshape(rows, ch)
            a_s[b, e, s] = jnp.concatenate([blank, mid, blank], axis=0).astype(BF16)
            b_s[b, e, s] = mid.astype(BF16)


def lay_faces(b, nb_ref, faces, a_s, b_s):
    rows, ch = SIDE * SIDE, a_s.shape[-1]
    xm, xp, ym, yp = [shifted_z(picked(ref, nb_ref[b, f], ch), 0.0, 0.0) for f, ref in enumerate(faces)]
    blank = jnp.zeros((SIDE, ch), F32)
    end = rows + 2 * SIDE
    for e in range(3):
        for s, face in ((0, xm), (SIDE + 1, xp)):
            mid = face[e].reshape(rows, ch)
            a_s[b, e, s] = jnp.concatenate([blank, mid, blank], axis=0).astype(BF16)
            b_s[b, e, s] = mid.astype(BF16)
        for s in range(1, SIDE + 1):
            first = a_s[b, e, s, : 2 * SIDE].astype(F32)
            last = a_s[b, e, s, end - 2 * SIDE :].astype(F32)
            a_s[b, e, s, : 2 * SIDE] = jnp.concatenate([ym[e][s - 1], first[SIDE:]], axis=0).astype(BF16)
            a_s[b, e, s, end - 2 * SIDE :] = jnp.concatenate([last[:SIDE], yp[e][s - 1]], axis=0).astype(BF16)


def conv_block(b, vox_s, w_s, a_s, b_s, mixed_ref, normed_ref):
    rows, ch = SIDE * SIDE, vox_s.shape[-1]
    own = vox_s[b].astype(F32).reshape(rows, SIDE, ch)

    def tile(c, e, unit):
        def slab(x):
            return b_s[b, e, x] if c == 1 else a_s[b, e, x, c * SIDE : c * SIDE + rows]

        pairs = [2 * k + 2 * unit for k in range(4)]
        return jnp.concatenate([jnp.concatenate([slab(x), slab(x + 1)], axis=1) for x in pairs], axis=0)

    def inner(*accs):
        for c in range(3):
            for e in range(3):
                for unit in range(2):
                    reg = (c * 3 + e) % 2
                    at = ((c * 3 + e) * 2 + unit) * LANES
                    pltpu.matmul_push_rhs(w_s[at : at + LANES], reg, unit)
                    pltpu.matmul_acc_lhs(accs[unit], tile(c, e, unit), load_staged_rhs=reg)
        return pltpu.matmul_pop(accs[0]) + pltpu.matmul_pop(accs[1])

    acc = pl.run_scoped(inner, *[pltpu.ACC(u)((4 * rows, LANES), F32) for u in range(2)])
    for k in range(4):
        for o in range(2):
            x = 2 * k + o
            here = own[x * SIDE : (x + 1) * SIDE].reshape(rows, ch)
            mixed = (here + acc[k * rows : (k + 1) * rows, o * ch : (o + 1) * ch]).astype(BF16)
            mixed_ref[b, x * rows : (x + 1) * rows] = mixed
            wide = mixed.astype(F32)
            square = jnp.mean(wide * wide, axis=-1, keepdims=True)
            normed_ref[b, x * rows : (x + 1) * rows] = (wide * lax.rsqrt(square + 1e-06)).astype(BF16)


def pair_weights(cw_ref, w_s):
    ch = cw_ref.shape[-1]
    for ce in range(9):
        for r in range(4):
            for o in range(2):
                row = (ce * 4 + r) * ch
                tap = r - o
                value = cw_ref[tap * 9 + ce] if 0 <= tap <= 2 else jnp.zeros((ch, ch), BF16)
                w_s[row : row + ch, o * ch : (o + 1) * ch] = value


def clear_operands(q_s, k_s, v_s):
    q_s[...] = jnp.zeros(q_s.shape, q_s.dtype)
    k_s[...] = jnp.zeros(k_s.shape, k_s.dtype)
    v_s[...] = jnp.ones(v_s.shape, v_s.dtype)


def put_queries(queries, q_s, width):
    for h in range(HEADS):
        q_s[h, h * width : (h + 1) * width] = queries[h * width : (h + 1) * width]


def put_key_set(keys, values, k_s, v_s, slot, width):
    k_s[slot, :, : HEADS * width] = keys
    for h in range(HEADS):
        v_s[slot, h, :width] = values[h * width : (h + 1) * width]


def largest_norm(x, width):
    wide = x.astype(F32)
    return jnp.max(jnp.sum((wide * wide).reshape(HEADS, width, -1), axis=1), axis=0, keepdims=True) * 1.02


def products(*terms):
    plans = []
    for lhs, rhs, transpose in terms:
        halves = rhs.shape[0 if transpose else 1] == LANES
        plans.append((lhs, rhs, transpose, halves, lhs.shape[0] // 2 if halves else lhs.shape[0]))

    def inner(*accs):
        reg = 0
        for p, (lhs, rhs, transpose, halves, rows) in enumerate(plans):
            for t in range(lhs.shape[1] // LANES):
                deep = slice(t * LANES, (t + 1) * LANES)
                for u in range(2):
                    part = lhs[u * rows : (u + 1) * rows] if halves else lhs
                    wide = slice(0, LANES) if halves else slice(u * LANES, (u + 1) * LANES)
                    tile = rhs[wide, deep] if transpose else rhs[deep, wide]
                    pltpu.matmul_push_rhs(tile, reg, u, transpose=transpose)
                    pltpu.matmul_acc_lhs(accs[2 * p + u], part[:, deep], load_staged_rhs=reg)
                reg = 1 - reg
        return [
            jnp.concatenate([pltpu.matmul_pop(acc) for acc in accs[2 * p : 2 * p + 2]], axis=0 if plan[3] else 1)
            for p, plan in enumerate(plans)
        ]

    return pl.run_scoped(inner, *[pltpu.ACC(u)((plan[4], LANES), F32) for plan in plans for u in range(2)])


def product(lhs, rhs, transpose=False):
    return products((lhs, rhs, transpose))[0]


def padded(x, rows, cols):
    if x.shape[1] < cols:
        x = jnp.concatenate([x, jnp.zeros((x.shape[0], cols - x.shape[1]), x.dtype)], axis=1)
    if x.shape[0] < rows:
        x = jnp.concatenate([x, jnp.zeros((rows - x.shape[0], x.shape[1]), x.dtype)], axis=0)
    return x


def add_chain(sets, q_s, k_s, v_s, score_acc, value_acc):
    per_tile, per_head = LANES // ROWS, k_s.shape[1] // ROWS
    ring = len(score_acc[0])
    units = range(2)
    steps = HEADS * len(sets)

    def chunk(unit, h, c):
        return score_acc[unit][(per_head * h + c) % ring]

    def stage_queries(h, unit, reg):
        pltpu.matmul_push_rhs(q_s[h % HEADS, :, unit * LANES : (unit + 1) * LANES], reg, unit)

    def score(h, unit, chunks, reg):
        for c in chunks:
            rows = k_s[sets[h // HEADS][0], c * ROWS : (c + 1) * ROWS]
            pltpu.matmul_acc_lhs(chunk(unit, h, c), rows, load_staged_rhs=reg if c == 0 else None)

    def stage_weights(h, unit, tile, reg):
        parts = [
            jnp.exp2(pltpu.matmul_pop(chunk(unit, h, c))).astype(BF16)
            for c in range(tile * per_tile, (tile + 1) * per_tile)
        ]
        pltpu.matmul_push_rhs(jnp.concatenate(parts, axis=0), reg, unit)

    def mix(h, unit, tile, reg):
        slot, there = sets[h // HEADS]
        rows = v_s[slot, h % HEADS, :, tile * LANES : (tile + 1) * LANES]
        if there is not None:
            rows = jnp.where(there, rows, jnp.zeros_like(rows))
        pltpu.matmul_acc_lhs(value_acc[unit][h % HEADS], rows, load_staged_rhs=reg)

    for u in units:
        stage_queries(0, u, 0)
    for u in units:
        score(0, u, range(per_head), 0)
    for u in units:
        stage_queries(1, u, 1)
    reg = 1
    for h in range(steps):
        if h + 1 < steps:
            for u in units:
                score(h + 1, u, range(per_tile), reg)
        for u in units:
            stage_weights(h, u, 0, 1 - reg)
        if h + 1 < steps:
            for u in units:
                score(h + 1, u, range(per_tile, per_head), None)
        for u in units:
            stage_weights(h, u, 1, reg)
        for u in units:
            mix(h, u, 0, 1 - reg)
        if h + 2 < steps:
            for u in units:
                stage_queries(h + 2, u, 1 - reg)
        for u in units:
            mix(h, u, 1, reg)
        reg = 1 - reg


def add_pairs(visit, store):
    ring = 6

    def inner(*accs):
        score_acc = [accs[:ring], accs[ring : 2 * ring]]
        value_acc = [accs[2 * ring : 2 * ring + HEADS], accs[2 * ring + HEADS :]]
        visit(lambda sets, q_s, k_s, v_s: add_chain(sets, q_s, k_s, v_s, score_acc, value_acc))
        for h in range(HEADS):
            for u in range(2):
                store(h, slice(u * LANES, (u + 1) * LANES), pltpu.matmul_pop(value_acc[u][h]))

    scores = [pltpu.ACC(u)((ROWS, LANES), F32) for u in range(2) for _ in range(ring)]
    values = [pltpu.ACC(u)((VALUE_ROWS, LANES), F32) for u in range(2) for _ in range(HEADS)]
    pl.run_scoped(inner, *scores, *values)


def add_pair_running(slot, q_s, k_s, v_s, o_s, m_s):
    for h in range(HEADS):
        scores = product(k_s[slot], q_s[h])
        old = m_s[h]
        new = jnp.maximum(old, jnp.max(scores, axis=0, keepdims=True))
        weights = jnp.exp2(scores - new).astype(BF16)
        o_s[h] = o_s[h] * jnp.exp2(old - new) + product(v_s[slot, h], weights)
        m_s[h] = new


def front_kernel(
    sizes, nb_ref, vox_ref, cube_ref, cw_ref, w_ref,
    mixed_ref, q_ref, k_ref, v_ref, sum_ref, den_ref, wt_ref, qn_ref, kn_ref, got0, got1, got2, got3,
    w_s, a_s, b_s, normed_s, face_s, q_s, k_s, v_s, vox_s, cw_s, mixed_s, queries_s, keys_s, values_s, sum_s, den_s, norm_s,
    face_out, face_in, send_sem, recv_sem, load_sem, save_sem
):
    gx, gy = lax.axis_index("gx"), lax.axis_index("gy")
    n_gx, n_gy = sizes
    blocks, _, ch = vox_s.shape
    width = ch // HEADS
    got = (got0, got1, got2, got3)
    up_x, down_x = lax.rem(gx + 1, n_gx), lax.rem(gx + n_gx - 1, n_gx)
    up_y, down_y = lax.rem(gy + 1, n_gy), lax.rem(gy + n_gy - 1, n_gy)
    peers = [(up_x, gy), (down_x, gy), (gx, up_y), (gx, down_y)]
    to = [gx < n_gx - 1, gx > 0, gy < n_gy - 1, gy > 0]
    since = [to[1], to[0], to[3], to[2]]
    order = (2, 3, 0, 1)
    layers = [cube_ref.at[:, SIDE - 1], cube_ref.at[:, 0], cube_ref.at[:, :, SIDE - 1], cube_ref.at[:, :, 0]]

    loads = [
        pltpu.make_async_copy(vox_ref, vox_s, load_sem.at[0]),
        pltpu.make_async_copy(cw_ref, cw_s, load_sem.at[1]),
    ]
    for load in loads:
        load.start()

    barrier = pltpu.get_barrier_semaphore()
    for side in order:

        @pl.when(to[side])
        def _(side=side):
            pl.semaphore_signal(barrier, inc=1, device_id=peers[side], device_id_type=MESH)

    pl.semaphore_wait(barrier, sum(there.astype(jnp.int32) for there in to))

    def face_copy(f):
        return pltpu.make_async_remote_copy(
            src_ref=layers[f], dst_ref=face_s.at[f], send_sem=face_out.at[f], recv_sem=face_in.at[f],
            device_id=peers[f], device_id_type=MESH,
        )

    def passing(b, side):
        return pltpu.make_async_remote_copy(
            src_ref=normed_s.at[b], dst_ref=got[side].at[b],
            send_sem=send_sem.at[side, b], recv_sem=recv_sem.at[side, b],
            device_id=peers[side], device_id_type=MESH,
        )

    def saves(b):
        pairs = (
            (mixed_s, mixed_ref), (queries_s, q_ref), (keys_s, k_ref), (values_s, v_ref), (sum_s, sum_ref), (den_s, den_ref)
        )
        return [
            pltpu.make_async_copy(here.at[b], there.at[b], save_sem.at[i, b]) for i, (here, there) in enumerate(pairs)
        ]

    def start_where(conditions, copy):
        for side in order:

            @pl.when(conditions[side])
            def _(side=side):
                copy(side).start()

    def wait_for(copy):
        for side in order:

            @pl.when(to[side])
            def _(side=side):
                copy(side).wait_send()

            @pl.when(since[side])
            def _(side=side):
                copy(side).wait_recv()

    start_where(to, face_copy)
    clear_operands(q_s, k_s, v_s)
    wt_ref[...] = w_ref[...].astype(F32).T.astype(BF16)
    loads[0].wait()

    @pl.loop(0, blocks)
    def _(b):
        lay_interior(b, nb_ref, vox_s, a_s, b_s)

    loads[1].wait()
    pair_weights(cw_s, w_s)
    wait_for(face_copy)
    faces = [face_s.at[f] for f in range(4)]

    @pl.loop(0, blocks)
    def _(b):
        lay_faces(b, nb_ref, faces, a_s, b_s)

        @pl.when(b > 0)
        def _():
            start_where(to, functools.partial(passing, b - 1))

        conv_block(b, vox_s, w_s, a_s, b_s, mixed_s, normed_s)

    start_where(to, functools.partial(passing, blocks - 1))

    @pl.loop(0, blocks)
    def _(b):
        factor = math.log2(math.e) / math.sqrt(width)
        normed = padded(normed_s[b], 0, LANES)
        keys, turned = products(
            (normed, padded(w_ref[:, ch : 2 * ch], LANES, LANES), False), (padded(wt_ref[...], 0, LANES), normed, True)
        )
        keys = keys[:, :ch].astype(BF16)
        queries = (turned[:ch] * factor).astype(BF16)
        values = turned[2 * ch :].astype(BF16)
        queries_s[b], keys_s[b], values_s[b] = queries, keys, values
        norm_s[0, b] = largest_norm(queries, width)
        norm_s[1, b] = largest_norm(turned[ch : 2 * ch], width)
        put_key_set(keys, values, k_s, v_s, b, width)

    @pl.loop(0, blocks)
    def _(b):
        put_queries(queries_s[b], q_s, width)

        def visit(add):
            below, above = nb_ref[b, 4], nb_ref[b, 5]
            own = (b, None)
            low = (jnp.where(below >= 0, below, b), below >= 0)
            high = (jnp.where(above >= 0, above, b), above >= 0)

            @pl.when(b == 0)
            def _():
                add([own, high], q_s, k_s, v_s)

            @pl.when(jnp.logical_and(b > 0, b < blocks - 1))
            def _():
                add([own, low, high], q_s, k_s, v_s)

            @pl.when(b == blocks - 1)
            def _():
                add([own, low], q_s, k_s, v_s)

        def store(h, lanes, value):
            sum_s[b, h * width : (h + 1) * width, lanes] = value[:width]
            den_s[b, h : h + 1, lanes] = value[width : width + 1]

        add_pairs(visit, store)

        @pl.when(b > 0)
        def _():
            for save in saves(b - 1):
                save.start()

    for save in saves(blocks - 1):
        save.start()
    for b in range(blocks):
        qn_ref[b] = jnp.max(norm_s[0, b])
        kn_ref[b] = jnp.max(norm_s[1, b])

    @pl.loop(0, blocks)
    def _(b):
        for save in saves(b):
            save.wait()
        wait_for(functools.partial(passing, b))


def back_kernel(
    nb_ref, cnt_ref, qn_ref, kn_ref, mixed_ref, q_ref, sum_ref, den_ref, k_ref, v_ref, r0, r1, r2, r3,
    w_ref, wt_ref, wo_ref, out_ref,
    q_s, k_s, v_s, o_s, m_s, key_s, value_s, mixed_s, queries_s, sum_s, den_s, got_s, out_s, blank_s,
    load_sem, got_sem, out_sem
):
    blocks, _, ch = mixed_s.shape
    width = ch // HEADS
    count = cnt_ref[0]
    got = (r0, r1, r2, r3)

    def loads(b):
        pairs = ((mixed_ref, mixed_s), (q_ref, queries_s), (sum_ref, sum_s), (den_ref, den_s))
        return [
            pltpu.make_async_copy(there.at[b], here.at[b], load_sem.at[i, b]) for i, (there, here) in enumerate(pairs)
        ]

    def fetch(b, face):
        slot = jnp.maximum(nb_ref[b, face], 0)
        return pltpu.make_async_copy(got[face].at[slot], got_s.at[face, b], got_sem.at[face, b])

    def save(b, source):
        return pltpu.make_async_copy(source, out_ref.at[b], out_sem.at[b])

    @pl.loop(0, count)
    def _(b):
        for face in range(4):

            @pl.when(nb_ref[b, face] >= 0)
            def _(face=face):
                fetch(b, face).start()

        for load in loads(b):
            load.start()

    blank_s[...] = jnp.zeros(blank_s.shape, blank_s.dtype)
    clear_operands(q_s, k_s, v_s)

    @pl.loop(count, blocks)
    def _(b):
        save(b, blank_s).start()

    @pl.loop(0, count)
    def _(b):
        n = jnp.int32(0)
        kn = kn_ref[b]
        for face in (4, 5):
            slot = nb_ref[b, face]
            kn = jnp.where(slot >= 0, jnp.maximum(kn, kn_ref[jnp.maximum(slot, 0)]), kn)
        for face in range(4):
            there = nb_ref[b, face] >= 0

            def put(face=face, n=n, kn=kn):
                fetch(b, face).wait()
                normed = padded(got_s[face, b], 0, LANES)
                keys, turned = products(
                    (normed, padded(w_ref[:, ch : 2 * ch], LANES, LANES), False),
                    (padded(wt_ref[ch:], 0, LANES), normed, True),
                )
                put_key_set(keys[:, :ch].astype(BF16), turned[ch:].astype(BF16), k_s, v_s, n, width)
                return jnp.maximum(kn, jnp.max(largest_norm(turned[:ch], width)))

            kn = lax.cond(there, put, lambda kn=kn: kn)
            n = jnp.where(there, n + 1, n)
        for load in loads(b):
            load.wait()
        fast = qn_ref[b] * kn <= LIMIT * LIMIT

        def finish(take):
            parts = []
            for h in range(HEADS):
                total, weight = take(h)
                parts.append(total * (1.0 / weight))
            attended = jnp.concatenate(parts, axis=0).T.astype(BF16)
            moved = product(padded(attended, 0, LANES), padded(wo_ref[...], LANES, LANES))[:, :ch]
            out_s[b] = (mixed_s[b].astype(F32) + moved).astype(BF16)

        def own(h):
            return sum_s[b, h * width : (h + 1) * width], den_s[b, h : h + 1]

        @pl.when(jnp.logical_and(fast, n == 0))
        def _():
            finish(own)

        @pl.when(jnp.logical_and(fast, n > 0))
        def _():
            put_queries(queries_s[b], q_s, width)

            def visit(add):
                @pl.loop(0, n)
                def _(i):
                    add([(i, None)], q_s, k_s, v_s)

            def store(h, lanes, value):
                o_s[h, :, lanes] = value

            add_pairs(visit, store)

            def both(h):
                total, weight = own(h)
                return total + o_s[h, :width], weight + o_s[h, width : width + 1]

            finish(both)

        @pl.when(jnp.logical_not(fast))
        def _():
            put_queries(queries_s[b], q_s, width)
            sets = n
            for slot in (b, nb_ref[b, 4], nb_ref[b, 5]):

                @pl.when(slot >= 0)
                def _(slot=slot, sets=sets):
                    pltpu.sync_copy(k_ref.at[slot], key_s)
                    pltpu.sync_copy(v_ref.at[slot], value_s)
                    put_key_set(key_s[...], value_s[...], k_s, v_s, sets, width)

                sets = jnp.where(slot >= 0, sets + 1, sets)
            o_s[...] = jnp.zeros(o_s.shape, F32)
            m_s[...] = jnp.full(m_s.shape, -1e30, F32)

            @pl.loop(0, sets)
            def _(i):
                add_pair_running(i, q_s, k_s, v_s, o_s, m_s)

            finish(lambda h: (o_s[h, :width], o_s[h, width : width + 1]))

        save(b, out_s.at[b]).start()

    @pl.loop(0, count)
    def _(b):
        save(b, out_s.at[b]).wait()

    @pl.loop(count, blocks)
    def _(b):
        save(b, blank_s).wait()


def body(voxels, neighbours, block_count, conv_weight, qkv_weight, out_weight):
    blocks, vox, ch = voxels.shape
    cubes = voxels.reshape(blocks, SIDE, SIDE, SIDE, ch)
    vmem = pl.BlockSpec(memory_space=pltpu.VMEM)
    smem = pl.BlockSpec(memory_space=pltpu.SMEM)
    hbm = pl.BlockSpec(memory_space=pl.ANY)
    like = jax.ShapeDtypeStruct(voxels.shape, BF16)
    turned = jax.ShapeDtypeStruct((blocks, ch, vox), BF16)
    scalars = jax.ShapeDtypeStruct((blocks,), F32)
    n_gx, n_gy = lax.axis_size("gx"), lax.axis_size("gy")

    def operands(slots):
        return [
            pltpu.VMEM((HEADS, 2 * ch, vox), BF16),
            pltpu.VMEM((slots, vox, 2 * ch), BF16),
            pltpu.VMEM((slots, HEADS, VALUE_ROWS, vox), BF16),
        ]

    mixed, q, k, v, total, weight, wt, qn, kn, *got = pl.pallas_call(
        functools.partial(front_kernel, (n_gx, n_gy)),
        out_shape=[
            like, turned, like, turned,
            jax.ShapeDtypeStruct((blocks, ch, vox), F32),
            jax.ShapeDtypeStruct((blocks, HEADS, vox), F32),
            jax.ShapeDtypeStruct((3 * ch, ch), BF16),
            scalars, scalars,
        ] + [like] * 4,
        in_specs=[smem, hbm, hbm, hbm, vmem],
        out_specs=[hbm] * 6 + [vmem] + [smem] * 2 + [hbm] * 4,
        scratch_shapes=[
            pltpu.VMEM((36 * ch, 2 * ch), BF16),
            pltpu.VMEM((blocks, 3, SIDE + 2, SIDE * SIDE + 2 * SIDE, ch), BF16),
            pltpu.VMEM((blocks, 3, SIDE + 2, SIDE * SIDE, ch), BF16),
            pltpu.VMEM(voxels.shape, BF16),
            pltpu.VMEM((4, blocks, SIDE, SIDE, ch), BF16),
            *operands(blocks),
            pltpu.VMEM(voxels.shape, BF16),
            pltpu.VMEM(conv_weight.shape, BF16),
            pltpu.VMEM(voxels.shape, BF16),
            pltpu.VMEM((blocks, ch, vox), BF16),
            pltpu.VMEM(voxels.shape, BF16),
            pltpu.VMEM((blocks, ch, vox), BF16),
            pltpu.VMEM((blocks, ch, vox), F32),
            pltpu.VMEM((blocks, HEADS, vox), F32),
            pltpu.VMEM((2, blocks, 1, vox), F32),
            pltpu.SemaphoreType.DMA((4,)),
            pltpu.SemaphoreType.DMA((4,)),
            pltpu.SemaphoreType.DMA((4, blocks)),
            pltpu.SemaphoreType.DMA((4, blocks)),
            pltpu.SemaphoreType.DMA((2,)),
            pltpu.SemaphoreType.DMA((6, blocks)),
        ],
        compiler_params=pltpu.CompilerParams(collective_id=0, has_side_effects=True),
        name="front",
    )(neighbours, voxels, cubes, conv_weight, qkv_weight)

    return pl.pallas_call(
        back_kernel,
        out_shape=like,
        in_specs=[smem] * 4 + [hbm] * 10 + [vmem] * 3,
        out_specs=hbm,
        scratch_shapes=[
            *operands(7),
            pltpu.VMEM((HEADS, VALUE_ROWS, vox), F32),
            pltpu.VMEM((HEADS, 1, vox), F32),
            pltpu.VMEM((vox, ch), BF16),
            pltpu.VMEM((ch, vox), BF16),
            pltpu.VMEM(voxels.shape, BF16),
            pltpu.VMEM((blocks, ch, vox), BF16),
            pltpu.VMEM((blocks, ch, vox), F32),
            pltpu.VMEM((blocks, HEADS, vox), F32),
            pltpu.VMEM((4,) + voxels.shape, BF16),
            pltpu.VMEM(voxels.shape, BF16),
            pltpu.VMEM((vox, ch), BF16),
            pltpu.SemaphoreType.DMA((4, blocks)),
            pltpu.SemaphoreType.DMA((4, blocks)),
            pltpu.SemaphoreType.DMA((blocks,)),
        ],
        name="back",
    )(neighbours, block_count, qn, kn, mixed, q, total, weight, k, v, *got, qkv_weight, wt, out_weight)


def solution(mesh):
    placed = (P(("gx", "gy"), None, None), P(("gx", "gy"), None), P(("gx", "gy")), P(), P(), P())
    return jax.shard_map(
        body, mesh=mesh, in_specs=placed, out_specs=P(("gx", "gy"), None, None), check_vma=False
    )
```

```python
import functools
import math

import jax
import jax.numpy as jnp
from jax import lax
from jax.experimental import pallas as pl
from jax.experimental.pallas import tpu as pltpu
from jax.sharding import PartitionSpec as P

HEADS = 4
SIDE = 8
LIMIT = 90.0
F32 = jnp.float32
BF16 = jnp.bfloat16
NT = (((1,), (1,)), ((), ()))
ROWS = 128
LANES = 256
VALUE_ROWS = 48
MESH = pl.DeviceIdType.MESH


def shifted_z(x, below, above):
    at = lax.broadcasted_iota(jnp.int32, x.shape, 1)
    down = pltpu.roll(jnp.where(at == SIDE - 1, below, x), 1, 1)
    up = pltpu.roll(jnp.where(at == 0, above, x), SIDE - 1, 1)
    return [down, x, up]


def picked(ref, slot, ch):
    value = ref[jnp.maximum(slot, 0)].astype(F32).reshape(-1, SIDE, ch)
    return jnp.where(slot >= 0, value, 0.0)


def lay_interior(b, nb_ref, vox_s, a_s, b_s):
    rows, ch = SIDE * SIDE, vox_s.shape[-1]
    own = vox_s[b].astype(F32).reshape(rows, SIDE, ch)
    inner = shifted_z(own, picked(vox_s, nb_ref[b, 4], ch), picked(vox_s, nb_ref[b, 5], ch))
    blank = jnp.zeros((SIDE, ch), F32)
    for e in range(3):
        for s in range(1, SIDE + 1):
            mid = inner[e][(s - 1) * SIDE : s * SIDE].reshape(rows, ch)
            a_s[b, e, s] = jnp.concatenate([blank, mid, blank], axis=0).astype(BF16)
            b_s[b, e, s] = mid.astype(BF16)


def lay_faces(b, nb_ref, faces, a_s, b_s):
    rows, ch = SIDE * SIDE, a_s.shape[-1]
    xm, xp, ym, yp = [shifted_z(picked(ref, nb_ref[b, f], ch), 0.0, 0.0) for f, ref in enumerate(faces)]
    blank = jnp.zeros((SIDE, ch), F32)
    end = rows + 2 * SIDE
    for e in range(3):
        for s, face in ((0, xm), (SIDE + 1, xp)):
            mid = face[e].reshape(rows, ch)
            a_s[b, e, s] = jnp.concatenate([blank, mid, blank], axis=0).astype(BF16)
            b_s[b, e, s] = mid.astype(BF16)
        for s in range(1, SIDE + 1):
            first = a_s[b, e, s, : 2 * SIDE].astype(F32)
            last = a_s[b, e, s, end - 2 * SIDE :].astype(F32)
            a_s[b, e, s, : 2 * SIDE] = jnp.concatenate([ym[e][s - 1], first[SIDE:]], axis=0).astype(BF16)
            a_s[b, e, s, end - 2 * SIDE :] = jnp.concatenate([last[:SIDE], yp[e][s - 1]], axis=0).astype(BF16)


def conv_block(b, vox_s, w_s, a_s, b_s, mixed_ref, normed_ref):
    rows, ch = SIDE * SIDE, vox_s.shape[-1]
    own = vox_s[b].astype(F32).reshape(rows, SIDE, ch)

    def tile(c, e, unit):
        def slab(x):
            return b_s[b, e, x] if c == 1 else a_s[b, e, x, c * SIDE : c * SIDE + rows]

        pairs = [2 * k + 2 * unit for k in range(4)]
        return jnp.concatenate([jnp.concatenate([slab(x), slab(x + 1)], axis=1) for x in pairs], axis=0)

    def inner(*accs):
        for c in range(3):
            for e in range(3):
                for unit in range(2):
                    reg = (c * 3 + e) % 2
                    at = ((c * 3 + e) * 2 + unit) * LANES
                    pltpu.matmul_push_rhs(w_s[at : at + LANES], reg, unit)
                    pltpu.matmul_acc_lhs(accs[unit], tile(c, e, unit), load_staged_rhs=reg)
        return pltpu.matmul_pop(accs[0]) + pltpu.matmul_pop(accs[1])

    acc = pl.run_scoped(inner, *[pltpu.ACC(u)((4 * rows, LANES), F32) for u in range(2)])
    for k in range(4):
        for o in range(2):
            x = 2 * k + o
            here = own[x * SIDE : (x + 1) * SIDE].reshape(rows, ch)
            mixed = (here + acc[k * rows : (k + 1) * rows, o * ch : (o + 1) * ch]).astype(BF16)
            mixed_ref[b, x * rows : (x + 1) * rows] = mixed
            wide = mixed.astype(F32)
            square = jnp.mean(wide * wide, axis=-1, keepdims=True)
            normed_ref[b, x * rows : (x + 1) * rows] = (wide * lax.rsqrt(square + 1e-06)).astype(BF16)


def pair_weights(cw_ref, w_s):
    ch = cw_ref.shape[-1]
    for ce in range(9):
        for r in range(4):
            for o in range(2):
                row = (ce * 4 + r) * ch
                tap = r - o
                value = cw_ref[tap * 9 + ce] if 0 <= tap <= 2 else jnp.zeros((ch, ch), BF16)
                w_s[row : row + ch, o * ch : (o + 1) * ch] = value


def clear_operands(q_s, k_s, v_s):
    q_s[...] = jnp.zeros(q_s.shape, q_s.dtype)
    k_s[...] = jnp.zeros(k_s.shape, k_s.dtype)
    v_s[...] = jnp.ones(v_s.shape, v_s.dtype)


def put_queries(queries, q_s, width):
    for h in range(HEADS):
        q_s[h, h * width : (h + 1) * width] = queries[h * width : (h + 1) * width]


def put_key_set(keys, values, k_s, v_s, slot, width):
    k_s[slot, :, : HEADS * width] = keys
    for h in range(HEADS):
        v_s[slot, h, :width] = values[h * width : (h + 1) * width]


def largest_norm(x, width):
    wide = x.astype(F32)
    return jnp.max(jnp.sum((wide * wide).reshape(HEADS, width, -1), axis=1), axis=0, keepdims=True) * 1.02


def products(*terms):
    plans = []
    for lhs, rhs, transpose in terms:
        halves = rhs.shape[0 if transpose else 1] == LANES
        plans.append((lhs, rhs, transpose, halves, lhs.shape[0] // 2 if halves else lhs.shape[0]))

    def inner(*accs):
        reg = 0
        for p, (lhs, rhs, transpose, halves, rows) in enumerate(plans):
            for t in range(lhs.shape[1] // LANES):
                deep = slice(t * LANES, (t + 1) * LANES)
                for u in range(2):
                    part = lhs[u * rows : (u + 1) * rows] if halves else lhs
                    wide = slice(0, LANES) if halves else slice(u * LANES, (u + 1) * LANES)
                    tile = rhs[wide, deep] if transpose else rhs[deep, wide]
                    pltpu.matmul_push_rhs(tile, reg, u, transpose=transpose)
                    pltpu.matmul_acc_lhs(accs[2 * p + u], part[:, deep], load_staged_rhs=reg)
                reg = 1 - reg
        return [
            jnp.concatenate([pltpu.matmul_pop(acc) for acc in accs[2 * p : 2 * p + 2]], axis=0 if plan[3] else 1)
            for p, plan in enumerate(plans)
        ]

    return pl.run_scoped(inner, *[pltpu.ACC(u)((plan[4], LANES), F32) for plan in plans for u in range(2)])


def product(lhs, rhs, transpose=False):
    return products((lhs, rhs, transpose))[0]


def padded(x, rows, cols):
    if x.shape[1] < cols:
        x = jnp.concatenate([x, jnp.zeros((x.shape[0], cols - x.shape[1]), x.dtype)], axis=1)
    if x.shape[0] < rows:
        x = jnp.concatenate([x, jnp.zeros((rows - x.shape[0], x.shape[1]), x.dtype)], axis=0)
    return x


def add_chain(sets, q_s, k_s, v_s, score_acc, value_acc):
    per_tile, per_head = LANES // ROWS, k_s.shape[1] // ROWS
    ring = len(score_acc[0])
    units = range(2)
    steps = HEADS * len(sets)

    def chunk(unit, h, c):
        return score_acc[unit][(per_head * h + c) % ring]

    def stage_queries(h, unit, reg):
        pltpu.matmul_push_rhs(q_s[h % HEADS, :, unit * LANES : (unit + 1) * LANES], reg, unit)

    def score(h, unit, chunks, reg):
        for c in chunks:
            rows = k_s[sets[h // HEADS][0], c * ROWS : (c + 1) * ROWS]
            pltpu.matmul_acc_lhs(chunk(unit, h, c), rows, load_staged_rhs=reg if c == 0 else None)

    def stage_weights(h, unit, tile, reg):
        parts = [
            jnp.exp2(pltpu.matmul_pop(chunk(unit, h, c))).astype(BF16)
            for c in range(tile * per_tile, (tile + 1) * per_tile)
        ]
        pltpu.matmul_push_rhs(jnp.concatenate(parts, axis=0), reg, unit)

    def mix(h, unit, tile, reg):
        slot, there = sets[h // HEADS]
        rows = v_s[slot, h % HEADS, :, tile * LANES : (tile + 1) * LANES]
        if there is not None:
            rows = jnp.where(there, rows, jnp.zeros_like(rows))
        pltpu.matmul_acc_lhs(value_acc[unit][h % HEADS], rows, load_staged_rhs=reg)

    for u in units:
        stage_queries(0, u, 0)
    for u in units:
        score(0, u, range(per_head), 0)
    for u in units:
        stage_queries(1, u, 1)
    reg = 1
    for h in range(steps):
        if h + 1 < steps:
            for u in units:
                score(h + 1, u, range(per_tile), reg)
        for u in units:
            stage_weights(h, u, 0, 1 - reg)
        if h + 1 < steps:
            for u in units:
                score(h + 1, u, range(per_tile, per_head), None)
        for u in units:
            stage_weights(h, u, 1, reg)
        for u in units:
            mix(h, u, 0, 1 - reg)
        if h + 2 < steps:
            for u in units:
                stage_queries(h + 2, u, 1 - reg)
        for u in units:
            mix(h, u, 1, reg)
        reg = 1 - reg


def add_pairs(visit, store):
    ring = 6

    def inner(*accs):
        score_acc = [accs[:ring], accs[ring : 2 * ring]]
        value_acc = [accs[2 * ring : 2 * ring + HEADS], accs[2 * ring + HEADS :]]
        visit(lambda sets, q_s, k_s, v_s: add_chain(sets, q_s, k_s, v_s, score_acc, value_acc))
        for h in range(HEADS):
            for u in range(2):
                store(h, slice(u * LANES, (u + 1) * LANES), pltpu.matmul_pop(value_acc[u][h]))

    scores = [pltpu.ACC(u)((ROWS, LANES), F32) for u in range(2) for _ in range(ring)]
    values = [pltpu.ACC(u)((VALUE_ROWS, LANES), F32) for u in range(2) for _ in range(HEADS)]
    pl.run_scoped(inner, *scores, *values)


def add_pair_running(slot, q_s, k_s, v_s, o_s, m_s):
    for h in range(HEADS):
        scores = product(k_s[slot], q_s[h])
        old = m_s[h]
        new = jnp.maximum(old, jnp.max(scores, axis=0, keepdims=True))
        weights = jnp.exp2(scores - new).astype(BF16)
        o_s[h] = o_s[h] * jnp.exp2(old - new) + product(v_s[slot, h], weights)
        m_s[h] = new


def front_kernel(
    sizes, nb_ref, vox_ref, cube_ref, cw_ref, w_ref,
    mixed_ref, q_ref, k_ref, v_ref, sum_ref, den_ref, wt_ref, qn_ref, kn_ref, got0, got1, got2, got3,
    w_s, a_s, b_s, normed_s, face_s, q_s, k_s, v_s, vox_s, cw_s, mixed_s, queries_s, keys_s, values_s, sum_s, den_s, norm_s,
    face_out, face_in, send_sem, recv_sem, load_sem, save_sem
):
    gx, gy = lax.axis_index("gx"), lax.axis_index("gy")
    n_gx, n_gy = sizes
    blocks, _, ch = vox_s.shape
    width = ch // HEADS
    got = (got0, got1, got2, got3)
    up_x, down_x = lax.rem(gx + 1, n_gx), lax.rem(gx + n_gx - 1, n_gx)
    up_y, down_y = lax.rem(gy + 1, n_gy), lax.rem(gy + n_gy - 1, n_gy)
    peers = [(up_x, gy), (down_x, gy), (gx, up_y), (gx, down_y)]
    to = [gx < n_gx - 1, gx > 0, gy < n_gy - 1, gy > 0]
    since = [to[1], to[0], to[3], to[2]]
    order = (2, 3, 0, 1)
    layers = [cube_ref.at[:, SIDE - 1], cube_ref.at[:, 0], cube_ref.at[:, :, SIDE - 1], cube_ref.at[:, :, 0]]

    loads = [
        pltpu.make_async_copy(vox_ref, vox_s, load_sem.at[0]),
        pltpu.make_async_copy(cw_ref, cw_s, load_sem.at[1]),
    ]
    for load in loads:
        load.start()

    barrier = pltpu.get_barrier_semaphore()
    for side in order:

        @pl.when(to[side])
        def _(side=side):
            pl.semaphore_signal(barrier, inc=1, device_id=peers[side], device_id_type=MESH)

    pl.semaphore_wait(barrier, sum(there.astype(jnp.int32) for there in to))

    def face_copy(f):
        return pltpu.make_async_remote_copy(
            src_ref=layers[f], dst_ref=face_s.at[f], send_sem=face_out.at[f], recv_sem=face_in.at[f],
            device_id=peers[f], device_id_type=MESH,
        )

    def passing(b, side):
        return pltpu.make_async_remote_copy(
            src_ref=normed_s.at[b], dst_ref=got[side].at[b],
            send_sem=send_sem.at[side, b], recv_sem=recv_sem.at[side, b],
            device_id=peers[side], device_id_type=MESH,
        )

    def saves(b):
        pairs = (
            (mixed_s, mixed_ref), (queries_s, q_ref), (keys_s, k_ref), (values_s, v_ref), (sum_s, sum_ref), (den_s, den_ref)
        )
        return [
            pltpu.make_async_copy(here.at[b], there.at[b], save_sem.at[i, b]) for i, (here, there) in enumerate(pairs)
        ]

    def start_where(conditions, copy):
        for side in order:

            @pl.when(conditions[side])
            def _(side=side):
                copy(side).start()

    def wait_for(copy):
        for side in order:

            @pl.when(to[side])
            def _(side=side):
                copy(side).wait_send()

            @pl.when(since[side])
            def _(side=side):
                copy(side).wait_recv()

    start_where(to, face_copy)
    clear_operands(q_s, k_s, v_s)
    wt_ref[...] = w_ref[...].astype(F32).T.astype(BF16)
    loads[0].wait()

    @pl.loop(0, blocks)
    def _(b):
        lay_interior(b, nb_ref, vox_s, a_s, b_s)

    loads[1].wait()
    pair_weights(cw_s, w_s)
    wait_for(face_copy)
    faces = [face_s.at[f] for f in range(4)]

    @pl.loop(0, blocks // 2)
    def _(i):
        b = 2 * i
        lay_faces(b, nb_ref, faces, a_s, b_s)
        lay_faces(b + 1, nb_ref, faces, a_s, b_s)

        @pl.when(i > 0)
        def _():
            start_where(to, functools.partial(passing, b - 2))
            start_where(to, functools.partial(passing, b - 1))

        conv_block(b, vox_s, w_s, a_s, b_s, mixed_s, normed_s)
        conv_block(b + 1, vox_s, w_s, a_s, b_s, mixed_s, normed_s)

    start_where(to, functools.partial(passing, blocks - 2))
    start_where(to, functools.partial(passing, blocks - 1))

    def project(b):
        factor = math.log2(math.e) / math.sqrt(width)
        normed = padded(normed_s[b], 0, LANES)
        keys, turned = products(
            (normed, padded(w_ref[:, ch : 2 * ch], LANES, LANES), False), (padded(wt_ref[...], 0, LANES), normed, True)
        )
        keys = keys[:, :ch].astype(BF16)
        queries = (turned[:ch] * factor).astype(BF16)
        values = turned[2 * ch :].astype(BF16)
        queries_s[b], keys_s[b], values_s[b] = queries, keys, values
        norm_s[0, b] = largest_norm(queries, width)
        norm_s[1, b] = largest_norm(turned[ch : 2 * ch], width)
        put_key_set(keys, values, k_s, v_s, b, width)

    @pl.loop(0, blocks // 2)
    def _(i):
        project(2 * i)
        project(2 * i + 1)

    @pl.loop(0, blocks)
    def _(b):
        put_queries(queries_s[b], q_s, width)

        def visit(add):
            below, above = nb_ref[b, 4], nb_ref[b, 5]
            own = (b, None)
            low = (jnp.where(below >= 0, below, b), below >= 0)
            high = (jnp.where(above >= 0, above, b), above >= 0)

            @pl.when(b == 0)
            def _():
                add([own, high], q_s, k_s, v_s)

            @pl.when(jnp.logical_and(b > 0, b < blocks - 1))
            def _():
                add([own, low, high], q_s, k_s, v_s)

            @pl.when(b == blocks - 1)
            def _():
                add([own, low], q_s, k_s, v_s)

        def store(h, lanes, value):
            sum_s[b, h * width : (h + 1) * width, lanes] = value[:width]
            den_s[b, h : h + 1, lanes] = value[width : width + 1]

        add_pairs(visit, store)

        @pl.when(b > 0)
        def _():
            for save in saves(b - 1):
                save.start()

    for save in saves(blocks - 1):
        save.start()
    for b in range(blocks):
        qn_ref[b] = jnp.max(norm_s[0, b])
        kn_ref[b] = jnp.max(norm_s[1, b])

    @pl.loop(0, blocks)
    def _(b):
        for save in saves(b):
            save.wait()
        wait_for(functools.partial(passing, b))


def back_kernel(
    nb_ref, cnt_ref, qn_ref, kn_ref, mixed_ref, q_ref, sum_ref, den_ref, k_ref, v_ref, r0, r1, r2, r3,
    w_ref, wt_ref, wo_ref, out_ref,
    q_s, k_s, v_s, o_s, m_s, key_s, value_s, mixed_s, queries_s, sum_s, den_s, got_s, out_s, blank_s, norm_s,
    load_sem, got_sem, out_sem
):
    blocks, _, ch = mixed_s.shape
    width = ch // HEADS
    count = cnt_ref[0]
    got = (r0, r1, r2, r3)

    def loads(b):
        pairs = ((mixed_ref, mixed_s), (q_ref, queries_s), (sum_ref, sum_s), (den_ref, den_s))
        return [
            pltpu.make_async_copy(there.at[b], here.at[b], load_sem.at[i, b]) for i, (there, here) in enumerate(pairs)
        ]

    def fetch(b, face):
        slot = jnp.maximum(nb_ref[b, face], 0)
        return pltpu.make_async_copy(got[face].at[slot], got_s.at[face, b], got_sem.at[face, b])

    def save(b, source):
        return pltpu.make_async_copy(source, out_ref.at[b], out_sem.at[b])

    @pl.loop(0, count)
    def _(b):
        for face in range(4):

            @pl.when(nb_ref[b, face] >= 0)
            def _(face=face):
                fetch(b, face).start()

        for load in loads(b):
            load.start()

    blank_s[...] = jnp.zeros(blank_s.shape, blank_s.dtype)
    clear_operands(q_s, k_s, v_s)

    @pl.loop(count, blocks)
    def _(b):
        save(b, blank_s).start()

    @pl.loop(0, count)
    def _(b):
        n = jnp.int32(0)
        kn = kn_ref[b]
        norm_s[...] = jnp.zeros(norm_s.shape, F32)
        for face in (4, 5):
            slot = nb_ref[b, face]
            kn = jnp.where(slot >= 0, jnp.maximum(kn, kn_ref[jnp.maximum(slot, 0)]), kn)
        for face in range(4):
            there = nb_ref[b, face] >= 0

            @pl.when(there)
            def _(face=face, n=n):
                fetch(b, face).wait()
                normed = padded(got_s[face, b], 0, LANES)
                keys, turned = products(
                    (normed, padded(w_ref[:, ch : 2 * ch], LANES, LANES), False),
                    (padded(wt_ref[ch:], 0, LANES), normed, True),
                )
                put_key_set(keys[:, :ch].astype(BF16), turned[ch:].astype(BF16), k_s, v_s, n, width)
                norm_s[...] = jnp.maximum(norm_s[...], largest_norm(turned[:ch], width))

            n = jnp.where(there, n + 1, n)
        kn = lax.cond(n > 0, lambda: jnp.maximum(kn, jnp.max(norm_s[...])), lambda: kn)
        for load in loads(b):
            load.wait()
        fast = qn_ref[b] * kn <= LIMIT * LIMIT

        def finish(take):
            parts = []
            for h in range(HEADS):
                total, weight = take(h)
                parts.append(total * (1.0 / weight))
            attended = jnp.concatenate(parts, axis=0).T.astype(BF16)
            moved = product(padded(attended, 0, LANES), padded(wo_ref[...], LANES, LANES))[:, :ch]
            out_s[b] = (mixed_s[b].astype(F32) + moved).astype(BF16)

        def own(h):
            return sum_s[b, h * width : (h + 1) * width], den_s[b, h : h + 1]

        @pl.when(jnp.logical_and(fast, n == 0))
        def _():
            finish(own)

        @pl.when(jnp.logical_and(fast, n > 0))
        def _():
            put_queries(queries_s[b], q_s, width)

            def visit(add):
                @pl.loop(0, n // 2)
                def _(i):
                    add([(2 * i, None), (2 * i + 1, None)], q_s, k_s, v_s)

                @pl.when(n % 2 == 1)
                def _():
                    add([(n - 1, None)], q_s, k_s, v_s)

            def store(h, lanes, value):
                o_s[h, :, lanes] = value

            add_pairs(visit, store)

            def both(h):
                total, weight = own(h)
                return total + o_s[h, :width], weight + o_s[h, width : width + 1]

            finish(both)

        @pl.when(jnp.logical_not(fast))
        def _():
            put_queries(queries_s[b], q_s, width)
            sets = n
            for slot in (b, nb_ref[b, 4], nb_ref[b, 5]):

                @pl.when(slot >= 0)
                def _(slot=slot, sets=sets):
                    pltpu.sync_copy(k_ref.at[slot], key_s)
                    pltpu.sync_copy(v_ref.at[slot], value_s)
                    put_key_set(key_s[...], value_s[...], k_s, v_s, sets, width)

                sets = jnp.where(slot >= 0, sets + 1, sets)
            o_s[...] = jnp.zeros(o_s.shape, F32)
            m_s[...] = jnp.full(m_s.shape, -1e30, F32)

            @pl.loop(0, sets)
            def _(i):
                add_pair_running(i, q_s, k_s, v_s, o_s, m_s)

            finish(lambda h: (o_s[h, :width], o_s[h, width : width + 1]))

        save(b, out_s.at[b]).start()

    @pl.loop(0, count)
    def _(b):
        save(b, out_s.at[b]).wait()

    @pl.loop(count, blocks)
    def _(b):
        save(b, blank_s).wait()


def body(voxels, neighbours, block_count, conv_weight, qkv_weight, out_weight):
    blocks, vox, ch = voxels.shape
    cubes = voxels.reshape(blocks, SIDE, SIDE, SIDE, ch)
    vmem = pl.BlockSpec(memory_space=pltpu.VMEM)
    smem = pl.BlockSpec(memory_space=pltpu.SMEM)
    hbm = pl.BlockSpec(memory_space=pl.ANY)
    like = jax.ShapeDtypeStruct(voxels.shape, BF16)
    turned = jax.ShapeDtypeStruct((blocks, ch, vox), BF16)
    scalars = jax.ShapeDtypeStruct((blocks,), F32)
    n_gx, n_gy = lax.axis_size("gx"), lax.axis_size("gy")

    def operands(slots):
        return [
            pltpu.VMEM((HEADS, 2 * ch, vox), BF16),
            pltpu.VMEM((slots, vox, 2 * ch), BF16),
            pltpu.VMEM((slots, HEADS, VALUE_ROWS, vox), BF16),
        ]

    mixed, q, k, v, total, weight, wt, qn, kn, *got = pl.pallas_call(
        functools.partial(front_kernel, (n_gx, n_gy)),
        out_shape=[
            like, turned, like, turned,
            jax.ShapeDtypeStruct((blocks, ch, vox), F32),
            jax.ShapeDtypeStruct((blocks, HEADS, vox), F32),
            jax.ShapeDtypeStruct((3 * ch, ch), BF16),
            scalars, scalars,
        ] + [like] * 4,
        in_specs=[smem, hbm, hbm, hbm, vmem],
        out_specs=[hbm] * 6 + [vmem] + [smem] * 2 + [hbm] * 4,
        scratch_shapes=[
            pltpu.VMEM((36 * ch, 2 * ch), BF16),
            pltpu.VMEM((blocks, 3, SIDE + 2, SIDE * SIDE + 2 * SIDE, ch), BF16),
            pltpu.VMEM((blocks, 3, SIDE + 2, SIDE * SIDE, ch), BF16),
            pltpu.VMEM(voxels.shape, BF16),
            pltpu.VMEM((4, blocks, SIDE, SIDE, ch), BF16),
            *operands(blocks),
            pltpu.VMEM(voxels.shape, BF16),
            pltpu.VMEM(conv_weight.shape, BF16),
            pltpu.VMEM(voxels.shape, BF16),
            pltpu.VMEM((blocks, ch, vox), BF16),
            pltpu.VMEM(voxels.shape, BF16),
            pltpu.VMEM((blocks, ch, vox), BF16),
            pltpu.VMEM((blocks, ch, vox), F32),
            pltpu.VMEM((blocks, HEADS, vox), F32),
            pltpu.VMEM((2, blocks, 1, vox), F32),
            pltpu.SemaphoreType.DMA((4,)),
            pltpu.SemaphoreType.DMA((4,)),
            pltpu.SemaphoreType.DMA((4, blocks)),
            pltpu.SemaphoreType.DMA((4, blocks)),
            pltpu.SemaphoreType.DMA((2,)),
            pltpu.SemaphoreType.DMA((6, blocks)),
        ],
        compiler_params=pltpu.CompilerParams(collective_id=0, has_side_effects=True),
        name="front",
    )(neighbours, voxels, cubes, conv_weight, qkv_weight)

    return pl.pallas_call(
        back_kernel,
        out_shape=like,
        in_specs=[smem] * 4 + [hbm] * 10 + [vmem] * 3,
        out_specs=hbm,
        scratch_shapes=[
            *operands(7),
            pltpu.VMEM((HEADS, VALUE_ROWS, vox), F32),
            pltpu.VMEM((HEADS, 1, vox), F32),
            pltpu.VMEM((vox, ch), BF16),
            pltpu.VMEM((ch, vox), BF16),
            pltpu.VMEM(voxels.shape, BF16),
            pltpu.VMEM((blocks, ch, vox), BF16),
            pltpu.VMEM((blocks, ch, vox), F32),
            pltpu.VMEM((blocks, HEADS, vox), F32),
            pltpu.VMEM((4,) + voxels.shape, BF16),
            pltpu.VMEM(voxels.shape, BF16),
            pltpu.VMEM((vox, ch), BF16),
            pltpu.VMEM((1, vox), F32),
            pltpu.SemaphoreType.DMA((4, blocks)),
            pltpu.SemaphoreType.DMA((4, blocks)),
            pltpu.SemaphoreType.DMA((blocks,)),
        ],
        name="back",
    )(neighbours, block_count, qn, kn, mixed, q, total, weight, k, v, *got, qkv_weight, wt, out_weight)


def solution(mesh):
    placed = (P(("gx", "gy"), None, None), P(("gx", "gy"), None), P(("gx", "gy")), P(), P(), P())
    return jax.shard_map(
        body, mesh=mesh, in_specs=placed, out_specs=P(("gx", "gy"), None, None), check_vma=False
    )
```

```python
import functools
import math

import jax
import jax.numpy as jnp
from jax import lax
from jax.experimental import pallas as pl
from jax.experimental.pallas import tpu as pltpu
from jax.sharding import PartitionSpec as P

HEADS = 4
SIDE = 8
LIMIT = 90.0
F32 = jnp.float32
BF16 = jnp.bfloat16
NT = (((1,), (1,)), ((), ()))
ROWS = 128
LANES = 256
VALUE_ROWS = 48
MESH = pl.DeviceIdType.MESH


def shifted_z(x, below, above):
    at = lax.broadcasted_iota(jnp.int32, x.shape, 1)
    down = pltpu.roll(jnp.where(at == SIDE - 1, below, x), 1, 1)
    up = pltpu.roll(jnp.where(at == 0, above, x), SIDE - 1, 1)
    return [down, x, up]


def picked(ref, slot, ch):
    value = ref[jnp.maximum(slot, 0)].astype(F32).reshape(-1, SIDE, ch)
    return jnp.where(slot >= 0, value, 0.0)


def lay_interior(b, nb_ref, vox_s, a_s, b_s):
    rows, ch = SIDE * SIDE, vox_s.shape[-1]
    own = vox_s[b].astype(F32).reshape(rows, SIDE, ch)
    inner = shifted_z(own, picked(vox_s, nb_ref[b, 4], ch), picked(vox_s, nb_ref[b, 5], ch))
    blank = jnp.zeros((SIDE, ch), F32)
    for e in range(3):
        for s in range(1, SIDE + 1):
            mid = inner[e][(s - 1) * SIDE : s * SIDE].reshape(rows, ch)
            a_s[b, e, s] = jnp.concatenate([blank, mid, blank], axis=0).astype(BF16)
            b_s[b, e, s] = mid.astype(BF16)


def lay_faces(b, nb_ref, faces, a_s, b_s):
    rows, ch = SIDE * SIDE, a_s.shape[-1]
    xm, xp, ym, yp = [shifted_z(picked(ref, nb_ref[b, f], ch), 0.0, 0.0) for f, ref in enumerate(faces)]
    blank = jnp.zeros((SIDE, ch), F32)
    end = rows + 2 * SIDE
    for e in range(3):
        for s, face in ((0, xm), (SIDE + 1, xp)):
            mid = face[e].reshape(rows, ch)
            a_s[b, e, s] = jnp.concatenate([blank, mid, blank], axis=0).astype(BF16)
            b_s[b, e, s] = mid.astype(BF16)
        for s in range(1, SIDE + 1):
            first = a_s[b, e, s, : 2 * SIDE].astype(F32)
            last = a_s[b, e, s, end - 2 * SIDE :].astype(F32)
            a_s[b, e, s, : 2 * SIDE] = jnp.concatenate([ym[e][s - 1], first[SIDE:]], axis=0).astype(BF16)
            a_s[b, e, s, end - 2 * SIDE :] = jnp.concatenate([last[:SIDE], yp[e][s - 1]], axis=0).astype(BF16)


def conv_block(b, vox_s, w_s, a_s, b_s, mixed_ref, normed_ref):
    rows, ch = SIDE * SIDE, vox_s.shape[-1]
    own = vox_s[b].astype(F32).reshape(rows, SIDE, ch)

    def tile(c, e, unit):
        def slab(x):
            return b_s[b, e, x] if c == 1 else a_s[b, e, x, c * SIDE : c * SIDE + rows]

        pairs = [2 * k + 2 * unit for k in range(4)]
        return jnp.concatenate([jnp.concatenate([slab(x), slab(x + 1)], axis=1) for x in pairs], axis=0)

    def inner(*accs):
        for c in range(3):
            for e in range(3):
                for unit in range(2):
                    reg = (c * 3 + e) % 2
                    at = ((c * 3 + e) * 2 + unit) * LANES
                    pltpu.matmul_push_rhs(w_s[at : at + LANES], reg, unit)
                    pltpu.matmul_acc_lhs(accs[unit], tile(c, e, unit), load_staged_rhs=reg)
        return pltpu.matmul_pop(accs[0]) + pltpu.matmul_pop(accs[1])

    acc = pl.run_scoped(inner, *[pltpu.ACC(u)((4 * rows, LANES), F32) for u in range(2)])
    for k in range(4):
        for o in range(2):
            x = 2 * k + o
            here = own[x * SIDE : (x + 1) * SIDE].reshape(rows, ch)
            mixed = (here + acc[k * rows : (k + 1) * rows, o * ch : (o + 1) * ch]).astype(BF16)
            mixed_ref[b, x * rows : (x + 1) * rows] = mixed
            wide = mixed.astype(F32)
            square = jnp.mean(wide * wide, axis=-1, keepdims=True)
            normed_ref[b, x * rows : (x + 1) * rows] = (wide * lax.rsqrt(square + 1e-06)).astype(BF16)


def pair_weights(cw_ref, w_s):
    ch = cw_ref.shape[-1]
    for ce in range(9):
        for r in range(4):
            for o in range(2):
                row = (ce * 4 + r) * ch
                tap = r - o
                value = cw_ref[tap * 9 + ce] if 0 <= tap <= 2 else jnp.zeros((ch, ch), BF16)
                w_s[row : row + ch, o * ch : (o + 1) * ch] = value


def clear_operands(q_s, k_s, v_s):
    q_s[...] = jnp.zeros(q_s.shape, q_s.dtype)
    k_s[...] = jnp.zeros(k_s.shape, k_s.dtype)
    v_s[...] = jnp.ones(v_s.shape, v_s.dtype)


def put_queries(queries, q_s, width):
    for h in range(HEADS):
        q_s[h, h * width : (h + 1) * width] = queries[h * width : (h + 1) * width]


def put_key_set(keys, values, k_s, v_s, slot, width):
    k_s[slot, :, : HEADS * width] = keys
    for h in range(HEADS):
        v_s[slot, h, :width] = values[h * width : (h + 1) * width]


def largest_norm(x, width):
    wide = x.astype(F32)
    return jnp.max(jnp.sum((wide * wide).reshape(HEADS, width, -1), axis=1), axis=0, keepdims=True) * 1.02


def products(*terms):
    plans = []
    for lhs, rhs, transpose in terms:
        halves = rhs.shape[0 if transpose else 1] == LANES
        plans.append((lhs, rhs, transpose, halves, lhs.shape[0] // 2 if halves else lhs.shape[0]))

    def inner(*accs):
        reg = 0
        for p, (lhs, rhs, transpose, halves, rows) in enumerate(plans):
            for t in range(lhs.shape[1] // LANES):
                deep = slice(t * LANES, (t + 1) * LANES)
                for u in range(2):
                    part = lhs[u * rows : (u + 1) * rows] if halves else lhs
                    wide = slice(0, LANES) if halves else slice(u * LANES, (u + 1) * LANES)
                    tile = rhs[wide, deep] if transpose else rhs[deep, wide]
                    pltpu.matmul_push_rhs(tile, reg, u, transpose=transpose)
                    pltpu.matmul_acc_lhs(accs[2 * p + u], part[:, deep], load_staged_rhs=reg)
                reg = 1 - reg
        return [
            jnp.concatenate([pltpu.matmul_pop(acc) for acc in accs[2 * p : 2 * p + 2]], axis=0 if plan[3] else 1)
            for p, plan in enumerate(plans)
        ]

    return pl.run_scoped(inner, *[pltpu.ACC(u)((plan[4], LANES), F32) for plan in plans for u in range(2)])


def product(lhs, rhs, transpose=False):
    return products((lhs, rhs, transpose))[0]


def padded(x, rows, cols):
    if x.shape[1] < cols:
        x = jnp.concatenate([x, jnp.zeros((x.shape[0], cols - x.shape[1]), x.dtype)], axis=1)
    if x.shape[0] < rows:
        x = jnp.concatenate([x, jnp.zeros((rows - x.shape[0], x.shape[1]), x.dtype)], axis=0)
    return x


def add_chain(sets, q_s, k_s, v_s, score_acc, value_acc):
    per_tile, per_head = LANES // ROWS, k_s.shape[1] // ROWS
    ring = len(score_acc[0])
    units = range(2)
    steps = HEADS * len(sets)

    def chunk(unit, h, c):
        return score_acc[unit][(per_head * h + c) % ring]

    def stage_queries(h, unit, reg):
        pltpu.matmul_push_rhs(q_s[h % HEADS, :, unit * LANES : (unit + 1) * LANES], reg, unit)

    def score(h, unit, chunks, reg):
        for c in chunks:
            rows = k_s[sets[h // HEADS][0], c * ROWS : (c + 1) * ROWS]
            pltpu.matmul_acc_lhs(chunk(unit, h, c), rows, load_staged_rhs=reg if c == 0 else None)

    def stage_weights(h, unit, tile, reg):
        parts = [
            jnp.exp2(pltpu.matmul_pop(chunk(unit, h, c))).astype(BF16)
            for c in range(tile * per_tile, (tile + 1) * per_tile)
        ]
        pltpu.matmul_push_rhs(jnp.concatenate(parts, axis=0), reg, unit)

    def mix(h, unit, tile, reg):
        slot, there = sets[h // HEADS]
        rows = v_s[slot, h % HEADS, :, tile * LANES : (tile + 1) * LANES]
        if there is not None:
            rows = jnp.where(there, rows, jnp.zeros_like(rows))
        pltpu.matmul_acc_lhs(value_acc[unit][h % HEADS], rows, load_staged_rhs=reg)

    for u in units:
        stage_queries(0, u, 0)
    for u in units:
        score(0, u, range(per_head), 0)
    for u in units:
        stage_queries(1, u, 1)
    reg = 1
    for h in range(steps):
        if h + 1 < steps:
            for u in units:
                score(h + 1, u, range(per_tile), reg)
        for u in units:
            stage_weights(h, u, 0, 1 - reg)
        if h + 1 < steps:
            for u in units:
                score(h + 1, u, range(per_tile, per_head), None)
        for u in units:
            stage_weights(h, u, 1, reg)
        for u in units:
            mix(h, u, 0, 1 - reg)
        if h + 2 < steps:
            for u in units:
                stage_queries(h + 2, u, 1 - reg)
        for u in units:
            mix(h, u, 1, reg)
        reg = 1 - reg


def add_pairs(visit, store):
    ring = 6

    def inner(*accs):
        score_acc = [accs[:ring], accs[ring : 2 * ring]]
        value_acc = [accs[2 * ring : 2 * ring + HEADS], accs[2 * ring + HEADS :]]
        visit(lambda sets, q_s, k_s, v_s: add_chain(sets, q_s, k_s, v_s, score_acc, value_acc))
        for h in range(HEADS):
            for u in range(2):
                store(h, slice(u * LANES, (u + 1) * LANES), pltpu.matmul_pop(value_acc[u][h]))

    scores = [pltpu.ACC(u)((ROWS, LANES), F32) for u in range(2) for _ in range(ring)]
    values = [pltpu.ACC(u)((VALUE_ROWS, LANES), F32) for u in range(2) for _ in range(HEADS)]
    pl.run_scoped(inner, *scores, *values)


def add_pair_running(slot, q_s, k_s, v_s, o_s, m_s):
    for h in range(HEADS):
        scores = product(k_s[slot], q_s[h])
        old = m_s[h]
        new = jnp.maximum(old, jnp.max(scores, axis=0, keepdims=True))
        weights = jnp.exp2(scores - new).astype(BF16)
        o_s[h] = o_s[h] * jnp.exp2(old - new) + product(v_s[slot, h], weights)
        m_s[h] = new


def front_kernel(
    sizes, nb_ref, vox_ref, cube_ref, cw_ref, w_ref,
    mixed_ref, q_ref, k_ref, v_ref, sum_ref, den_ref, wt_ref, qn_ref, kn_ref, got0, got1, got2, got3,
    w_s, a_s, b_s, normed_s, face_s, q_s, k_s, v_s, vox_s, cw_s, mixed_s, queries_s, keys_s, values_s, sum_s, den_s, norm_s,
    face_out, face_in, send_sem, recv_sem, load_sem, save_sem
):
    gx, gy = lax.axis_index("gx"), lax.axis_index("gy")
    n_gx, n_gy = sizes
    blocks, _, ch = vox_s.shape
    width = ch // HEADS
    got = (got0, got1, got2, got3)
    up_x, down_x = lax.rem(gx + 1, n_gx), lax.rem(gx + n_gx - 1, n_gx)
    up_y, down_y = lax.rem(gy + 1, n_gy), lax.rem(gy + n_gy - 1, n_gy)
    peers = [(up_x, gy), (down_x, gy), (gx, up_y), (gx, down_y)]
    to = [gx < n_gx - 1, gx > 0, gy < n_gy - 1, gy > 0]
    since = [to[1], to[0], to[3], to[2]]
    order = (2, 3, 0, 1)
    layers = [cube_ref.at[:, SIDE - 1], cube_ref.at[:, 0], cube_ref.at[:, :, SIDE - 1], cube_ref.at[:, :, 0]]

    loads = [
        pltpu.make_async_copy(vox_ref, vox_s, load_sem.at[0]),
        pltpu.make_async_copy(cw_ref, cw_s, load_sem.at[1]),
    ]
    for load in loads:
        load.start()

    barrier = pltpu.get_barrier_semaphore()
    for side in order:

        @pl.when(to[side])
        def _(side=side):
            pl.semaphore_signal(barrier, inc=1, device_id=peers[side], device_id_type=MESH)

    pl.semaphore_wait(barrier, sum(there.astype(jnp.int32) for there in to))

    def face_copy(f):
        return pltpu.make_async_remote_copy(
            src_ref=layers[f], dst_ref=face_s.at[f], send_sem=face_out.at[f], recv_sem=face_in.at[f],
            device_id=peers[f], device_id_type=MESH,
        )

    def passing(b, side):
        return pltpu.make_async_remote_copy(
            src_ref=normed_s.at[b], dst_ref=got[side].at[b],
            send_sem=send_sem.at[side, b], recv_sem=recv_sem.at[side, b],
            device_id=peers[side], device_id_type=MESH,
        )

    def saves(b):
        pairs = (
            (mixed_s, mixed_ref), (queries_s, q_ref), (keys_s, k_ref), (values_s, v_ref), (sum_s, sum_ref), (den_s, den_ref)
        )
        return [
            pltpu.make_async_copy(here.at[b], there.at[b], save_sem.at[i, b]) for i, (here, there) in enumerate(pairs)
        ]

    def start_where(conditions, copy):
        for side in order:

            @pl.when(conditions[side])
            def _(side=side):
                copy(side).start()

    def wait_for(copy):
        for side in order:

            @pl.when(to[side])
            def _(side=side):
                copy(side).wait_send()

            @pl.when(since[side])
            def _(side=side):
                copy(side).wait_recv()

    start_where(to, face_copy)
    clear_operands(q_s, k_s, v_s)
    wt_ref[...] = w_ref[...].astype(F32).T.astype(BF16)
    loads[0].wait()

    @pl.loop(0, blocks)
    def _(b):
        lay_interior(b, nb_ref, vox_s, a_s, b_s)

    loads[1].wait()
    pair_weights(cw_s, w_s)
    wait_for(face_copy)
    faces = [face_s.at[f] for f in range(4)]

    @pl.loop(0, blocks // 2)
    def _(i):
        b = 2 * i
        lay_faces(b, nb_ref, faces, a_s, b_s)
        lay_faces(b + 1, nb_ref, faces, a_s, b_s)

        @pl.when(i > 0)
        def _():
            start_where(to, functools.partial(passing, b - 2))
            start_where(to, functools.partial(passing, b - 1))

        conv_block(b, vox_s, w_s, a_s, b_s, mixed_s, normed_s)
        conv_block(b + 1, vox_s, w_s, a_s, b_s, mixed_s, normed_s)

    start_where(to, functools.partial(passing, blocks - 2))
    start_where(to, functools.partial(passing, blocks - 1))

    def project(b):
        factor = math.log2(math.e) / math.sqrt(width)
        normed = padded(normed_s[b], 0, LANES)
        keys, turned = products(
            (normed, padded(w_ref[:, ch : 2 * ch], LANES, LANES), False), (padded(wt_ref[...], 0, LANES), normed, True)
        )
        keys = keys[:, :ch].astype(BF16)
        queries = (turned[:ch] * factor).astype(BF16)
        values = turned[2 * ch :].astype(BF16)
        queries_s[b], keys_s[b], values_s[b] = queries, keys, values
        norm_s[0, b] = largest_norm(queries, width)
        norm_s[1, b] = largest_norm(turned[ch : 2 * ch], width)
        put_key_set(keys, values, k_s, v_s, b, width)

    @pl.loop(0, blocks // 4)
    def _(i):
        for k in range(4):
            project(4 * i + k)

    @pl.loop(0, blocks)
    def _(b):
        put_queries(queries_s[b], q_s, width)

        def visit(add):
            below, above = nb_ref[b, 4], nb_ref[b, 5]
            own = (b, None)
            low = (jnp.where(below >= 0, below, b), below >= 0)
            high = (jnp.where(above >= 0, above, b), above >= 0)

            @pl.when(b == 0)
            def _():
                add([own, high], q_s, k_s, v_s)

            @pl.when(jnp.logical_and(b > 0, b < blocks - 1))
            def _():
                add([own, low, high], q_s, k_s, v_s)

            @pl.when(b == blocks - 1)
            def _():
                add([own, low], q_s, k_s, v_s)

        def store(h, lanes, value):
            sum_s[b, h * width : (h + 1) * width, lanes] = value[:width]
            den_s[b, h : h + 1, lanes] = value[width : width + 1]

        add_pairs(visit, store)

        @pl.when(b > 0)
        def _():
            for save in saves(b - 1):
                save.start()

    for save in saves(blocks - 1):
        save.start()
    for b in range(blocks):
        qn_ref[b] = jnp.max(norm_s[0, b])
        kn_ref[b] = jnp.max(norm_s[1, b])

    @pl.loop(0, blocks)
    def _(b):
        for save in saves(b):
            save.wait()
        wait_for(functools.partial(passing, b))


def back_kernel(
    nb_ref, cnt_ref, qn_ref, kn_ref, mixed_ref, q_ref, sum_ref, den_ref, k_ref, v_ref, r0, r1, r2, r3,
    w_ref, wt_ref, wo_ref, out_ref,
    q_s, k_s, v_s, o_s, m_s, key_s, value_s, mixed_s, queries_s, sum_s, den_s, got_s, out_s, blank_s, norm_s,
    load_sem, got_sem, out_sem
):
    blocks, _, ch = mixed_s.shape
    width = ch // HEADS
    count = cnt_ref[0]
    got = (r0, r1, r2, r3)

    def loads(b):
        pairs = ((mixed_ref, mixed_s), (q_ref, queries_s), (sum_ref, sum_s), (den_ref, den_s))
        return [
            pltpu.make_async_copy(there.at[b], here.at[b], load_sem.at[i, b]) for i, (there, here) in enumerate(pairs)
        ]

    def fetch(b, face):
        slot = jnp.maximum(nb_ref[b, face], 0)
        return pltpu.make_async_copy(got[face].at[slot], got_s.at[face, b], got_sem.at[face, b])

    def save(b, source):
        return pltpu.make_async_copy(source, out_ref.at[b], out_sem.at[b])

    @pl.loop(0, count)
    def _(b):
        for face in range(4):

            @pl.when(nb_ref[b, face] >= 0)
            def _(face=face):
                fetch(b, face).start()

        for load in loads(b):
            load.start()

    blank_s[...] = jnp.zeros(blank_s.shape, blank_s.dtype)
    clear_operands(q_s, k_s, v_s)

    @pl.loop(count, blocks)
    def _(b):
        save(b, blank_s).start()

    @pl.loop(0, count)
    def _(b):
        n = jnp.int32(0)
        kn = kn_ref[b]
        norm_s[...] = jnp.zeros(norm_s.shape, F32)
        for face in (4, 5):
            slot = nb_ref[b, face]
            kn = jnp.where(slot >= 0, jnp.maximum(kn, kn_ref[jnp.maximum(slot, 0)]), kn)
        for face in range(4):
            there = nb_ref[b, face] >= 0

            @pl.when(there)
            def _(face=face, n=n):
                fetch(b, face).wait()
                normed = padded(got_s[face, b], 0, LANES)
                keys, turned = products(
                    (normed, padded(w_ref[:, ch : 2 * ch], LANES, LANES), False),
                    (padded(wt_ref[ch:], 0, LANES), normed, True),
                )
                put_key_set(keys[:, :ch].astype(BF16), turned[ch:].astype(BF16), k_s, v_s, n, width)
                norm_s[...] = jnp.maximum(norm_s[...], largest_norm(turned[:ch], width))

            n = jnp.where(there, n + 1, n)
        kn = lax.cond(n > 0, lambda: jnp.maximum(kn, jnp.max(norm_s[...])), lambda: kn)
        for load in loads(b):
            load.wait()
        fast = qn_ref[b] * kn <= LIMIT * LIMIT

        def finish(take):
            parts = []
            for h in range(HEADS):
                total, weight = take(h)
                parts.append(total * (1.0 / weight))
            attended = jnp.concatenate(parts, axis=0).T.astype(BF16)
            moved = product(padded(attended, 0, LANES), padded(wo_ref[...], LANES, LANES))[:, :ch]
            out_s[b] = (mixed_s[b].astype(F32) + moved).astype(BF16)

        def own(h):
            return sum_s[b, h * width : (h + 1) * width], den_s[b, h : h + 1]

        @pl.when(jnp.logical_and(fast, n == 0))
        def _():
            finish(own)

        @pl.when(jnp.logical_and(fast, n > 0))
        def _():
            put_queries(queries_s[b], q_s, width)

            def visit(add):
                @pl.loop(0, n // 2)
                def _(i):
                    add([(2 * i, None), (2 * i + 1, None)], q_s, k_s, v_s)

                @pl.when(n % 2 == 1)
                def _():
                    add([(n - 1, None)], q_s, k_s, v_s)

            def store(h, lanes, value):
                o_s[h, :, lanes] = value

            add_pairs(visit, store)

            def both(h):
                total, weight = own(h)
                return total + o_s[h, :width], weight + o_s[h, width : width + 1]

            finish(both)

        @pl.when(jnp.logical_not(fast))
        def _():
            put_queries(queries_s[b], q_s, width)
            sets = n
            for slot in (b, nb_ref[b, 4], nb_ref[b, 5]):

                @pl.when(slot >= 0)
                def _(slot=slot, sets=sets):
                    pltpu.sync_copy(k_ref.at[slot], key_s)
                    pltpu.sync_copy(v_ref.at[slot], value_s)
                    put_key_set(key_s[...], value_s[...], k_s, v_s, sets, width)

                sets = jnp.where(slot >= 0, sets + 1, sets)
            o_s[...] = jnp.zeros(o_s.shape, F32)
            m_s[...] = jnp.full(m_s.shape, -1e30, F32)

            @pl.loop(0, sets)
            def _(i):
                add_pair_running(i, q_s, k_s, v_s, o_s, m_s)

            finish(lambda h: (o_s[h, :width], o_s[h, width : width + 1]))

        save(b, out_s.at[b]).start()

    @pl.loop(0, count)
    def _(b):
        save(b, out_s.at[b]).wait()

    @pl.loop(count, blocks)
    def _(b):
        save(b, blank_s).wait()


def body(voxels, neighbours, block_count, conv_weight, qkv_weight, out_weight):
    blocks, vox, ch = voxels.shape
    cubes = voxels.reshape(blocks, SIDE, SIDE, SIDE, ch)
    vmem = pl.BlockSpec(memory_space=pltpu.VMEM)
    smem = pl.BlockSpec(memory_space=pltpu.SMEM)
    hbm = pl.BlockSpec(memory_space=pl.ANY)
    like = jax.ShapeDtypeStruct(voxels.shape, BF16)
    turned = jax.ShapeDtypeStruct((blocks, ch, vox), BF16)
    scalars = jax.ShapeDtypeStruct((blocks,), F32)
    n_gx, n_gy = lax.axis_size("gx"), lax.axis_size("gy")

    def operands(slots):
        return [
            pltpu.VMEM((HEADS, 2 * ch, vox), BF16),
            pltpu.VMEM((slots, vox, 2 * ch), BF16),
            pltpu.VMEM((slots, HEADS, VALUE_ROWS, vox), BF16),
        ]

    mixed, q, k, v, total, weight, wt, qn, kn, *got = pl.pallas_call(
        functools.partial(front_kernel, (n_gx, n_gy)),
        out_shape=[
            like, turned, like, turned,
            jax.ShapeDtypeStruct((blocks, ch, vox), F32),
            jax.ShapeDtypeStruct((blocks, HEADS, vox), F32),
            jax.ShapeDtypeStruct((3 * ch, ch), BF16),
            scalars, scalars,
        ] + [like] * 4,
        in_specs=[smem, hbm, hbm, hbm, vmem],
        out_specs=[hbm] * 6 + [vmem] + [smem] * 2 + [hbm] * 4,
        scratch_shapes=[
            pltpu.VMEM((36 * ch, 2 * ch), BF16),
            pltpu.VMEM((blocks, 3, SIDE + 2, SIDE * SIDE + 2 * SIDE, ch), BF16),
            pltpu.VMEM((blocks, 3, SIDE + 2, SIDE * SIDE, ch), BF16),
            pltpu.VMEM(voxels.shape, BF16),
            pltpu.VMEM((4, blocks, SIDE, SIDE, ch), BF16),
            *operands(blocks),
            pltpu.VMEM(voxels.shape, BF16),
            pltpu.VMEM(conv_weight.shape, BF16),
            pltpu.VMEM(voxels.shape, BF16),
            pltpu.VMEM((blocks, ch, vox), BF16),
            pltpu.VMEM(voxels.shape, BF16),
            pltpu.VMEM((blocks, ch, vox), BF16),
            pltpu.VMEM((blocks, ch, vox), F32),
            pltpu.VMEM((blocks, HEADS, vox), F32),
            pltpu.VMEM((2, blocks, 1, vox), F32),
            pltpu.SemaphoreType.DMA((4,)),
            pltpu.SemaphoreType.DMA((4,)),
            pltpu.SemaphoreType.DMA((4, blocks)),
            pltpu.SemaphoreType.DMA((4, blocks)),
            pltpu.SemaphoreType.DMA((2,)),
            pltpu.SemaphoreType.DMA((6, blocks)),
        ],
        compiler_params=pltpu.CompilerParams(collective_id=0, has_side_effects=True),
        name="front",
    )(neighbours, voxels, cubes, conv_weight, qkv_weight)

    return pl.pallas_call(
        back_kernel,
        out_shape=like,
        in_specs=[smem] * 4 + [hbm] * 10 + [vmem] * 3,
        out_specs=hbm,
        scratch_shapes=[
            *operands(7),
            pltpu.VMEM((HEADS, VALUE_ROWS, vox), F32),
            pltpu.VMEM((HEADS, 1, vox), F32),
            pltpu.VMEM((vox, ch), BF16),
            pltpu.VMEM((ch, vox), BF16),
            pltpu.VMEM(voxels.shape, BF16),
            pltpu.VMEM((blocks, ch, vox), BF16),
            pltpu.VMEM((blocks, ch, vox), F32),
            pltpu.VMEM((blocks, HEADS, vox), F32),
            pltpu.VMEM((4,) + voxels.shape, BF16),
            pltpu.VMEM(voxels.shape, BF16),
            pltpu.VMEM((vox, ch), BF16),
            pltpu.VMEM((1, vox), F32),
            pltpu.SemaphoreType.DMA((4, blocks)),
            pltpu.SemaphoreType.DMA((4, blocks)),
            pltpu.SemaphoreType.DMA((blocks,)),
        ],
        name="back",
    )(neighbours, block_count, qn, kn, mixed, q, total, weight, k, v, *got, qkv_weight, wt, out_weight)


def solution(mesh):
    placed = (P(("gx", "gy"), None, None), P(("gx", "gy"), None), P(("gx", "gy")), P(), P(), P())
    return jax.shard_map(
        body, mesh=mesh, in_specs=placed, out_specs=P(("gx", "gy"), None, None), check_vma=False
    )
```
